32 devices in a mesh: dp: 8 (over z, y), tensor: 4 (over x, core).
Axes of the slice: x: 2, y: 2, z: 4, core: 2. Of those that a mesh axis runs over, the one named last changes fastest.
Arguments:
- tokens: bfloat16 [16384, 1024], P(('dp', 'tensor')), may hold values from -6 to 6
- grad_out: bfloat16 [16384, 1024], P(('dp', 'tensor')), may hold values from -6 to 6
- lengths: int32 [8, 10], P('dp'), may hold values from 0 to 1568, as said below
- coords: int32 [3, 16384], P(None, 'dp'), may hold values from 0 to 20, as said below
- w_qkv: bfloat16 [3, 1024, 1024], P(None, None, 'tensor'), may hold values from -0.1875 to 0.1875
- b_qkv: bfloat16 [3, 1024], P(None, 'tensor'), may hold values from -1.796875 to 1.796875
- w_proj: bfloat16 [1024, 1024], P('tensor'), may hold values from -1.5 to 1.5
- w_fc1: bfloat16 [1024, 4096], P(None, 'tensor'), may hold values from -0.1875 to 0.1875
- b_fc1: bfloat16 [4096], P('tensor'), may hold values from -1.796875 to 1.796875
- w_fc2: bfloat16 [4096, 1024], P('tensor'), may hold values from -0.09375 to 0.09375
- norm_gains: bfloat16 [2, 1024], replicated, may hold values from 0.5 to 1.5
- shift_biases: bfloat16 [4, 1024], replicated, may hold values from -1.796875 to 1.796875
Outputs:
- output: bfloat16 [16384, 1024], P(('dp', 'tensor'))
- grad_tokens: bfloat16 [16384, 1024], P(('dp', 'tensor'))
- grad_w_qkv: float32 [3, 1024, 1024], P(None, None, 'tensor')
- grad_b_qkv: float32 [3, 1024], P(None, 'tensor')
- grad_w_proj: float32 [1024, 1024], P('tensor')
- grad_w_fc1: float32 [1024, 4096], P(None, 'tensor')
- grad_b_fc1: float32 [4096], P('tensor')
- grad_w_fc2: float32 [4096, 1024], P('tensor')
- grad_norm_gains: float32 [2, 1024], replicated
- grad_shift_biases: float32 [4, 1024], replicated
The draws below stay inside these ranges and needn't reach their ends.
Inputs may be any that keep to these rules, and one draw needn't show every extreme that they name: `lengths`: each row lists one group's sequences: at most one video of 1568 tokens in slot 0, then images of 196 tokens, then empty slots of 0; a row sums to at most 2048; row 0 holds a video. `coords`: A token's coordinates are its tubelet's frame pair, row and column within its sequence on a 14 x 14 grid, each plus an offset of 0 to 7 drawn for the sequence and axis; padding tokens have 0.
All inputs are finite; a program needn't handle non-finite values.
Results may differ from the reference program's by a relative error of at most 0.018.
Values may be sent and summed in bfloat16 or wider, within the bound.
No kernel may reach another device: no remote copies, remote signals or barrier semaphores. Data moves between devices by JAX's collectives and lax.ppermute only.
A program may use at most 192 MiB of HBM per device.

```python
import jax
import jax.numpy as jnp
from jax import lax

D = 1024
HEADS = 16
HDIM = 64
FF = 4096
GRID = 14
IMG = 196
VID = 1568
TOK_GRP = 2048
GROUPS = 8
TOKENS = 16384
SLOTS = 10
N_TENSOR = 4


def layout(key):
    room_video = (TOK_GRP - VID) // IMG
    room_image = TOK_GRP // IMG
    key_kind, key_video, key_image = jax.random.split(key, 3)
    is_video = jax.random.randint(key_kind, (GROUPS,), 0, 2)
    is_video = is_video.at[0].set(1)
    extra_video = jax.random.randint(key_video, (GROUPS,), 0, room_video + 1)
    count_image = jax.random.randint(key_image, (GROUPS,), room_image // 2 + 1, room_image + 1)
    slot_ids = jnp.arange(SLOTS)[None, :]
    video_row = jnp.where(slot_ids == 0, VID, jnp.where(slot_ids <= extra_video[:, None], IMG, 0))
    image_row = jnp.where(slot_ids < count_image[:, None], IMG, 0)
    return jnp.where(is_video[:, None] == 1, video_row, image_row).astype(jnp.int32)


def draw_lengths(key, part):
    return layout(jax.random.fold_in(key, 7))


def draw_coords(key, part):
    lengths = layout(jax.random.fold_in(key, 7))
    offsets = jax.random.randint(jax.random.fold_in(key, 11), (GROUPS, SLOTS, 3), 0, GRID // 2 + 1)
    offsets = offsets.at[0, 0, :].set(GRID // 2)
    seq_ends = jnp.cumsum(lengths, axis=1)
    starts = seq_ends - lengths
    places = jnp.arange(TOK_GRP, dtype=jnp.int32)
    slot_of = jnp.sum((places[None, :, None] >= seq_ends[:, None, :]).astype(jnp.int32), axis=2)
    live = places[None, :] < seq_ends[:, -1:]
    clipped = jnp.minimum(slot_of, SLOTS - 1)
    start_tok = jnp.take_along_axis(starts, clipped, axis=1)
    local_pos = places[None, :] - start_tok
    frame_pos = local_pos // IMG
    row_pos = local_pos // GRID % GRID
    column_pos = local_pos % GRID
    shift_tok = jnp.take_along_axis(offsets, clipped[:, :, None], axis=1)
    stacked = jnp.stack([frame_pos, row_pos, column_pos], axis=-1) + shift_tok
    stacked = jnp.where(live[:, :, None], stacked, 0)
    return stacked.transpose(2, 0, 1).reshape(3, TOKENS).astype(jnp.int32)


def levels(stream_key, dims, cuts, smallest, top_value):
    loudness, own = 1.0, jax.random.fold_in(stream_key, 6)
    for axis_at, parts in cuts:
        heights = jnp.exp(jax.random.uniform(jax.random.fold_in(own, axis_at), (parts,), jnp.float32, smallest / len(cuts), top_value / len(cuts)))
        loudness = loudness * jnp.repeat(heights, dims[axis_at] // parts).reshape([-1 if axis == axis_at else 1 for axis in range(len(dims))])
    return loudness


def bell_draw(key, extent, spread, reach, cuts=(), kind=jnp.bfloat16):
    loudness = levels(key, extent, cuts, -0.22, 0.18) if cuts else 1.0
    array = jax.random.normal(key, extent, jnp.float32) * spread * loudness
    return jnp.minimum(jnp.maximum(array, -reach), reach).astype(kind)


def setup_inputs(seed: int = 0) -> dict:
    streams_of = jax.random.split(jax.random.key(seed), 13)
    tokens = bell_draw(streams_of[0], (TOKENS, D), 1.0, 6.0, ((0, 32),))
    grad_out = bell_draw(streams_of[1], (TOKENS, D), 1.0, 6.0, ((0, 32),))
    lengths = draw_lengths(jax.random.fold_in(streams_of[12], 71), 0)
    coords = draw_coords(jax.random.fold_in(streams_of[12], 71), 0)
    w_qkv = bell_draw(streams_of[4], (3, D, D), D ** -0.5, 0.1875, ((2, 4),))
    b_qkv = bell_draw(streams_of[5], (3, D), 0.3, 1.796875, ((1, 4),))
    w_proj = bell_draw(streams_of[6], (D, D), (D // 64) ** -0.5, 1.5, ((0, 4),))
    w_fc1 = bell_draw(streams_of[7], (D, FF), D ** -0.5, 0.1875, ((1, 4),))
    b_fc1 = bell_draw(streams_of[8], (FF,), 0.3, 1.796875, ((0, 4),))
    w_fc2 = bell_draw(streams_of[9], (FF, D), FF ** -0.5, 0.09375, ((0, 4),))
    norm_gains = jnp.clip(1.0 + 0.1 * jax.random.normal(streams_of[10], (2, D), jnp.float32), 0.5, 1.5).astype(jnp.bfloat16)
    shift_biases = bell_draw(streams_of[11], (4, D), 0.3, 1.796875)
    return dict(tokens=tokens, grad_out=grad_out, lengths=lengths, coords=coords, w_qkv=w_qkv, b_qkv=b_qkv, w_proj=w_proj, w_fc1=w_fc1, b_fc1=b_fc1, w_fc2=w_fc2, norm_gains=norm_gains, shift_biases=shift_biases)


@jax.custom_vjp
def low(v):
    return lax.optimization_barrier(v.astype(jnp.bfloat16)).astype(jnp.float32)

@jax.custom_vjp
def low_back(v):
    return v

def low_keep(v):
    return (low(v), None)

def low_pass(kept, grad):
    return (grad,)

def back_keep(v):
    return (v, None)

def back_low(kept, grad):
    return (low(grad),)
low.defvjp(low_keep, low_pass)
low_back.defvjp(back_keep, back_low)

def norm_rows(values_in, gain_row, shift_row):
    row_mean = lax.optimization_barrier(jnp.mean(values_in, axis=-1, keepdims=True))
    centred = values_in - row_mean
    variance = lax.optimization_barrier(jnp.mean(centred * centred, axis=-1, keepdims=True))
    return centred * lax.rsqrt(variance + 1e-06) * gain_row + shift_row

def segment_of(lengths_row, count):
    seq_ends = jnp.cumsum(lengths_row)
    places = jnp.arange(count, dtype=jnp.int32)
    seg_ids = lax.optimization_barrier(jnp.sum((places[:, None] >= seq_ends[None, :]).astype(jnp.int32), axis=1))
    return (seg_ids, places < seq_ends[-1])

def angle_table(coords_grp, half_dim):
    pair_ids = jnp.arange(half_dim)
    frequency = 100.0 ** (-(pair_ids // 3).astype(jnp.float32) / (half_dim // 3 + 1))
    angles = jnp.zeros((coords_grp.shape[1], half_dim), jnp.float32)
    for axis_id in range(3):
        chosen = jnp.where(pair_ids % 3 == axis_id, frequency, 0.0)
        angles = angles + coords_grp[axis_id].astype(jnp.float32)[:, None] * chosen[None, :]
    return (jnp.cos(angles), jnp.sin(angles))

def rotate(heads_in, cosine, sine):
    half_dim = heads_in.shape[-1] // 2
    first_half = heads_in[..., :half_dim]
    second_half = heads_in[..., half_dim:]
    return jnp.concatenate([first_half * cosine - second_half * sine, first_half * sine + second_half * cosine], axis=-1)

def attend(query_low, key_low, value_low, seg_ids):
    group_rows = query_low.shape[0]
    block_rows = min(512, group_rows)
    nblocks = group_rows // block_rows
    score_scale = HDIM ** (-0.5)

    def one_block(items):
        query_blk, seg_blk = items
        scores = jnp.einsum('qhd,khd->hqk', query_blk, key_low, precision=lax.Precision.HIGHEST) * score_scale
        scores = low_back(scores)
        allowed = seg_blk[:, None] == seg_ids[None, :]
        scores = jnp.where(allowed[None], scores, -1e+30)
        top_score = lax.optimization_barrier(jnp.max(scores, axis=-1, keepdims=True))
        expd = jnp.exp(scores - top_score)
        probs = low(expd / lax.optimization_barrier(jnp.sum(expd, axis=-1, keepdims=True)))
        return jnp.einsum('hqk,khd->qhd', probs, value_low, precision=lax.Precision.HIGHEST)
    blocks = lax.map(jax.checkpoint(one_block), (query_low.reshape(nblocks, block_rows, HEADS, HDIM), seg_ids.reshape(nblocks, block_rows)))
    return blocks.reshape(group_rows, HEADS * HDIM)

def group_layer(x_grp, seg_grp, cos_grp, sin_grp, wqkv, bqkv, wproj, wone, bone, wtwo, gains, shifts):
    high = lax.Precision.HIGHEST
    group_rows = x_grp.shape[0]
    head_width = D // N_TENSOR
    unit_width = FF // N_TENSOR
    normed_one = low(norm_rows(x_grp, gains[0], shifts[0]))
    pieces = []
    for shard in range(N_TENSOR):
        normed_copy = low_back(normed_one)
        pieces.append(jnp.einsum('td,cde->cte', normed_copy, wqkv[:, :, shard * head_width:(shard + 1) * head_width], precision=high))
    projected = jnp.concatenate(pieces, axis=-1) + bqkv[:, None, :]
    projected = low_back(projected)
    shaped = projected.reshape(3, group_rows, HEADS, HDIM)
    query_low = low(rotate(shaped[0], cos_grp[:, None, :], sin_grp[:, None, :]))
    key_low = low(rotate(shaped[1], cos_grp[:, None, :], sin_grp[:, None, :]))
    value_low = low(shaped[2])
    attended = attend(query_low, key_low, value_low, seg_grp)
    attended = low(low_back(attended))
    attn_sum = jnp.zeros((group_rows, D), jnp.float32)
    for shard in range(N_TENSOR):
        cols = slice(shard * head_width, (shard + 1) * head_width)
        attn_sum = attn_sum + low(jnp.dot(attended[:, cols], wproj[cols, :], precision=high))
    attn_branch = low_back(attn_sum + shifts[2])
    resid_one = x_grp + attn_branch
    normed_two = low(norm_rows(resid_one, gains[1], shifts[1]))
    pre_pieces = []
    for shard in range(N_TENSOR):
        normed_copy = low_back(normed_two)
        pre_pieces.append(jnp.dot(normed_copy, wone[:, shard * unit_width:(shard + 1) * unit_width], precision=high))
    hidden_pre = low_back(jnp.concatenate(pre_pieces, axis=-1) + bone)
    hidden_low = low(jax.nn.gelu(hidden_pre, approximate=False))
    mlp_sum = jnp.zeros((group_rows, D), jnp.float32)
    for shard in range(N_TENSOR):
        cols = slice(shard * unit_width, (shard + 1) * unit_width)
        mlp_sum = mlp_sum + low(jnp.dot(hidden_low[:, cols], wtwo[cols, :], precision=high))
    mlp_branch = low_back(mlp_sum + shifts[3])
    return resid_one + mlp_branch

def reference(tokens, grad_out, lengths, coords, w_qkv, b_qkv, w_proj, w_fc1, b_fc1, w_fc2, norm_gains, shift_biases):
    group_rows = TOK_GRP
    seg_all, live_all = jax.vmap(lambda lengths_row: segment_of(lengths_row, group_rows))(lengths)
    coords_grp = coords.reshape(3, GROUPS, group_rows).transpose(1, 0, 2)
    cos_all, sin_all = jax.vmap(lambda coords_one: angle_table(coords_one, HDIM // 2))(coords_grp)
    x_all = tokens.astype(jnp.float32).reshape(GROUPS, group_rows, D)
    live_f = live_all.astype(jnp.float32)
    cotangent = grad_out.astype(jnp.float32).reshape(GROUPS, group_rows, D) * live_f[:, :, None]
    params = (w_qkv.astype(jnp.float32), b_qkv.astype(jnp.float32), w_proj.astype(jnp.float32), w_fc1.astype(jnp.float32), b_fc1.astype(jnp.float32), w_fc2.astype(jnp.float32), norm_gains.astype(jnp.float32), shift_biases.astype(jnp.float32))

    def forward(x_in, wqkv, bqkv, wproj, wone, bone, wtwo, gains, shifts):

        def one_group(items):
            x_grp, seg_grp, cos_grp, sin_grp = items
            return group_layer(x_grp, seg_grp, cos_grp, sin_grp, wqkv, bqkv, wproj, wone, bone, wtwo, gains, shifts)
        return lax.map(jax.checkpoint(one_group), (x_in, seg_all, cos_all, sin_all))
    result, pullback = jax.vjp(forward, x_all, *params)
    grads = pullback(cotangent)
    output = result.reshape(TOKENS, D).astype(jnp.bfloat16)
    grad_tokens = grads[0].reshape(TOKENS, D).astype(jnp.bfloat16)
    return (output, grad_tokens, grads[1], grads[2], grads[3], grads[4], grads[5], grads[6], grads[7], grads[8])
```

```python
from functools import partial

import jax
import jax.numpy as jnp
from jax import lax
from jax.experimental import pallas as pl
from jax.experimental.pallas import tpu as pltpu
from jax.sharding import PartitionSpec as P

HDIM=64
LOG2E=1.4426950408889634
LN2=0.6931471805599453
f32=jnp.float32; bf16=jnp.bfloat16
BLK=256
VROWS=80
NT=(((1,),(1,)),((),()))

def work(flops):
    return pl.CostEstimate(flops=flops,bytes_accessed=0,transcendentals=0)

def lane_half(shape, which):
    lane=lax.broadcasted_iota(jnp.int32, shape, 1)
    return (lane//HDIM)%2==which

def attn_fwd_kernel(codes, q_ref, k_ref, v_ref, segq_ref, segk_ref, o_ref, lse_ref, vt, qm, m_sc, acc):
    step=pl.program_id(0)
    nkb=k_ref.shape[0]//BLK
    heads=q_ref.shape[1]//HDIM
    @pl.when(step==0)
    def _():
        for blk in range(nkb):
            rows=pl.ds(blk*BLK,BLK)
            vT=v_ref[rows,:].T
            for h in range(heads):
                vt[h*VROWS:h*VROWS+HDIM, rows]=vT[h*HDIM:(h+1)*HDIM,:]
        for h in range(heads):
            vt[h*VROWS+HDIM:(h+1)*VROWS,:]=jnp.ones((VROWS-HDIM,vt.shape[1]),bf16)
    for p in range(heads//2):
        qp=q_ref[:,p*128:(p+1)*128]
        for w in range(2):
            qm[2*p+w]=jnp.where(lane_half(qp.shape,w),qp,jnp.zeros_like(qp))
    m_sc[...]=jnp.full(m_sc.shape,-1e30,f32)
    acc[...]=jnp.zeros(acc.shape,f32)
    scale=HDIM**-0.5*LOG2E

    def tile(kb,masked):
        rows=pl.ds(pl.multiple_of(kb*BLK,BLK),BLK)
        if masked:
            allowed=segk_ref[rows,:][:,0:1]==segq_ref[0:1,:]
        for h in range(heads):
            p=h//2
            s=lax.dot_general(k_ref[rows,p*128:(p+1)*128],qm[h],NT,preferred_element_type=f32)*scale
            if masked: s=jnp.where(allowed,s,-1e30)
            m_prev=m_sc[h:h+1,:]
            m_new=jnp.maximum(m_prev,jnp.max(s,axis=0,keepdims=True))
            alpha=jnp.exp2(m_prev-m_new)
            prob=jnp.exp2(s-m_new).astype(bf16)
            m_sc[h:h+1,:]=m_new
            arows=slice(h*VROWS,(h+1)*VROWS)
            acc[arows,:]=acc[arows,:]*alpha+jnp.dot(vt[arows,rows],prob,preferred_element_type=f32)

    def body(kb,carry):
        code=codes[step,kb]
        @pl.when(code==1)
        def _(): tile(kb,False)
        @pl.when(code==2)
        def _(): tile(kb,True)
        return carry
    lax.fori_loop(0,nkb,body,0)
    outs=[]
    for h in range(heads):
        total=acc[h*VROWS+HDIM:h*VROWS+HDIM+1,:]
        outs.append(acc[h*VROWS:h*VROWS+HDIM,:]/total)
        lse_ref[h:h+1,:]=m_sc[h:h+1,:]+jnp.log2(total)
    for h in range(heads,8):
        lse_ref[h:h+1,:]=jnp.zeros((1,BLK),f32)
    o_ref[...]=jnp.concatenate(outs,axis=0).T.astype(bf16)

def attn_fwd(codes,q,k,v,segq,segk,block0,nblocks):
    rows,cols=k.shape
    heads=cols//HDIM
    full=lambda i,c:(0,0)
    return pl.pallas_call(
        attn_fwd_kernel,
        out_shape=(jax.ShapeDtypeStruct((nblocks*BLK,cols),bf16),jax.ShapeDtypeStruct((8,nblocks*BLK),f32)),
        grid_spec=pltpu.PrefetchScalarGridSpec(num_scalar_prefetch=1,grid=(nblocks,),
            in_specs=[pl.BlockSpec((BLK,cols),lambda i,c:(i+block0,0)),
                      pl.BlockSpec((rows,cols),full),pl.BlockSpec((rows,cols),full),
                      pl.BlockSpec((1,BLK),lambda i,c:(0,i+block0)),
                      pl.BlockSpec((rows,1),full)],
            out_specs=[pl.BlockSpec((BLK,cols),lambda i,c:(i,0)),pl.BlockSpec((8,BLK),lambda i,c:(0,i))],
            scratch_shapes=[pltpu.VMEM((heads*VROWS,rows),bf16),pltpu.VMEM((heads,BLK,128),bf16),
                            pltpu.VMEM((8,BLK),f32),pltpu.VMEM((heads*VROWS,BLK),f32)]),
        compiler_params=pltpu.CompilerParams(dimension_semantics=("arbitrary",)),
        name="attn_fwd",
        cost_estimate=work(64*nblocks*BLK*rows*cols),
    )(codes,q,k,v,segq,segk)

def swap_halves(x):
    n=x.shape[1]
    lane=lax.broadcasted_iota(jnp.int32,x.shape,1)
    up=pltpu.roll(x,n-HDIM//2,1)
    down=pltpu.roll(x,HDIM//2,1)
    return jnp.where(lane%HDIM<HDIM//2,up,down)

def attn_bwd_kernel(last, pair, codes, q_ref,k_ref,v_ref,do_ref,o_ref,lse_ref,segq_ref,segk_ref,cos_ref,sin_ref,cosk_ref,sink_ref,*rest):
    if last:
        dk0_ref,dv0_ref,gq_ref,gk_ref,gv_ref,bsum_ref,kt,qm,dom,delta,dq,dk,dv=rest
    else:
        gq_ref,gk_ref,gv_ref,bsum_ref,kt,qm,dom,delta,dq,dk,dv=rest
    step=pl.program_id(0)
    nkb=pl.num_programs(0)
    nqb=q_ref.shape[0]//BLK
    heads=q_ref.shape[1]//HDIM
    scale=HDIM**-0.5
    def unrotate(x,cos,sin):
        out=[]
        for p in range(heads//2):
            xp=x[:,p*128:(p+1)*128]
            out.append(xp*cos-swap_halves(xp)*sin)
        return jnp.concatenate(out,axis=1)
    @pl.when(step==0)
    def _():
        def prep(blk,carry):
            rows=pl.ds(pl.multiple_of(blk*BLK,BLK),BLK)
            for p in range(heads//2):
                lanes=slice(p*128,(p+1)*128)
                qp=q_ref[rows,lanes]; dp=do_ref[rows,lanes]
                for w in range(2):
                    sel=lane_half(qp.shape,w)
                    qm[2*p+w,rows,:]=jnp.where(sel,qp,jnp.zeros_like(qp))
                    dom[2*p+w,rows,:]=jnp.where(sel,dp,jnp.zeros_like(dp))
            prod=(do_ref[rows,:].astype(f32)*o_ref[rows,:].astype(f32)).T
            for h in range(heads):
                delta[h:h+1,rows]=jnp.sum(prod[h*HDIM:(h+1)*HDIM,:],axis=0,keepdims=True)
            return carry
        lax.fori_loop(0,nqb,prep,0)
        dq[...]=jnp.zeros(dq.shape,f32)
        bsum_ref[...]=jnp.zeros(bsum_ref.shape,f32)
    kt[...]=k_ref[...].T
    if last:
        dk[...]=dk0_ref[...]
        dv[...]=dv0_ref[...]
    else:
        dk[...]=jnp.zeros(dk.shape,f32)
        dv[...]=jnp.zeros(dv.shape,f32)

    def tile(qb,masked):
        rows=pl.ds(pl.multiple_of(qb*BLK,BLK),BLK)
        if masked:
            allowed=segk_ref[:,0:1]==segq_ref[0:1,rows]
        for h in range(heads):
            p=h//2
            lanes=slice(p*128,(p+1)*128)
            hr=slice(h*HDIM,(h+1)*HDIM)
            qh=qm[h,rows,:]; dh=dom[h,rows,:]
            s=lax.dot_general(k_ref[:,lanes],qh,NT,preferred_element_type=f32)*(scale*LOG2E)
            prob=jnp.exp2(s-lse_ref[2*pair+h:2*pair+h+1,rows])
            if masked: prob=jnp.where(allowed,prob,0.0)
            dp=lax.dot_general(v_ref[:,lanes],dh,NT,preferred_element_type=f32)
            ds=(prob*(dp-delta[h:h+1,rows])).astype(bf16)
            dv[:,lanes]+=jnp.dot(prob.astype(bf16),dh,preferred_element_type=f32)
            dk[:,lanes]+=jnp.dot(ds,qh,preferred_element_type=f32)
            dq[hr,rows]+=jnp.dot(kt[hr,:],ds,preferred_element_type=f32)

    def body(qb,carry):
        code=codes[qb,step]
        @pl.when(code==1)
        def _(): tile(qb,False)
        @pl.when(code==2)
        def _(): tile(qb,True)
        return carry
    lax.fori_loop(0,nqb,body,0)

    if last:
        gk=unrotate(dk[...]*scale,cosk_ref[...],sink_ref[...]).astype(bf16)
        gv=dv[...].astype(bf16)
        gk_ref[...]=gk
        gv_ref[...]=gv
        bsum_ref[1:2,:]+=jnp.sum(gk.astype(f32),axis=0,keepdims=True)
        bsum_ref[2:3,:]+=jnp.sum(gv.astype(f32),axis=0,keepdims=True)
    else:
        gk_ref[...]=dk[...]
        gv_ref[...]=dv[...]

    @pl.when(step==nkb-1)
    def _():
        def fin(blk,carry):
            rows=pl.ds(pl.multiple_of(blk*BLK,BLK),BLK)
            gq=unrotate(dq[:,rows].T*scale,cos_ref[rows,:],sin_ref[rows,:]).astype(bf16)
            gq_ref[rows,:]=gq
            bsum_ref[0:1,:]+=jnp.sum(gq.astype(f32),axis=0,keepdims=True)
            return carry
        lax.fori_loop(0,nqb,fin,0)

def attn_bwd(codes,q,k,v,do,o,lse,segq,segk,cos,sin,part,pair,carried):
    rows=k.shape[0]
    cols=2*HDIM
    half=do.shape[0]
    nb=rows//BLK
    last=carried is not None
    here=lambda n: pl.BlockSpec((half,n),lambda i,c:(0,0))
    mine=lambda n,col: pl.BlockSpec((half,n),lambda i,c:(part,col))
    held=pl.BlockSpec((half,cols),lambda i,c:(0,pair))
    blk=lambda n,col: pl.BlockSpec((BLK,n),lambda i,c:(i,col))
    kdtype=bf16 if last else f32
    return pl.pallas_call(
        partial(attn_bwd_kernel,last,pair),
        out_shape=(jax.ShapeDtypeStruct((half,cols),bf16),jax.ShapeDtypeStruct((rows,cols),kdtype),
                   jax.ShapeDtypeStruct((rows,cols),kdtype),jax.ShapeDtypeStruct((8,cols),f32)),
        grid_spec=pltpu.PrefetchScalarGridSpec(num_scalar_prefetch=1,grid=(nb,),
            in_specs=[mine(cols,pair),blk(cols,pair),blk(cols,pair),held,held,pl.BlockSpec((8,half),lambda i,c:(0,0)),
                      pl.BlockSpec((1,half),lambda i,c:(0,part)),blk(1,0),mine(128,0),mine(128,0),blk(128,0),blk(128,0)]
                     +([blk(cols,0),blk(cols,0)] if last else []),
            out_specs=[here(cols),blk(cols,0),blk(cols,0),pl.BlockSpec((8,cols),lambda i,c:(0,0))],
            scratch_shapes=[pltpu.VMEM((cols,BLK),bf16),pltpu.VMEM((2,half,128),bf16),pltpu.VMEM((2,half,128),bf16),
                            pltpu.VMEM((8,half),f32),pltpu.VMEM((cols,half),f32),pltpu.VMEM((BLK,cols),f32),pltpu.VMEM((BLK,cols),f32)]),
        compiler_params=pltpu.CompilerParams(dimension_semantics=("arbitrary",)),
        name="attn_bwd",
        cost_estimate=work(60*half*rows*cols),
    )(codes,q,k,v,do,o,lse,segq,segk,cos,sin,cos,sin,*(carried or ()))

def block_codes(seg,pad_seg,skip_pad):
    sb=seg.reshape(-1,BLK)
    lo=jnp.min(sb,axis=1); hi=jnp.max(sb,axis=1)
    meet=(lo[:,None]<=hi[None,:])&(lo[None,:]<=hi[:,None])
    whole=(lo==hi)
    same=whole[:,None]&whole[None,:]&(lo[:,None]==lo[None,:])
    code=jnp.where(meet,jnp.where(same,1,2),0).astype(jnp.int32)
    if skip_pad:
        alive=lo<pad_seg
        code=jnp.where(alive[:,None]&alive[None,:],code,0)
    return code


def pick(i,n,a_ref,b_ref):
    return jnp.where(i<n,a_ref[...],b_ref[...])


def qkv_kernel(n, xa_ref, xb_ref, w_ref, b_ref, cos_ref, sin_ref, *rest):
    x=pick(pl.program_id(0),n,xa_ref,xb_ref)
    cos=cos_ref[...]; sin=sin_ref[...]
    for c,o_ref in enumerate(rest[-3:]):
        y=jnp.dot(x,w_ref[c],preferred_element_type=f32)+b_ref[c:c+1,:]
        if c<2:
            parts=[]
            for p in range(y.shape[1]//128):
                yp=y[:,p*128:(p+1)*128]
                parts.append(yp*cos+swap_halves(yp)*sin)
            y=jnp.concatenate(parts,axis=1)
        o_ref[...]=y.astype(bf16)


def two(tile,n,width):
    return [pl.BlockSpec((tile,width),lambda i:(jnp.minimum(i,n-1),0)),
            pl.BlockSpec((tile,width),lambda i:(jnp.maximum(i-n,0),0))]


def qkv_rows(xa,xb,w,b,cos,sin,part,full):
    rows,d=xa.shape
    cols=w.shape[2]
    tile=min(512,rows)
    n=rows//tile
    off=part*2*n
    row=lambda m: pl.BlockSpec((tile,m),lambda i:(i+off,0))
    kept=[] if full is None else list(full)
    return pl.pallas_call(
        partial(qkv_kernel,n),
        grid=(2*n,),
        out_shape=[jax.ShapeDtypeStruct((cos.shape[0],cols),bf16)]*3,
        in_specs=two(tile,n,d)+[pl.BlockSpec(w.shape,lambda i:(0,0,0)),pl.BlockSpec(b.shape,lambda i:(0,0)),
                  row(128),row(128)]+[pl.BlockSpec(memory_space=pl.ANY)]*len(kept),
        out_specs=[row(cols)]*3,
        input_output_aliases={6+i:i for i in range(len(kept))},
        compiler_params=pltpu.CompilerParams(dimension_semantics=("arbitrary",)),
        name="qkv",
        cost_estimate=work(20*rows*d*cols*2),
    )(xa,xb,w,b,cos,sin,*kept)


def mlp_kernel(n,xa_ref,xb_ref,ga_ref,gb_ref,w1_ref,b1_ref,w2_ref,*rest):
    hid_ref,gp_ref,na_ref,nb_ref,db_ref=rest[-5:]
    i=pl.program_id(0)
    @pl.when(i==0)
    def _():
        db_ref[...]=jnp.zeros(db_ref.shape,f32)
    pre=jnp.dot(pick(i,n,xa_ref,xb_ref),w1_ref[...],preferred_element_type=f32)+b1_ref[...]
    phi=0.5+0.5*lax.erf(pre*0.7071067811865476)
    hid_ref[...]=(pre*phi).astype(bf16)
    slope=phi+pre*(0.3989422804014327*jnp.exp2(pre*pre*(-0.5*LOG2E)))
    gh=lax.dot_general(pick(i,n,ga_ref,gb_ref),w2_ref[...],NT,preferred_element_type=f32)
    gp=(gh*slope).astype(bf16)
    gp_ref[...]=gp
    db_ref[...]+=jnp.sum(gp.astype(f32),axis=0,keepdims=True)
    gn=lax.dot_general(gp,w1_ref[...],NT,preferred_element_type=f32).astype(bf16)
    @pl.when(i<n)
    def _(): na_ref[...]=gn
    @pl.when(i>=n)
    def _(): nb_ref[...]=gn


def mlp_rows(xs,gs,w1,b1,w2,part,full):
    rows,d=xs[0].shape
    units=w1.shape[1]
    tile=min(256,rows)
    n=rows//tile
    off=part*2*n
    row=lambda m: pl.BlockSpec((tile,m),lambda i:(i+off,0))
    whole=lambda a: pl.BlockSpec(a.shape,lambda i:(0,0))
    kept=[] if full is None else list(full)
    return pl.pallas_call(
        partial(mlp_kernel,n),
        grid=(2*n,),
        out_shape=[jax.ShapeDtypeStruct((rows*4,units),bf16)]*2+[jax.ShapeDtypeStruct((rows,d),bf16)]*2+
                  [jax.ShapeDtypeStruct((1,units),f32)],
        in_specs=two(tile,n,d)+two(tile,n,d)+[whole(w1),whole(b1),whole(w2)]+[pl.BlockSpec(memory_space=pl.ANY)]*len(kept),
        out_specs=[row(units),row(units)]+two(tile,n,d)+[pl.BlockSpec((1,units),lambda i:(0,0))],
        input_output_aliases={7+i:i for i in range(len(kept))},
        compiler_params=pltpu.CompilerParams(dimension_semantics=("arbitrary",)),
        name="mlp",
        cost_estimate=work(12*rows*d*units),
    )(*xs,*gs,w1,b1,w2,*kept)


def back_kernel(n,pairs,*refs):
    i=pl.program_id(0)
    w_ref,oa_ref,ob_ref=refs[-3:]
    y=0.0
    for c in range(3):
        g=jnp.concatenate([refs[c*pairs+p][...] for p in range(pairs)],axis=1)
        y=y+lax.dot_general(g,w_ref[c],NT,preferred_element_type=f32)
    y=y.astype(bf16)
    @pl.when(i<n)
    def _(): oa_ref[...]=y
    @pl.when(i>=n)
    def _(): ob_ref[...]=y


def back_rows(gq,gk,gv,w,part):
    half,cols=gq[0].shape
    rows=half//2
    d=w.shape[1]
    tile=min(512,rows)
    n=rows//tile
    off=part*2*n
    row=pl.BlockSpec((tile,cols),lambda i:(i+off,0))
    pairs=len(gq)
    return pl.pallas_call(
        partial(back_kernel,n,pairs),
        grid=(2*n,),
        out_shape=[jax.ShapeDtypeStruct((rows,d),bf16)]*2,
        in_specs=[pl.BlockSpec((tile,cols),lambda i:(i,0))]*pairs+[row]*(2*pairs)+[pl.BlockSpec(w.shape,lambda i:(0,0,0))],
        out_specs=two(tile,n,d),
        compiler_params=pltpu.CompilerParams(dimension_semantics=("arbitrary",)),
        name="back",
        cost_estimate=work(12*rows*d*cols*pairs),
    )(*gq,*gk,*gv,w)


def norm_rows(values_in, gain_row, shift_row):
    row_mean = jnp.mean(values_in, axis=-1, keepdims=True)
    centred = values_in - row_mean
    variance = jnp.mean(centred * centred, axis=-1, keepdims=True)
    return centred * lax.rsqrt(variance + 1e-06) * gain_row + shift_row


def flip(x,bits):
    n=lax.axis_size("tensor")
    return lax.ppermute(x,"tensor",[(i,i^bits) for i in range(n)])


def pair_sum(mine,other):
    return mine.astype(f32)+flip(other,1).astype(f32)


def dp_flip(x,bit):
    n=lax.axis_size("dp")
    return lax.ppermute(x,"dp",[(i,i^(1<<bit)) for i in range(n)])


class DpSum:
    def __init__(self,x,order):
        self.cur=x
        self.stages=[(bit,True) for bit in order]+[(bit,False) for bit in reversed(order)]
        self.at=0

    def operand(self):
        bit,halving=self.stages[self.at]
        if not halving: return self.cur
        half=self.cur.shape[0]//2
        up=(lax.axis_index("dp")>>bit)&1
        self.kept=lax.dynamic_slice_in_dim(self.cur,up*half,half,0)
        return lax.dynamic_slice_in_dim(self.cur,(1-up)*half,half,0)

    def start(self,operand):
        self.sent=operand
        self.got=dp_flip(operand,self.stages[self.at][0])

    def finish(self,got):
        bit,halving=self.stages[self.at]
        self.at+=1
        if halving:
            self.cur=(self.kept.astype(f32)+got.astype(f32)).astype(bf16)
        else:
            up=((lax.axis_index("dp")>>bit)&1)==1
            self.cur=jnp.concatenate([jnp.where(up,got,self.sent),jnp.where(up,self.sent,got)],axis=0)

    def rest(self):
        while self.at<len(self.stages):
            self.start(self.operand())
            self.finish(self.got)
        return self.cur


def begin(sums,value):
    value,*sends=lax.optimization_barrier((value,*[s.operand() for s in sums]))
    for s,x in zip(sums,sends): s.start(x)
    return value


def settle(sums,value):
    value,*gots=lax.optimization_barrier((value,*[s.got for s in sums]))
    for s,x in zip(sums,gots): s.finish(x)
    return value


def all_sum(x):
    for bits in (1,2):
        x=x+flip(x,bits)
    for bit in range(lax.axis_size("dp").bit_length()-1):
        x=x+dp_flip(x,bit)
    return x


def after(x,*others):
    return lax.optimization_barrier((x,)+others)[0]


def shards(tokens,grad_out,lengths,coords,w_qkv,b_qkv,w_proj,w_fc1,b_fc1,w_fc2,norm_gains,shift_biases):
    tok=tokens.shape[0]
    ranks=lax.axis_size("tensor")
    bits=lax.axis_size("dp").bit_length()-1
    me=lax.axis_index("tensor")
    rows_all=tok*ranks
    half=rows_all//2
    cols=w_qkv.shape[2]
    ends=jnp.cumsum(lengths[0])
    slots=lengths.shape[1]
    rel=jnp.arange(rows_all,dtype=jnp.int32)
    place=((rel//tok)^me)*tok+rel%tok
    seg=jnp.sum((place[:,None]>=ends[None,:]).astype(jnp.int32),axis=1)
    live=(place[:tok]<ends[-1]).astype(f32)[:,None]
    cgrp=jnp.concatenate([lax.dynamic_slice_in_dim(coords,(me^j)*tok,tok,1) for j in range(ranks)],axis=1).astype(f32)
    lane=jnp.arange(128,dtype=jnp.int32)
    pair=lane%(HDIM//2)
    freq=100.0**(-(pair//3).astype(f32)/(HDIM//2//3+1))
    angle=jnp.zeros((rows_all,128),f32)
    for a in range(3):
        angle=angle+cgrp[a][:,None]*jnp.where(pair%3==a,freq,0.0)[None,:]
    cos=jnp.cos(angle)
    sin=jnp.sin(angle)*jnp.where(lane%HDIM<HDIM//2,-1.0,1.0)[None,:]
    gains=norm_gains.astype(f32)
    shifts=shift_biases.astype(f32)
    x_rows=tokens.astype(f32)

    normed_one,norm_one_back=jax.vjp(norm_rows,x_rows,gains[0],shifts[0])
    low_one=normed_one.astype(bf16)
    far=flip(low_one,2)
    near=flip(low_one,1)
    grad_y=grad_out.astype(f32)*live
    grad_mlp=grad_y.astype(bf16)

    bq=b_qkv.astype(f32)
    qkv=qkv_rows(low_one,near,w_qkv,bq,cos,sin,0,None)
    far,*qkv=lax.optimization_barrier((far,*qkv))
    far_pair=flip(far,1)
    q,k,v=qkv_rows(far,far_pair,w_qkv,bq,cos,sin,1,qkv)
    n1=[low_one,near,far,far_pair]
    late,q,k,v=lax.optimization_barrier((grad_mlp,q,k,v))
    gm=[late,flip(late,1),flip(late,2)]
    segq=seg[None,:]; segk=seg[:,None]
    hb=half//BLK
    codes=block_codes(seg,slots,False)
    att_far,lse_far=attn_fwd(codes[hb:],q,k,v,segq,segk,hb,hb)
    proj=lambda a: jnp.dot(a,w_proj,preferred_element_type=f32).astype(bf16)
    across=pair_sum(proj(att_far[tok:]),proj(att_far[:tok])).astype(bf16)
    q_late,across,g2=lax.optimization_barrier((q,across,gm[2]))
    gm=[gm[0],gm[1],g2,flip(g2,1)]
    across=flip(across,3)
    att_near,lse_near=attn_fwd(codes[:hb],q_late,k,v,segq,segk,0,hb)
    across,att_near=lax.optimization_barrier((across,att_near))
    mine=pair_sum(proj(att_near[:tok]),proj(att_near[tok:]))
    resid_one=x_rows+mine+across.astype(f32)+shifts[2]
    normed_two,norm_two_back=jax.vjp(norm_rows,resid_one,gains[1],shifts[1])
    low_two=normed_two.astype(bf16)
    far=flip(low_two,2)
    near=flip(low_two,1)
    b1=b_fc1.astype(f32)[None,:]
    hid,gp,gn0,gn1,db0=mlp_rows((low_two,near),(gm[0],gm[1]),w_fc1,b1,w_fc2,0,None)
    far,hid,gp=lax.optimization_barrier((far,hid,gp))
    far_pair=flip(far,1)
    hid,gp,gn2,gn3,db1=mlp_rows((far,far_pair),(gm[2],gm[3]),w_fc1,b1,w_fc2,1,(hid,gp))
    db=db0+db1
    across=pair_sum(gn3,gn2).astype(bf16)
    hid,gp,across=lax.optimization_barrier((hid,gp,across))
    across=flip(across,3)
    mine=pair_sum(gn0,gn1)
    tn=lambda a,b: lax.dot_general(a,b,(((0,),(0,)),((),())),preferred_element_type=f32)
    grad_w1=tn(jnp.concatenate([low_two,near,far,far_pair],axis=0),gp).astype(bf16)
    grad_w2=tn(hid,jnp.concatenate(gm,axis=0)).astype(bf16)
    across,grad_w1,grad_w2=lax.optimization_barrier((across,grad_w1,grad_w2))
    low_order=tuple(range(bits))
    swapped=(1,0)+tuple(range(2,bits))
    wsums=[DpSum(grad_w1,low_order),DpSum(grad_w2,swapped)]
    grad_resid_two,grad_gain_two,grad_shift_two=norm_two_back(mine+across.astype(f32))

    grad_resid_one=grad_y+grad_resid_two
    grad_attn=grad_resid_one.astype(bf16)
    far=flip(grad_attn,2)
    near=flip(grad_attn,1)
    ghead=lambda a: lax.dot_general(a,w_proj,NT,preferred_element_type=f32).astype(bf16)
    bcodes=block_codes(seg,slots,True)
    do_near=jnp.concatenate([ghead(grad_attn),ghead(near)],axis=0)
    do_near=begin(wsums,do_near)
    bwd_near=lambda pair,do: attn_bwd(bcodes[:hb],q,k,v,do,att_near,lse_near,segq,segk,cos,sin,0,pair,None)
    bwd_far=lambda pair,do,carried: attn_bwd(bcodes[hb:],q,k,v,do,att_far,lse_far,segq,segk,cos,sin,1,pair,carried)
    gq0n,dk,dv,bs0=bwd_near(0,do_near)
    far,dk,dv=lax.optimization_barrier((far,dk,dv))
    dk=settle(wsums,dk)
    far_pair=flip(far,1)
    do_far=jnp.concatenate([ghead(far),ghead(far_pair)],axis=0)
    do_far=begin(wsums,do_far)
    gq0f,gk0,gv0,bs1=bwd_far(0,do_far,(dk,dv))
    gk0=settle(wsums,gk0)
    all1=jnp.concatenate(n1,axis=0)
    wpart=lambda gqn,gqf,gk,gv: tn(all1,jnp.concatenate([jnp.concatenate([gqn,gqf],axis=0),gk,gv],axis=1)).astype(bf16)
    do_near,gk0=lax.optimization_barrier((do_near,gk0))
    do_near=begin(wsums,do_near)
    gq1n,dk,dv,bs2=bwd_near(1,do_near)
    dk=settle(wsums,dk)
    dk=begin(wsums,dk)
    dk,gq0n,alla,atts=lax.optimization_barrier((dk,gq0n,jnp.concatenate([grad_attn,near,far,far_pair],axis=0),
                                                jnp.concatenate([att_near,att_far],axis=0)))
    tail0=[DpSum(wpart(gq0n,gq0f,gk0,gv0),low_order),DpSum(tn(atts,alla).astype(bf16),swapped)]
    dk=begin(tail0,dk)
    gq1f,gk1,gv1,bs3=bwd_far(1,do_far,(dk,dv))
    gk1=settle(wsums+tail0,gk1)
    gk1=begin(wsums+tail0,gk1)
    r2,r3=back_rows([gq0f,gq1f],[gk0,gk1],[gv0,gv1],w_qkv,1)
    across=pair_sum(r3,r2).astype(bf16)
    gq1n,across,hid=lax.optimization_barrier((gq1n,across,hid))
    across=flip(across,3)
    wqkv1=wpart(gq1n,gq1f,gk1,gv1)
    early=jnp.stack([grad_gain_two,grad_shift_two,jnp.sum(grad_attn,axis=0,dtype=f32),jnp.sum(grad_mlp,axis=0,dtype=f32)])
    early=early+flip(early,1)
    early=early+flip(early,2)
    d=tokens.shape[1]
    bsum=jnp.concatenate([(bs0+bs1)[:3],(bs2+bs3)[:3]],axis=1)
    sizes=(3*cols,db.shape[1],early.size)
    width=wqkv1.shape[1]
    pad=(-sum(sizes))%(width*8<<bits)
    small=jnp.concatenate([bsum.reshape(-1),db[0],early.reshape(-1),jnp.zeros((pad,),f32)]).astype(bf16).reshape(-1,width)
    hd=d//2
    tail1=[DpSum(wqkv1[:hd],low_order),DpSum(jnp.concatenate([wqkv1[hd:],small],axis=0),swapped)]
    gq_near=[gq0n,gq1n]
    gq1n_late=begin(tail1,gq1n)
    r0,r1=back_rows([gq0n,gq1n_late],[gk0,gk1],[gv0,gv1],w_qkv,0)
    r0=settle(wsums+tail0,r0)
    r0=begin(wsums+tail0,r0)
    mine=pair_sum(r0,r1)
    across,hid=lax.optimization_barrier((across,hid))
    o=[jnp.dot(hid[j*tok:(j+1)*tok],w_fc2,preferred_element_type=f32).astype(bf16) for j in range(ranks)]
    o_across=flip(pair_sum(o[3],o[2]).astype(bf16),3)
    output=(resid_one+pair_sum(o[0],o[1])+o_across.astype(f32)+shifts[3]).astype(bf16)
    for t in wsums+tail0+tail1:
        if hasattr(t,"got"): t.finish(t.got)
    grad_w1,grad_w2=[t.rest() for t in wsums]
    wqkv0,grad_proj=[t.rest() for t in tail0]
    tail_a,tail_b=[t.rest() for t in tail1]
    wqkv1=jnp.concatenate([tail_a,tail_b[:d-hd]],axis=0)
    spread=lambda w: jnp.stack([w[:,c*width//3:(c+1)*width//3] for c in range(3)])
    grad_wqkv=jnp.concatenate([spread(wqkv0),spread(wqkv1)],axis=2).astype(f32)
    small=tail_b[d-hd:].reshape(-1).astype(f32)
    grad_bqkv=small[:sizes[0]].reshape(3,cols)
    grad_b1=small[sizes[0]:sizes[0]+sizes[1]]
    early=small[sizes[0]+sizes[1]:sum(sizes)].reshape(4,d)
    grad_x_norm,grad_gain_one,grad_shift_one=norm_one_back(mine+across.astype(f32))
    grad_tokens=(grad_resid_one+grad_x_norm).astype(bf16)
    one=all_sum(jnp.stack([grad_gain_one,grad_shift_one]))
    return (output,grad_tokens,grad_wqkv,grad_bqkv,grad_proj.astype(f32),grad_w1.astype(f32),grad_b1,grad_w2.astype(f32),
            jnp.stack([one[0],early[0]]),jnp.stack([one[1],early[1],early[2],early[3]]))


def solution(mesh):
    rows=P(("dp","tensor"),None)
    return jax.shard_map(shards,mesh=mesh,
        in_specs=(rows,rows,P("dp",None),P(None,"dp"),P(None,None,"tensor"),P(None,"tensor"),P("tensor",None),
                  P(None,"tensor"),P("tensor"),P("tensor",None),P(),P()),
        out_specs=(rows,rows,P(None,None,"tensor"),P(None,"tensor"),P("tensor",None),P(None,"tensor"),P("tensor"),
                   P("tensor",None),P(),P()),
        check_vma=False)
```

```python
from functools import partial

import jax
import jax.numpy as jnp
from jax import lax
from jax.experimental import pallas as pl
from jax.experimental.pallas import tpu as pltpu
from jax.sharding import PartitionSpec as P

HDIM=64
LOG2E=1.4426950408889634
LN2=0.6931471805599453
f32=jnp.float32; bf16=jnp.bfloat16
BLK=256
VROWS=80
NT=(((1,),(1,)),((),()))

def work(flops):
    return pl.CostEstimate(flops=flops,bytes_accessed=0,transcendentals=0)

def lane_half(shape, which):
    lane=lax.broadcasted_iota(jnp.int32, shape, 1)
    return (lane//HDIM)%2==which

def attn_fwd_kernel(codes, q_ref, k_ref, v_ref, segq_ref, segk_ref, o_ref, lse_ref, vt, qm, m_sc, acc):
    step=pl.program_id(0)
    nkb=k_ref.shape[0]//BLK
    heads=q_ref.shape[1]//HDIM
    @pl.when(step==0)
    def _():
        for blk in range(nkb):
            rows=pl.ds(blk*BLK,BLK)
            vT=v_ref[rows,:].T
            for h in range(heads):
                vt[h*VROWS:h*VROWS+HDIM, rows]=vT[h*HDIM:(h+1)*HDIM,:]
        for h in range(heads):
            vt[h*VROWS+HDIM:(h+1)*VROWS,:]=jnp.ones((VROWS-HDIM,vt.shape[1]),bf16)
    for p in range(heads//2):
        qp=q_ref[:,p*128:(p+1)*128]
        for w in range(2):
            qm[2*p+w]=jnp.where(lane_half(qp.shape,w),qp,jnp.zeros_like(qp))
    m_sc[...]=jnp.full(m_sc.shape,-1e30,f32)
    acc[...]=jnp.zeros(acc.shape,f32)
    scale=HDIM**-0.5*LOG2E

    def tile(kb,masked):
        rows=pl.ds(pl.multiple_of(kb*BLK,BLK),BLK)
        if masked:
            allowed=segk_ref[rows,:][:,0:1]==segq_ref[0:1,:]
        for h in range(heads):
            p=h//2
            s=lax.dot_general(k_ref[rows,p*128:(p+1)*128],qm[h],NT,preferred_element_type=f32)*scale
            if masked: s=jnp.where(allowed,s,-1e30)
            m_prev=m_sc[h:h+1,:]
            m_new=jnp.maximum(m_prev,jnp.max(s,axis=0,keepdims=True))
            alpha=jnp.exp2(m_prev-m_new)
            prob=jnp.exp2(s-m_new).astype(bf16)
            m_sc[h:h+1,:]=m_new
            arows=slice(h*VROWS,(h+1)*VROWS)
            acc[arows,:]=acc[arows,:]*alpha+jnp.dot(vt[arows,rows],prob,preferred_element_type=f32)

    def body(kb,carry):
        code=codes[step,kb]
        @pl.when(code==1)
        def _(): tile(kb,False)
        @pl.when(code==2)
        def _(): tile(kb,True)
        return carry
    lax.fori_loop(0,nkb,body,0)
    outs=[]
    for h in range(heads):
        total=acc[h*VROWS+HDIM:h*VROWS+HDIM+1,:]
        outs.append(acc[h*VROWS:h*VROWS+HDIM,:]/total)
        lse_ref[h:h+1,:]=m_sc[h:h+1,:]+jnp.log2(total)
    for h in range(heads,8):
        lse_ref[h:h+1,:]=jnp.zeros((1,BLK),f32)
    o_ref[...]=jnp.concatenate(outs,axis=0).T.astype(bf16)

def attn_fwd(codes,q,k,v,segq,segk,block0,nblocks):
    rows,cols=k.shape
    heads=cols//HDIM
    full=lambda i,c:(0,0)
    return pl.pallas_call(
        attn_fwd_kernel,
        out_shape=(jax.ShapeDtypeStruct((nblocks*BLK,cols),bf16),jax.ShapeDtypeStruct((8,nblocks*BLK),f32)),
        grid_spec=pltpu.PrefetchScalarGridSpec(num_scalar_prefetch=1,grid=(nblocks,),
            in_specs=[pl.BlockSpec((BLK,cols),lambda i,c:(i+block0,0)),
                      pl.BlockSpec((rows,cols),full),pl.BlockSpec((rows,cols),full),
                      pl.BlockSpec((1,BLK),lambda i,c:(0,i+block0)),
                      pl.BlockSpec((rows,1),full)],
            out_specs=[pl.BlockSpec((BLK,cols),lambda i,c:(i,0)),pl.BlockSpec((8,BLK),lambda i,c:(0,i))],
            scratch_shapes=[pltpu.VMEM((heads*VROWS,rows),bf16),pltpu.VMEM((heads,BLK,128),bf16),
                            pltpu.VMEM((8,BLK),f32),pltpu.VMEM((heads*VROWS,BLK),f32)]),
        compiler_params=pltpu.CompilerParams(dimension_semantics=("arbitrary",)),
        name="attn_fwd",
        cost_estimate=work(64*nblocks*BLK*rows*cols),
    )(codes,q,k,v,segq,segk)

def swap_halves(x):
    n=x.shape[1]
    lane=lax.broadcasted_iota(jnp.int32,x.shape,1)
    up=pltpu.roll(x,n-HDIM//2,1)
    down=pltpu.roll(x,HDIM//2,1)
    return jnp.where(lane%HDIM<HDIM//2,up,down)

def attn_bwd_kernel(last, codes, q_ref,k_ref,v_ref,do_ref,o_ref,lse_ref,segq_ref,segk_ref,cos_ref,sin_ref,cosk_ref,sink_ref,*rest):
    if last:
        dk0_ref,dv0_ref,gq_ref,gk_ref,gv_ref,bsum_ref,kt,qm,dom,delta,dq,dk,dv=rest
    else:
        gq_ref,gk_ref,gv_ref,bsum_ref,kt,qm,dom,delta,dq,dk,dv=rest
    step=pl.program_id(0)
    nkb=pl.num_programs(0)
    nqb=q_ref.shape[0]//BLK
    heads=q_ref.shape[1]//HDIM
    scale=HDIM**-0.5
    def unrotate(x,cos,sin):
        out=[]
        for p in range(heads//2):
            xp=x[:,p*128:(p+1)*128]
            out.append(xp*cos-swap_halves(xp)*sin)
        return jnp.concatenate(out,axis=1)
    @pl.when(step==0)
    def _():
        def prep(blk,carry):
            rows=pl.ds(pl.multiple_of(blk*BLK,BLK),BLK)
            for p in range(heads//2):
                lanes=slice(p*128,(p+1)*128)
                qp=q_ref[rows,lanes]; dp=do_ref[rows,lanes]
                for w in range(2):
                    sel=lane_half(qp.shape,w)
                    qm[2*p+w,rows,:]=jnp.where(sel,qp,jnp.zeros_like(qp))
                    dom[2*p+w,rows,:]=jnp.where(sel,dp,jnp.zeros_like(dp))
            prod=(do_ref[rows,:].astype(f32)*o_ref[rows,:].astype(f32)).T
            for h in range(heads):
                delta[h:h+1,rows]=jnp.sum(prod[h*HDIM:(h+1)*HDIM,:],axis=0,keepdims=True)
            return carry
        lax.fori_loop(0,nqb,prep,0)
        dq[...]=jnp.zeros(dq.shape,f32)
        bsum_ref[...]=jnp.zeros(bsum_ref.shape,f32)
    kt[...]=k_ref[...].T
    if last:
        dk[...]=dk0_ref[...]
        dv[...]=dv0_ref[...]
    else:
        dk[...]=jnp.zeros(dk.shape,f32)
        dv[...]=jnp.zeros(dv.shape,f32)

    def tile(qb,masked):
        rows=pl.ds(pl.multiple_of(qb*BLK,BLK),BLK)
        if masked:
            allowed=segk_ref[:,0:1]==segq_ref[0:1,rows]
        for h in range(heads):
            p=h//2
            lanes=slice(p*128,(p+1)*128)
            hr=slice(h*HDIM,(h+1)*HDIM)
            qh=qm[h,rows,:]; dh=dom[h,rows,:]
            s=lax.dot_general(k_ref[:,lanes],qh,NT,preferred_element_type=f32)*(scale*LOG2E)
            prob=jnp.exp2(s-lse_ref[h:h+1,rows])
            if masked: prob=jnp.where(allowed,prob,0.0)
            dp=lax.dot_general(v_ref[:,lanes],dh,NT,preferred_element_type=f32)
            ds=(prob*(dp-delta[h:h+1,rows])).astype(bf16)
            dv[:,lanes]+=jnp.dot(prob.astype(bf16),dh,preferred_element_type=f32)
            dk[:,lanes]+=jnp.dot(ds,qh,preferred_element_type=f32)
            dq[hr,rows]+=jnp.dot(kt[hr,:],ds,preferred_element_type=f32)

    def body(qb,carry):
        code=codes[qb,step]
        @pl.when(code==1)
        def _(): tile(qb,False)
        @pl.when(code==2)
        def _(): tile(qb,True)
        return carry
    lax.fori_loop(0,nqb,body,0)

    if last:
        gk=unrotate(dk[...]*scale,cosk_ref[...],sink_ref[...]).astype(bf16)
        gv=dv[...].astype(bf16)
        gk_ref[...]=gk
        gv_ref[...]=gv
        bsum_ref[1:2,:]+=jnp.sum(gk.astype(f32),axis=0,keepdims=True)
        bsum_ref[2:3,:]+=jnp.sum(gv.astype(f32),axis=0,keepdims=True)
    else:
        gk_ref[...]=dk[...]
        gv_ref[...]=dv[...]

    @pl.when(step==nkb-1)
    def _():
        def fin(blk,carry):
            rows=pl.ds(pl.multiple_of(blk*BLK,BLK),BLK)
            gq=unrotate(dq[:,rows].T*scale,cos_ref[rows,:],sin_ref[rows,:]).astype(bf16)
            gq_ref[rows,:]=gq
            bsum_ref[0:1,:]+=jnp.sum(gq.astype(f32),axis=0,keepdims=True)
            return carry
        lax.fori_loop(0,nqb,fin,0)

def attn_bwd(codes,q,k,v,do,o,lse,segq,segk,cos,sin,part,carried):
    rows,cols=k.shape
    half=do.shape[0]
    heads=cols//HDIM
    nb=rows//BLK
    last=carried is not None
    mine=lambda n: pl.BlockSpec((half,n),lambda i,c:(part,0))
    here=lambda n: pl.BlockSpec((half,n),lambda i,c:(0,0))
    blk=lambda n: pl.BlockSpec((BLK,n),lambda i,c:(i,0))
    kdtype=bf16 if last else f32
    return pl.pallas_call(
        partial(attn_bwd_kernel,last),
        out_shape=(jax.ShapeDtypeStruct((half,cols),bf16),jax.ShapeDtypeStruct((rows,cols),kdtype),
                   jax.ShapeDtypeStruct((rows,cols),kdtype),jax.ShapeDtypeStruct((8,cols),f32)),
        grid_spec=pltpu.PrefetchScalarGridSpec(num_scalar_prefetch=1,grid=(nb,),
            in_specs=[mine(cols),blk(cols),blk(cols),here(cols),here(cols),pl.BlockSpec((8,half),lambda i,c:(0,0)),
                      pl.BlockSpec((1,half),lambda i,c:(0,part)),blk(1),mine(128),mine(128),blk(128),blk(128)]
                     +([blk(cols),blk(cols)] if last else []),
            out_specs=[here(cols),blk(cols),blk(cols),pl.BlockSpec((8,cols),lambda i,c:(0,0))],
            scratch_shapes=[pltpu.VMEM((cols,BLK),bf16),pltpu.VMEM((heads,half,128),bf16),pltpu.VMEM((heads,half,128),bf16),
                            pltpu.VMEM((8,half),f32),pltpu.VMEM((cols,half),f32),pltpu.VMEM((BLK,cols),f32),pltpu.VMEM((BLK,cols),f32)]),
        compiler_params=pltpu.CompilerParams(dimension_semantics=("arbitrary",)),
        name="attn_bwd",
        cost_estimate=work(1),
    )(codes,q,k,v,do,o,lse,segq,segk,cos,sin,cos,sin,*(carried or ()))

def block_codes(seg,pad_seg,skip_pad):
    sb=seg.reshape(-1,BLK)
    lo=jnp.min(sb,axis=1); hi=jnp.max(sb,axis=1)
    meet=(lo[:,None]<=hi[None,:])&(lo[None,:]<=hi[:,None])
    whole=(lo==hi)
    same=whole[:,None]&whole[None,:]&(lo[:,None]==lo[None,:])
    code=jnp.where(meet,jnp.where(same,1,2),0).astype(jnp.int32)
    if skip_pad:
        alive=lo<pad_seg
        code=jnp.where(alive[:,None]&alive[None,:],code,0)
    return code


def pick(i,n,a_ref,b_ref):
    return jnp.where(i<n,a_ref[...],b_ref[...])


def qkv_kernel(n, xa_ref, xb_ref, w_ref, b_ref, cos_ref, sin_ref, *rest):
    x=pick(pl.program_id(0),n,xa_ref,xb_ref)
    cos=cos_ref[...]; sin=sin_ref[...]
    for c,o_ref in enumerate(rest[-3:]):
        y=jnp.dot(x,w_ref[c],preferred_element_type=f32)+b_ref[c:c+1,:]
        if c<2:
            parts=[]
            for p in range(y.shape[1]//128):
                yp=y[:,p*128:(p+1)*128]
                parts.append(yp*cos+swap_halves(yp)*sin)
            y=jnp.concatenate(parts,axis=1)
        o_ref[...]=y.astype(bf16)


def two(tile,n,width):
    return [pl.BlockSpec((tile,width),lambda i:(jnp.minimum(i,n-1),0)),
            pl.BlockSpec((tile,width),lambda i:(jnp.maximum(i-n,0),0))]


def qkv_rows(xa,xb,w,b,cos,sin,part,full):
    rows,d=xa.shape
    cols=w.shape[2]
    tile=min(512,rows)
    n=rows//tile
    off=part*2*n
    row=lambda m: pl.BlockSpec((tile,m),lambda i:(i+off,0))
    kept=[] if full is None else list(full)
    return pl.pallas_call(
        partial(qkv_kernel,n),
        grid=(2*n,),
        out_shape=[jax.ShapeDtypeStruct((cos.shape[0],cols),bf16)]*3,
        in_specs=two(tile,n,d)+[pl.BlockSpec(w.shape,lambda i:(0,0,0)),pl.BlockSpec(b.shape,lambda i:(0,0)),
                  row(128),row(128)]+[pl.BlockSpec(memory_space=pl.ANY)]*len(kept),
        out_specs=[row(cols)]*3,
        input_output_aliases={6+i:i for i in range(len(kept))},
        compiler_params=pltpu.CompilerParams(dimension_semantics=("arbitrary",)),
        name="qkv",
        cost_estimate=work(20*rows*d*cols*2),
    )(xa,xb,w,b,cos,sin,*kept)


def mlp_kernel(n,xa_ref,xb_ref,ga_ref,gb_ref,w1_ref,b1_ref,w2_ref,*rest):
    hid_ref,gp_ref,na_ref,nb_ref,db_ref=rest[-5:]
    i=pl.program_id(0)
    @pl.when(i==0)
    def _():
        db_ref[...]=jnp.zeros(db_ref.shape,f32)
    pre=jnp.dot(pick(i,n,xa_ref,xb_ref),w1_ref[...],preferred_element_type=f32)+b1_ref[...]
    phi=0.5+0.5*lax.erf(pre*0.7071067811865476)
    hid_ref[...]=(pre*phi).astype(bf16)
    slope=phi+pre*(0.3989422804014327*jnp.exp2(pre*pre*(-0.5*LOG2E)))
    gh=lax.dot_general(pick(i,n,ga_ref,gb_ref),w2_ref[...],NT,preferred_element_type=f32)
    gp=(gh*slope).astype(bf16)
    gp_ref[...]=gp
    db_ref[...]+=jnp.sum(gp.astype(f32),axis=0,keepdims=True)
    gn=lax.dot_general(gp,w1_ref[...],NT,preferred_element_type=f32).astype(bf16)
    @pl.when(i<n)
    def _(): na_ref[...]=gn
    @pl.when(i>=n)
    def _(): nb_ref[...]=gn


def mlp_rows(xs,gs,w1,b1,w2,part,full):
    rows,d=xs[0].shape
    units=w1.shape[1]
    tile=min(256,rows)
    n=rows//tile
    off=part*2*n
    row=lambda m: pl.BlockSpec((tile,m),lambda i:(i+off,0))
    whole=lambda a: pl.BlockSpec(a.shape,lambda i:(0,0))
    kept=[] if full is None else list(full)
    return pl.pallas_call(
        partial(mlp_kernel,n),
        grid=(2*n,),
        out_shape=[jax.ShapeDtypeStruct((rows*4,units),bf16)]*2+[jax.ShapeDtypeStruct((rows,d),bf16)]*2+
                  [jax.ShapeDtypeStruct((1,units),f32)],
        in_specs=two(tile,n,d)+two(tile,n,d)+[whole(w1),whole(b1),whole(w2)]+[pl.BlockSpec(memory_space=pl.ANY)]*len(kept),
        out_specs=[row(units),row(units)]+two(tile,n,d)+[pl.BlockSpec((1,units),lambda i:(0,0))],
        input_output_aliases={7+i:i for i in range(len(kept))},
        compiler_params=pltpu.CompilerParams(dimension_semantics=("arbitrary",)),
        name="mlp",
        cost_estimate=work(12*rows*d*units),
    )(*xs,*gs,w1,b1,w2,*kept)


def back_kernel(n,gq_ref,gk_ref,gv_ref,w_ref,oa_ref,ob_ref):
    i=pl.program_id(0)
    y=lax.dot_general(gq_ref[...],w_ref[0],NT,preferred_element_type=f32)
    y=y+lax.dot_general(gk_ref[...],w_ref[1],NT,preferred_element_type=f32)
    y=(y+lax.dot_general(gv_ref[...],w_ref[2],NT,preferred_element_type=f32)).astype(bf16)
    @pl.when(i<n)
    def _(): oa_ref[...]=y
    @pl.when(i>=n)
    def _(): ob_ref[...]=y


def back_rows(gq,gk,gv,w,part):
    half,cols=gq.shape
    rows=half//2
    d=w.shape[1]
    tile=min(512,rows)
    n=rows//tile
    off=part*2*n
    row=pl.BlockSpec((tile,cols),lambda i:(i+off,0))
    return pl.pallas_call(
        partial(back_kernel,n),
        grid=(2*n,),
        out_shape=[jax.ShapeDtypeStruct((rows,d),bf16)]*2,
        in_specs=[pl.BlockSpec((tile,cols),lambda i:(i,0)),row,row,pl.BlockSpec(w.shape,lambda i:(0,0,0))],
        out_specs=two(tile,n,d),
        compiler_params=pltpu.CompilerParams(dimension_semantics=("arbitrary",)),
        name="back",
        cost_estimate=work(1),
    )(gq,gk,gv,w)


def norm_rows(values_in, gain_row, shift_row):
    row_mean = jnp.mean(values_in, axis=-1, keepdims=True)
    centred = values_in - row_mean
    variance = jnp.mean(centred * centred, axis=-1, keepdims=True)
    return centred * lax.rsqrt(variance + 1e-06) * gain_row + shift_row


def flip(x,bits):
    n=lax.axis_size("tensor")
    return lax.ppermute(x,"tensor",[(i,i^bits) for i in range(n)])


def pair_sum(mine,other):
    return mine.astype(f32)+flip(other,1).astype(f32)


def dp_flip(x,bit):
    n=lax.axis_size("dp")
    return lax.ppermute(x,"dp",[(i,i^(1<<bit)) for i in range(n)])


class DpSum:
    def __init__(self,x,order):
        self.cur=x
        self.stages=[(bit,True) for bit in order]+[(bit,False) for bit in reversed(order)]
        self.at=0

    def operand(self):
        bit,halving=self.stages[self.at]
        if not halving: return self.cur
        up=(lax.axis_index("dp")>>bit)&1
        halves=self.cur.reshape(2,-1,self.cur.shape[1])
        self.kept=lax.dynamic_index_in_dim(halves,up,0,False)
        return lax.dynamic_index_in_dim(halves,1-up,0,False)

    def start(self,operand):
        self.sent=operand
        self.got=dp_flip(operand,self.stages[self.at][0])

    def finish(self,got):
        bit,halving=self.stages[self.at]
        self.at+=1
        if halving:
            self.cur=(self.kept.astype(f32)+got.astype(f32)).astype(bf16)
        else:
            up=((lax.axis_index("dp")>>bit)&1)==1
            self.cur=jnp.concatenate([jnp.where(up,got,self.sent),jnp.where(up,self.sent,got)],axis=0)

    def rest(self):
        while self.at<len(self.stages):
            self.start(self.operand())
            self.finish(self.got)
        return self.cur


def begin(sums,value):
    value,*sends=lax.optimization_barrier((value,*[s.operand() for s in sums]))
    for s,x in zip(sums,sends): s.start(x)
    return value


def settle(sums,value):
    value,*gots=lax.optimization_barrier((value,*[s.got for s in sums]))
    for s,x in zip(sums,gots): s.finish(x)
    return value


def all_sum(x):
    for bits in (1,2):
        x=x+flip(x,bits)
    for bit in range(lax.axis_size("dp").bit_length()-1):
        x=x+dp_flip(x,bit)
    return x


def after(x,*others):
    return lax.optimization_barrier((x,)+others)[0]


def shards(tokens,grad_out,lengths,coords,w_qkv,b_qkv,w_proj,w_fc1,b_fc1,w_fc2,norm_gains,shift_biases):
    tok=tokens.shape[0]
    ranks=lax.axis_size("tensor")
    bits=lax.axis_size("dp").bit_length()-1
    me=lax.axis_index("tensor")
    rows_all=tok*ranks
    half=rows_all//2
    cols=w_qkv.shape[2]
    ends=jnp.cumsum(lengths[0])
    slots=lengths.shape[1]
    rel=jnp.arange(rows_all,dtype=jnp.int32)
    place=((rel//tok)^me)*tok+rel%tok
    seg=jnp.sum((place[:,None]>=ends[None,:]).astype(jnp.int32),axis=1)
    live=(place[:tok]<ends[-1]).astype(f32)[:,None]
    cgrp=jnp.concatenate([lax.dynamic_slice_in_dim(coords,(me^j)*tok,tok,1) for j in range(ranks)],axis=1).astype(f32)
    lane=jnp.arange(128,dtype=jnp.int32)
    pair=lane%(HDIM//2)
    freq=100.0**(-(pair//3).astype(f32)/(HDIM//2//3+1))
    angle=jnp.zeros((rows_all,128),f32)
    for a in range(3):
        angle=angle+cgrp[a][:,None]*jnp.where(pair%3==a,freq,0.0)[None,:]
    cos=jnp.cos(angle)
    sin=jnp.sin(angle)*jnp.where(lane%HDIM<HDIM//2,-1.0,1.0)[None,:]
    gains=norm_gains.astype(f32)
    shifts=shift_biases.astype(f32)
    x_rows=tokens.astype(f32)

    normed_one,norm_one_back=jax.vjp(norm_rows,x_rows,gains[0],shifts[0])
    low_one=normed_one.astype(bf16)
    far=flip(low_one,2)
    near=flip(low_one,1)
    grad_y=grad_out.astype(f32)*live
    grad_mlp=grad_y.astype(bf16)

    bq=b_qkv.astype(f32)
    qkv=qkv_rows(low_one,near,w_qkv,bq,cos,sin,0,None)
    far,*qkv=lax.optimization_barrier((far,*qkv))
    far_pair=flip(far,1)
    q,k,v=qkv_rows(far,far_pair,w_qkv,bq,cos,sin,1,qkv)
    n1=[low_one,near,far,far_pair]
    late,q,k,v=lax.optimization_barrier((grad_mlp,q,k,v))
    gm=[late,flip(late,1),flip(late,2)]
    segq=seg[None,:]; segk=seg[:,None]
    hb=half//BLK
    codes=block_codes(seg,slots,False)
    att_far,lse_far=attn_fwd(codes[hb:],q,k,v,segq,segk,hb,hb)
    proj=lambda a: jnp.dot(a,w_proj,preferred_element_type=f32).astype(bf16)
    across=pair_sum(proj(att_far[tok:]),proj(att_far[:tok])).astype(bf16)
    q_late,across,g2=lax.optimization_barrier((q,across,gm[2]))
    gm=[gm[0],gm[1],g2,flip(g2,1)]
    across=flip(across,3)
    att_near,lse_near=attn_fwd(codes[:hb],q_late,k,v,segq,segk,0,hb)
    across,att_near=lax.optimization_barrier((across,att_near))
    mine=pair_sum(proj(att_near[:tok]),proj(att_near[tok:]))
    resid_one=x_rows+mine+across.astype(f32)+shifts[2]
    normed_two,norm_two_back=jax.vjp(norm_rows,resid_one,gains[1],shifts[1])
    low_two=normed_two.astype(bf16)
    far=flip(low_two,2)
    near=flip(low_two,1)
    b1=b_fc1.astype(f32)[None,:]
    hid,gp,gn0,gn1,db0=mlp_rows((low_two,near),(gm[0],gm[1]),w_fc1,b1,w_fc2,0,None)
    far,hid,gp=lax.optimization_barrier((far,hid,gp))
    far_pair=flip(far,1)
    hid,gp,gn2,gn3,db1=mlp_rows((far,far_pair),(gm[2],gm[3]),w_fc1,b1,w_fc2,1,(hid,gp))
    db=db0+db1
    across=pair_sum(gn3,gn2).astype(bf16)
    hid,gp,across=lax.optimization_barrier((hid,gp,across))
    across=flip(across,3)
    mine=pair_sum(gn0,gn1)
    tn=lambda a,b: lax.dot_general(a,b,(((0,),(0,)),((),())),preferred_element_type=f32)
    grad_w1=tn(jnp.concatenate([low_two,near,far,far_pair],axis=0),gp).astype(bf16)
    grad_w2=tn(hid,jnp.concatenate(gm,axis=0)).astype(bf16)
    across,grad_w1,grad_w2=lax.optimization_barrier((across,grad_w1,grad_w2))
    wsum=lax.psum_scatter(jnp.concatenate([grad_w1,grad_w2],axis=0),"dp",scatter_dimension=0,tiled=True)
    grad_resid_two,grad_gain_two,grad_shift_two=norm_two_back(mine+across.astype(f32))

    grad_resid_one=grad_y+grad_resid_two
    grad_attn=grad_resid_one.astype(bf16)
    far=flip(grad_attn,2)
    near=flip(grad_attn,1)
    ghead=lambda a: lax.dot_general(a,w_proj,NT,preferred_element_type=f32).astype(bf16)
    bcodes=block_codes(seg,slots,True)
    do_near=jnp.concatenate([ghead(grad_attn),ghead(near)],axis=0)
    early=jnp.stack([grad_gain_two,grad_shift_two,jnp.sum(grad_attn,axis=0,dtype=f32),jnp.sum(grad_mlp,axis=0,dtype=f32)])
    early=early+flip(early,1)
    early=early+flip(early,2)
    do_near,early=lax.optimization_barrier((do_near,early))
    gq_near,dk,dv,bs0=attn_bwd(bcodes[:hb],q,k,v,do_near,att_near,lse_near,segq,segk,cos,sin,0,None)
    far,dk,dv=lax.optimization_barrier((far,dk,dv))
    far_pair=flip(far,1)
    do_far=jnp.concatenate([ghead(far),ghead(far_pair)],axis=0)
    alla=jnp.concatenate([grad_attn,near,far,far_pair],axis=0)
    grad_proj=tn(jnp.concatenate([att_near,att_far],axis=0),alla).astype(bf16)
    do_far,grad_proj=lax.optimization_barrier((do_far,grad_proj))
    gq_far,gk,gv,bs1=attn_bwd(bcodes[hb:],q,k,v,do_far,att_far,lse_far,segq,segk,cos,sin,1,(dk,dv))
    gk,wsum=lax.optimization_barrier((gk,wsum))
    wsum=lax.all_gather(wsum,"dp",axis=0,tiled=True)
    grad_w1,grad_w2=wsum[:tokens.shape[1]],wsum[tokens.shape[1]:]
    r2,r3=back_rows(gq_far,gk,gv,w_qkv,1)
    across=pair_sum(r3,r2).astype(bf16)
    gq_near,gk,gv,across,early=lax.optimization_barrier((gq_near,gk,gv,across,early))
    across=flip(across,3)
    g_all=jnp.concatenate([jnp.concatenate([gq_near,gq_far],axis=0),gk,gv],axis=1)
    grad_wqkv=tn(jnp.concatenate(n1,axis=0),g_all).astype(bf16)
    d=tokens.shape[1]
    sizes=(3*cols,db.shape[1],early.size)
    pad=(-sum(sizes))%(8*cols<<bits)
    small=jnp.concatenate([(bs0+bs1)[:3].reshape(-1),db[0],early.reshape(-1),jnp.zeros((pad,),f32)]).astype(bf16).reshape(-1,cols)
    tail_a=DpSum(jnp.concatenate([grad_wqkv[:,:cols],grad_wqkv[:,cols:2*cols]],axis=0),tuple(range(bits)))
    tail_b=DpSum(jnp.concatenate([grad_wqkv[:,2*cols:],grad_proj.reshape(-1,cols),small],axis=0),(1,0)+tuple(range(2,bits)))
    tails=(tail_a,tail_b)
    for t in tails: t.start(t.operand())
    *gots,hid,gq_near=lax.optimization_barrier((tail_a.got,tail_b.got,hid,gq_near))
    for t,got in zip(tails,gots): t.finish(got)
    tail_a,tail_b=[t.rest() for t in tails]
    r0,r1=back_rows(gq_near,gk,gv,w_qkv,0)
    mine=pair_sum(r0,r1)
    o=[jnp.dot(hid[j*tok:(j+1)*tok],w_fc2,preferred_element_type=f32).astype(bf16) for j in range(ranks)]
    o_across=flip(pair_sum(o[3],o[2]).astype(bf16),3)
    output=(resid_one+pair_sum(o[0],o[1])+o_across.astype(f32)+shifts[3]).astype(bf16)
    grad_wqkv=jnp.stack([tail_a[:d],tail_a[d:],tail_b[:d]]).astype(f32)
    grad_wproj=tail_b[d:2*d].reshape(cols,d).astype(f32)
    small=tail_b[2*d:].reshape(-1).astype(f32)
    grad_bqkv=small[:sizes[0]].reshape(3,cols)
    grad_b1=small[sizes[0]:sizes[0]+sizes[1]]
    early=small[sizes[0]+sizes[1]:sum(sizes)].reshape(4,d)
    grad_x_norm,grad_gain_one,grad_shift_one=norm_one_back(mine+across.astype(f32))
    grad_tokens=(grad_resid_one+grad_x_norm).astype(bf16)
    one=all_sum(jnp.stack([grad_gain_one,grad_shift_one]))
    return (output,grad_tokens,grad_wqkv,grad_bqkv,grad_wproj,grad_w1.astype(f32),grad_b1,grad_w2.astype(f32),
            jnp.stack([one[0],early[0]]),jnp.stack([one[1],early[1],early[2],early[3]]))


def solution(mesh):
    rows=P(("dp","tensor"),None)
    return jax.shard_map(shards,mesh=mesh,
        in_specs=(rows,rows,P("dp",None),P(None,"dp"),P(None,None,"tensor"),P(None,"tensor"),P("tensor",None),
                  P(None,"tensor"),P("tensor"),P("tensor",None),P(),P()),
        out_specs=(rows,rows,P(None,None,"tensor"),P(None,"tensor"),P("tensor",None),P(None,"tensor"),P("tensor"),
                   P("tensor",None),P(),P()),
        check_vma=False)
```

```python
from functools import partial

import jax
import jax.numpy as jnp
from jax import lax
from jax.experimental import pallas as pl
from jax.experimental.pallas import tpu as pltpu
from jax.sharding import PartitionSpec as P

HDIM=64
LOG2E=1.4426950408889634
LN2=0.6931471805599453
f32=jnp.float32; bf16=jnp.bfloat16
BLK=256
VROWS=80
NT=(((1,),(1,)),((),()))

def work(flops):
    return pl.CostEstimate(flops=flops,bytes_accessed=0,transcendentals=0)

def lane_half(shape, which):
    lane=lax.broadcasted_iota(jnp.int32, shape, 1)
    return (lane//HDIM)%2==which

def attn_fwd_kernel(codes, q_ref, k_ref, v_ref, segq_ref, segk_ref, o_ref, lse_ref, vt, qm, m_sc, acc):
    step=pl.program_id(0)
    nkb=k_ref.shape[0]//BLK
    heads=q_ref.shape[1]//HDIM
    @pl.when(step==0)
    def _():
        for blk in range(nkb):
            rows=pl.ds(blk*BLK,BLK)
            vT=v_ref[rows,:].T
            for h in range(heads):
                vt[h*VROWS:h*VROWS+HDIM, rows]=vT[h*HDIM:(h+1)*HDIM,:]
        for h in range(heads):
            vt[h*VROWS+HDIM:(h+1)*VROWS,:]=jnp.ones((VROWS-HDIM,vt.shape[1]),bf16)
    for p in range(heads//2):
        qp=q_ref[:,p*128:(p+1)*128]
        for w in range(2):
            qm[2*p+w]=jnp.where(lane_half(qp.shape,w),qp,jnp.zeros_like(qp))
    m_sc[...]=jnp.full(m_sc.shape,-1e30,f32)
    acc[...]=jnp.zeros(acc.shape,f32)
    scale=HDIM**-0.5*LOG2E

    def tile(kb,masked):
        rows=pl.ds(pl.multiple_of(kb*BLK,BLK),BLK)
        if masked:
            allowed=segk_ref[rows,:][:,0:1]==segq_ref[0:1,:]
        for h in range(heads):
            p=h//2
            s=lax.dot_general(k_ref[rows,p*128:(p+1)*128],qm[h],NT,preferred_element_type=f32)*scale
            if masked: s=jnp.where(allowed,s,-1e30)
            m_prev=m_sc[h:h+1,:]
            m_new=jnp.maximum(m_prev,jnp.max(s,axis=0,keepdims=True))
            alpha=jnp.exp2(m_prev-m_new)
            prob=jnp.exp2(s-m_new).astype(bf16)
            m_sc[h:h+1,:]=m_new
            arows=slice(h*VROWS,(h+1)*VROWS)
            acc[arows,:]=acc[arows,:]*alpha+jnp.dot(vt[arows,rows],prob,preferred_element_type=f32)

    def body(kb,carry):
        code=codes[step,kb]
        @pl.when(code==1)
        def _(): tile(kb,False)
        @pl.when(code==2)
        def _(): tile(kb,True)
        return carry
    lax.fori_loop(0,nkb,body,0)
    outs=[]
    for h in range(heads):
        total=acc[h*VROWS+HDIM:h*VROWS+HDIM+1,:]
        outs.append(acc[h*VROWS:h*VROWS+HDIM,:]/total)
        lse_ref[h:h+1,:]=m_sc[h:h+1,:]+jnp.log2(total)
    for h in range(heads,8):
        lse_ref[h:h+1,:]=jnp.zeros((1,BLK),f32)
    o_ref[...]=jnp.concatenate(outs,axis=0).T.astype(bf16)

def attn_fwd(codes,q,k,v,segq,segk,block0,nblocks):
    rows,cols=k.shape
    heads=cols//HDIM
    full=lambda i,c:(0,0)
    return pl.pallas_call(
        attn_fwd_kernel,
        out_shape=(jax.ShapeDtypeStruct((nblocks*BLK,cols),bf16),jax.ShapeDtypeStruct((8,nblocks*BLK),f32)),
        grid_spec=pltpu.PrefetchScalarGridSpec(num_scalar_prefetch=1,grid=(nblocks,),
            in_specs=[pl.BlockSpec((BLK,cols),lambda i,c:(i+block0,0)),
                      pl.BlockSpec((rows,cols),full),pl.BlockSpec((rows,cols),full),
                      pl.BlockSpec((1,BLK),lambda i,c:(0,i+block0)),
                      pl.BlockSpec((rows,1),full)],
            out_specs=[pl.BlockSpec((BLK,cols),lambda i,c:(i,0)),pl.BlockSpec((8,BLK),lambda i,c:(0,i))],
            scratch_shapes=[pltpu.VMEM((heads*VROWS,rows),bf16),pltpu.VMEM((heads,BLK,128),bf16),
                            pltpu.VMEM((8,BLK),f32),pltpu.VMEM((heads*VROWS,BLK),f32)]),
        compiler_params=pltpu.CompilerParams(dimension_semantics=("arbitrary",)),
        name="attn_fwd",
        cost_estimate=work(64*nblocks*BLK*rows*cols),
    )(codes,q,k,v,segq,segk)

def swap_halves(x):
    n=x.shape[1]
    lane=lax.broadcasted_iota(jnp.int32,x.shape,1)
    up=pltpu.roll(x,n-HDIM//2,1)
    down=pltpu.roll(x,HDIM//2,1)
    return jnp.where(lane%HDIM<HDIM//2,up,down)

def attn_bwd_kernel(last, codes, q_ref,k_ref,v_ref,do_ref,o_ref,lse_ref,segq_ref,segk_ref,cos_ref,sin_ref,cosk_ref,sink_ref,*rest):
    if last:
        dk0_ref,dv0_ref,gq_ref,gk_ref,gv_ref,bsum_ref,kt,qm,dom,delta,dq,dk,dv=rest
    else:
        gq_ref,gk_ref,gv_ref,bsum_ref,kt,qm,dom,delta,dq,dk,dv=rest
    step=pl.program_id(0)
    nkb=pl.num_programs(0)
    nqb=q_ref.shape[0]//BLK
    heads=q_ref.shape[1]//HDIM
    scale=HDIM**-0.5
    def unrotate(x,cos,sin):
        out=[]
        for p in range(heads//2):
            xp=x[:,p*128:(p+1)*128]
            out.append(xp*cos-swap_halves(xp)*sin)
        return jnp.concatenate(out,axis=1)
    @pl.when(step==0)
    def _():
        def prep(blk,carry):
            rows=pl.ds(pl.multiple_of(blk*BLK,BLK),BLK)
            for p in range(heads//2):
                lanes=slice(p*128,(p+1)*128)
                qp=q_ref[rows,lanes]; dp=do_ref[rows,lanes]
                for w in range(2):
                    sel=lane_half(qp.shape,w)
                    qm[2*p+w,rows,:]=jnp.where(sel,qp,jnp.zeros_like(qp))
                    dom[2*p+w,rows,:]=jnp.where(sel,dp,jnp.zeros_like(dp))
            prod=(do_ref[rows,:].astype(f32)*o_ref[rows,:].astype(f32)).T
            for h in range(heads):
                delta[h:h+1,rows]=jnp.sum(prod[h*HDIM:(h+1)*HDIM,:],axis=0,keepdims=True)
            return carry
        lax.fori_loop(0,nqb,prep,0)
        dq[...]=jnp.zeros(dq.shape,f32)
        bsum_ref[...]=jnp.zeros(bsum_ref.shape,f32)
    kt[...]=k_ref[...].T
    if last:
        dk[...]=dk0_ref[...]
        dv[...]=dv0_ref[...]
    else:
        dk[...]=jnp.zeros(dk.shape,f32)
        dv[...]=jnp.zeros(dv.shape,f32)

    def tile(qb,masked):
        rows=pl.ds(pl.multiple_of(qb*BLK,BLK),BLK)
        if masked:
            allowed=segk_ref[:,0:1]==segq_ref[0:1,rows]
        for h in range(heads):
            p=h//2
            lanes=slice(p*128,(p+1)*128)
            hr=slice(h*HDIM,(h+1)*HDIM)
            qh=qm[h,rows,:]; dh=dom[h,rows,:]
            s=lax.dot_general(k_ref[:,lanes],qh,NT,preferred_element_type=f32)*(scale*LOG2E)
            prob=jnp.exp2(s-lse_ref[h:h+1,rows])
            if masked: prob=jnp.where(allowed,prob,0.0)
            dp=lax.dot_general(v_ref[:,lanes],dh,NT,preferred_element_type=f32)
            ds=(prob*(dp-delta[h:h+1,rows])).astype(bf16)
            dv[:,lanes]+=jnp.dot(prob.astype(bf16),dh,preferred_element_type=f32)
            dk[:,lanes]+=jnp.dot(ds,qh,preferred_element_type=f32)
            dq[hr,rows]+=jnp.dot(kt[hr,:],ds,preferred_element_type=f32)

    def body(qb,carry):
        code=codes[qb,step]
        @pl.when(code==1)
        def _(): tile(qb,False)
        @pl.when(code==2)
        def _(): tile(qb,True)
        return carry
    lax.fori_loop(0,nqb,body,0)

    if last:
        gk=unrotate(dk[...]*scale,cosk_ref[...],sink_ref[...]).astype(bf16)
        gv=dv[...].astype(bf16)
        gk_ref[...]=gk
        gv_ref[...]=gv
        bsum_ref[1:2,:]+=jnp.sum(gk.astype(f32),axis=0,keepdims=True)
        bsum_ref[2:3,:]+=jnp.sum(gv.astype(f32),axis=0,keepdims=True)
    else:
        gk_ref[...]=dk[...]
        gv_ref[...]=dv[...]

    @pl.when(step==nkb-1)
    def _():
        def fin(blk,carry):
            rows=pl.ds(pl.multiple_of(blk*BLK,BLK),BLK)
            gq=unrotate(dq[:,rows].T*scale,cos_ref[rows,:],sin_ref[rows,:]).astype(bf16)
            gq_ref[rows,:]=gq
            bsum_ref[0:1,:]+=jnp.sum(gq.astype(f32),axis=0,keepdims=True)
            return carry
        lax.fori_loop(0,nqb,fin,0)

def attn_bwd(codes,q,k,v,do,o,lse,segq,segk,cos,sin,part,carried):
    rows,cols=k.shape
    half=do.shape[0]
    heads=cols//HDIM
    nb=rows//BLK
    last=carried is not None
    mine=lambda n: pl.BlockSpec((half,n),lambda i,c:(part,0))
    here=lambda n: pl.BlockSpec((half,n),lambda i,c:(0,0))
    blk=lambda n: pl.BlockSpec((BLK,n),lambda i,c:(i,0))
    kdtype=bf16 if last else f32
    return pl.pallas_call(
        partial(attn_bwd_kernel,last),
        out_shape=(jax.ShapeDtypeStruct((half,cols),bf16),jax.ShapeDtypeStruct((rows,cols),kdtype),
                   jax.ShapeDtypeStruct((rows,cols),kdtype),jax.ShapeDtypeStruct((8,cols),f32)),
        grid_spec=pltpu.PrefetchScalarGridSpec(num_scalar_prefetch=1,grid=(nb,),
            in_specs=[mine(cols),blk(cols),blk(cols),here(cols),here(cols),pl.BlockSpec((8,half),lambda i,c:(0,0)),
                      pl.BlockSpec((1,half),lambda i,c:(0,part)),blk(1),mine(128),mine(128),blk(128),blk(128)]
                     +([blk(cols),blk(cols)] if last else []),
            out_specs=[here(cols),blk(cols),blk(cols),pl.BlockSpec((8,cols),lambda i,c:(0,0))],
            scratch_shapes=[pltpu.VMEM((cols,BLK),bf16),pltpu.VMEM((heads,half,128),bf16),pltpu.VMEM((heads,half,128),bf16),
                            pltpu.VMEM((8,half),f32),pltpu.VMEM((cols,half),f32),pltpu.VMEM((BLK,cols),f32),pltpu.VMEM((BLK,cols),f32)]),
        compiler_params=pltpu.CompilerParams(dimension_semantics=("arbitrary",)),
        name="attn_bwd",
        cost_estimate=work(1),
    )(codes,q,k,v,do,o,lse,segq,segk,cos,sin,cos,sin,*(carried or ()))

def block_codes(seg,pad_seg,skip_pad):
    sb=seg.reshape(-1,BLK)
    lo=jnp.min(sb,axis=1); hi=jnp.max(sb,axis=1)
    meet=(lo[:,None]<=hi[None,:])&(lo[None,:]<=hi[:,None])
    whole=(lo==hi)
    same=whole[:,None]&whole[None,:]&(lo[:,None]==lo[None,:])
    code=jnp.where(meet,jnp.where(same,1,2),0).astype(jnp.int32)
    if skip_pad:
        alive=lo<pad_seg
        code=jnp.where(alive[:,None]&alive[None,:],code,0)
    return code


def pick(i,n,a_ref,b_ref):
    return jnp.where(i<n,a_ref[...],b_ref[...])


def qkv_kernel(n, xa_ref, xb_ref, w_ref, b_ref, cos_ref, sin_ref, *rest):
    x=pick(pl.program_id(0),n,xa_ref,xb_ref)
    cos=cos_ref[...]; sin=sin_ref[...]
    for c,o_ref in enumerate(rest[-3:]):
        y=jnp.dot(x,w_ref[c],preferred_element_type=f32)+b_ref[c:c+1,:]
        if c<2:
            parts=[]
            for p in range(y.shape[1]//128):
                yp=y[:,p*128:(p+1)*128]
                parts.append(yp*cos+swap_halves(yp)*sin)
            y=jnp.concatenate(parts,axis=1)
        o_ref[...]=y.astype(bf16)


def two(tile,n,width):
    return [pl.BlockSpec((tile,width),lambda i:(jnp.minimum(i,n-1),0)),
            pl.BlockSpec((tile,width),lambda i:(jnp.maximum(i-n,0),0))]


def qkv_rows(xa,xb,w,b,cos,sin,part,full):
    rows,d=xa.shape
    cols=w.shape[2]
    tile=min(512,rows)
    n=rows//tile
    off=part*2*n
    row=lambda m: pl.BlockSpec((tile,m),lambda i:(i+off,0))
    kept=[] if full is None else list(full)
    return pl.pallas_call(
        partial(qkv_kernel,n),
        grid=(2*n,),
        out_shape=[jax.ShapeDtypeStruct((cos.shape[0],cols),bf16)]*3,
        in_specs=two(tile,n,d)+[pl.BlockSpec(w.shape,lambda i:(0,0,0)),pl.BlockSpec(b.shape,lambda i:(0,0)),
                  row(128),row(128)]+[pl.BlockSpec(memory_space=pl.ANY)]*len(kept),
        out_specs=[row(cols)]*3,
        input_output_aliases={6+i:i for i in range(len(kept))},
        compiler_params=pltpu.CompilerParams(dimension_semantics=("arbitrary",)),
        name="qkv",
        cost_estimate=work(20*rows*d*cols*2),
    )(xa,xb,w,b,cos,sin,*kept)


def mlp_kernel(n,xa_ref,xb_ref,ga_ref,gb_ref,w1_ref,b1_ref,w2_ref,*rest):
    hid_ref,gp_ref,na_ref,nb_ref,db_ref=rest[-5:]
    i=pl.program_id(0)
    @pl.when(i==0)
    def _():
        db_ref[...]=jnp.zeros(db_ref.shape,f32)
    pre=jnp.dot(pick(i,n,xa_ref,xb_ref),w1_ref[...],preferred_element_type=f32)+b1_ref[...]
    phi=0.5+0.5*lax.erf(pre*0.7071067811865476)
    hid_ref[...]=(pre*phi).astype(bf16)
    slope=phi+pre*(0.3989422804014327*jnp.exp2(pre*pre*(-0.5*LOG2E)))
    gh=lax.dot_general(pick(i,n,ga_ref,gb_ref),w2_ref[...],NT,preferred_element_type=f32)
    gp=(gh*slope).astype(bf16)
    gp_ref[...]=gp
    db_ref[...]+=jnp.sum(gp.astype(f32),axis=0,keepdims=True)
    gn=lax.dot_general(gp,w1_ref[...],NT,preferred_element_type=f32).astype(bf16)
    @pl.when(i<n)
    def _(): na_ref[...]=gn
    @pl.when(i>=n)
    def _(): nb_ref[...]=gn


def mlp_rows(xs,gs,w1,b1,w2,part,full):
    rows,d=xs[0].shape
    units=w1.shape[1]
    tile=min(256,rows)
    n=rows//tile
    off=part*2*n
    row=lambda m: pl.BlockSpec((tile,m),lambda i:(i+off,0))
    whole=lambda a: pl.BlockSpec(a.shape,lambda i:(0,0))
    kept=[] if full is None else list(full)
    return pl.pallas_call(
        partial(mlp_kernel,n),
        grid=(2*n,),
        out_shape=[jax.ShapeDtypeStruct((rows*4,units),bf16)]*2+[jax.ShapeDtypeStruct((rows,d),bf16)]*2+
                  [jax.ShapeDtypeStruct((1,units),f32)],
        in_specs=two(tile,n,d)+two(tile,n,d)+[whole(w1),whole(b1),whole(w2)]+[pl.BlockSpec(memory_space=pl.ANY)]*len(kept),
        out_specs=[row(units),row(units)]+two(tile,n,d)+[pl.BlockSpec((1,units),lambda i:(0,0))],
        input_output_aliases={7+i:i for i in range(len(kept))},
        compiler_params=pltpu.CompilerParams(dimension_semantics=("arbitrary",)),
        name="mlp",
        cost_estimate=work(12*rows*d*units),
    )(*xs,*gs,w1,b1,w2,*kept)


def back_kernel(n,gq_ref,gk_ref,gv_ref,w_ref,oa_ref,ob_ref):
    i=pl.program_id(0)
    y=lax.dot_general(gq_ref[...],w_ref[0],NT,preferred_element_type=f32)
    y=y+lax.dot_general(gk_ref[...],w_ref[1],NT,preferred_element_type=f32)
    y=(y+lax.dot_general(gv_ref[...],w_ref[2],NT,preferred_element_type=f32)).astype(bf16)
    @pl.when(i<n)
    def _(): oa_ref[...]=y
    @pl.when(i>=n)
    def _(): ob_ref[...]=y


def back_rows(gq,gk,gv,w,part):
    half,cols=gq.shape
    rows=half//2
    d=w.shape[1]
    tile=min(512,rows)
    n=rows//tile
    off=part*2*n
    row=pl.BlockSpec((tile,cols),lambda i:(i+off,0))
    return pl.pallas_call(
        partial(back_kernel,n),
        grid=(2*n,),
        out_shape=[jax.ShapeDtypeStruct((rows,d),bf16)]*2,
        in_specs=[pl.BlockSpec((tile,cols),lambda i:(i,0)),row,row,pl.BlockSpec(w.shape,lambda i:(0,0,0))],
        out_specs=two(tile,n,d),
        compiler_params=pltpu.CompilerParams(dimension_semantics=("arbitrary",)),
        name="back",
        cost_estimate=work(1),
    )(gq,gk,gv,w)


def norm_rows(values_in, gain_row, shift_row):
    row_mean = jnp.mean(values_in, axis=-1, keepdims=True)
    centred = values_in - row_mean
    variance = jnp.mean(centred * centred, axis=-1, keepdims=True)
    return centred * lax.rsqrt(variance + 1e-06) * gain_row + shift_row


def flip(x,bits):
    n=lax.axis_size("tensor")
    return lax.ppermute(x,"tensor",[(i,i^bits) for i in range(n)])


def pair_sum(mine,other):
    return mine.astype(f32)+flip(other,1).astype(f32)


def dp_flip(x,bit):
    n=lax.axis_size("dp")
    return lax.ppermute(x,"dp",[(i,i^(1<<bit)) for i in range(n)])


class DpSum:
    def __init__(self,x,order):
        self.cur=x
        self.stages=[(bit,True) for bit in order]+[(bit,False) for bit in reversed(order)]
        self.at=0

    def operand(self):
        bit,halving=self.stages[self.at]
        if not halving: return self.cur
        up=(lax.axis_index("dp")>>bit)&1
        halves=self.cur.reshape(2,-1,self.cur.shape[1])
        self.kept=lax.dynamic_index_in_dim(halves,up,0,False)
        return lax.dynamic_index_in_dim(halves,1-up,0,False)

    def start(self,operand):
        self.sent=operand
        self.got=dp_flip(operand,self.stages[self.at][0])

    def finish(self,got):
        bit,halving=self.stages[self.at]
        self.at+=1
        if halving:
            self.cur=(self.kept.astype(f32)+got.astype(f32)).astype(bf16)
        else:
            up=((lax.axis_index("dp")>>bit)&1)==1
            self.cur=jnp.concatenate([jnp.where(up,got,self.sent),jnp.where(up,self.sent,got)],axis=0)

    def rest(self):
        while self.at<len(self.stages):
            self.start(self.operand())
            self.finish(self.got)
        return self.cur


def begin(sums,value):
    value,*sends=lax.optimization_barrier((value,*[s.operand() for s in sums]))
    for s,x in zip(sums,sends): s.start(x)
    return value


def settle(sums,value):
    value,*gots=lax.optimization_barrier((value,*[s.got for s in sums]))
    for s,x in zip(sums,gots): s.finish(x)
    return value


def all_sum(x):
    for bits in (1,2):
        x=x+flip(x,bits)
    for bit in range(lax.axis_size("dp").bit_length()-1):
        x=x+dp_flip(x,bit)
    return x


def after(x,*others):
    return lax.optimization_barrier((x,)+others)[0]


def shards(tokens,grad_out,lengths,coords,w_qkv,b_qkv,w_proj,w_fc1,b_fc1,w_fc2,norm_gains,shift_biases):
    tok=tokens.shape[0]
    ranks=lax.axis_size("tensor")
    bits=lax.axis_size("dp").bit_length()-1
    me=lax.axis_index("tensor")
    rows_all=tok*ranks
    half=rows_all//2
    cols=w_qkv.shape[2]
    ends=jnp.cumsum(lengths[0])
    slots=lengths.shape[1]
    rel=jnp.arange(rows_all,dtype=jnp.int32)
    place=((rel//tok)^me)*tok+rel%tok
    seg=jnp.sum((place[:,None]>=ends[None,:]).astype(jnp.int32),axis=1)
    live=(place[:tok]<ends[-1]).astype(f32)[:,None]
    cgrp=jnp.concatenate([lax.dynamic_slice_in_dim(coords,(me^j)*tok,tok,1) for j in range(ranks)],axis=1).astype(f32)
    lane=jnp.arange(128,dtype=jnp.int32)
    pair=lane%(HDIM//2)
    freq=100.0**(-(pair//3).astype(f32)/(HDIM//2//3+1))
    angle=jnp.zeros((rows_all,128),f32)
    for a in range(3):
        angle=angle+cgrp[a][:,None]*jnp.where(pair%3==a,freq,0.0)[None,:]
    cos=jnp.cos(angle)
    sin=jnp.sin(angle)*jnp.where(lane%HDIM<HDIM//2,-1.0,1.0)[None,:]
    gains=norm_gains.astype(f32)
    shifts=shift_biases.astype(f32)
    x_rows=tokens.astype(f32)

    normed_one,norm_one_back=jax.vjp(norm_rows,x_rows,gains[0],shifts[0])
    low_one=normed_one.astype(bf16)
    far=flip(low_one,2)
    near=flip(low_one,1)
    grad_y=grad_out.astype(f32)*live
    grad_mlp=grad_y.astype(bf16)

    bq=b_qkv.astype(f32)
    qkv=qkv_rows(low_one,near,w_qkv,bq,cos,sin,0,None)
    far,*qkv=lax.optimization_barrier((far,*qkv))
    far_pair=flip(far,1)
    q,k,v=qkv_rows(far,far_pair,w_qkv,bq,cos,sin,1,qkv)
    n1=[low_one,near,far,far_pair]
    late,q,k,v=lax.optimization_barrier((grad_mlp,q,k,v))
    gm=[late,flip(late,1),flip(late,2)]
    segq=seg[None,:]; segk=seg[:,None]
    hb=half//BLK
    codes=block_codes(seg,slots,False)
    att_far,lse_far=attn_fwd(codes[hb:],q,k,v,segq,segk,hb,hb)
    att_far,g2=lax.optimization_barrier((att_far,gm[2]))
    proj=lambda a: jnp.dot(a,w_proj,preferred_element_type=f32).astype(bf16)
    across=pair_sum(proj(att_far[tok:]),proj(att_far[:tok])).astype(bf16)
    q_late,across=lax.optimization_barrier((q,across))
    gm=[gm[0],gm[1],g2,flip(g2,1)]
    across=flip(across,3)
    att_near,lse_near=attn_fwd(codes[:hb],q_late,k,v,segq,segk,0,hb)
    across,att_near=lax.optimization_barrier((across,att_near))
    mine=pair_sum(proj(att_near[:tok]),proj(att_near[tok:]))
    resid_one=x_rows+mine+across.astype(f32)+shifts[2]
    normed_two,norm_two_back=jax.vjp(norm_rows,resid_one,gains[1],shifts[1])
    low_two=normed_two.astype(bf16)
    far=flip(low_two,2)
    near=flip(low_two,1)
    b1=b_fc1.astype(f32)[None,:]
    hid,gp,gn0,gn1,db0=mlp_rows((low_two,near),(gm[0],gm[1]),w_fc1,b1,w_fc2,0,None)
    far,hid,gp=lax.optimization_barrier((far,hid,gp))
    far_pair=flip(far,1)
    hid,gp,gn2,gn3,db1=mlp_rows((far,far_pair),(gm[2],gm[3]),w_fc1,b1,w_fc2,1,(hid,gp))
    db=db0+db1
    across=pair_sum(gn3,gn2).astype(bf16)
    hid,gp,across=lax.optimization_barrier((hid,gp,across))
    across=flip(across,3)
    mine=pair_sum(gn0,gn1)
    tn=lambda a,b: lax.dot_general(a,b,(((0,),(0,)),((),())),preferred_element_type=f32)
    grad_w1=tn(jnp.concatenate([low_two,near,far,far_pair],axis=0),gp).astype(bf16)
    grad_w2=tn(hid,jnp.concatenate(gm,axis=0)).astype(bf16)
    across,grad_w1,grad_w2=lax.optimization_barrier((across,grad_w1,grad_w2))
    wsum=lax.psum_scatter(jnp.concatenate([grad_w1,grad_w2],axis=0),"dp",scatter_dimension=0,tiled=True)
    grad_resid_two,grad_gain_two,grad_shift_two=norm_two_back(mine+across.astype(f32))

    grad_resid_one=grad_y+grad_resid_two
    grad_attn=grad_resid_one.astype(bf16)
    far=flip(grad_attn,2)
    near=flip(grad_attn,1)
    ghead=lambda a: lax.dot_general(a,w_proj,NT,preferred_element_type=f32).astype(bf16)
    bcodes=block_codes(seg,slots,True)
    do_near=jnp.concatenate([ghead(grad_attn),ghead(near)],axis=0)
    gq_near,dk,dv,bs0=attn_bwd(bcodes[:hb],q,k,v,do_near,att_near,lse_near,segq,segk,cos,sin,0,None)
    early=jnp.stack([grad_gain_two,grad_shift_two,jnp.sum(grad_attn,axis=0,dtype=f32),jnp.sum(grad_mlp,axis=0,dtype=f32)])
    far,dk,dv,early=lax.optimization_barrier((far,dk,dv,early))
    early=early+flip(early,1)
    early=early+flip(early,2)
    far_pair=flip(far,1)
    do_far=jnp.concatenate([ghead(far),ghead(far_pair)],axis=0)
    alla=jnp.concatenate([grad_attn,near,far,far_pair],axis=0)
    grad_proj=tn(jnp.concatenate([att_near,att_far],axis=0),alla).astype(bf16)
    do_far,grad_proj,early=lax.optimization_barrier((do_far,grad_proj,early))
    gq_far,gk,gv,bs1=attn_bwd(bcodes[hb:],q,k,v,do_far,att_far,lse_far,segq,segk,cos,sin,1,(dk,dv))
    gk,wsum=lax.optimization_barrier((gk,wsum))
    wsum=lax.all_gather(wsum,"dp",axis=0,tiled=True)
    r2,r3=back_rows(gq_far,gk,gv,w_qkv,1)
    across=pair_sum(r3,r2).astype(bf16)
    gq_near,gk,gv,across,early=lax.optimization_barrier((gq_near,gk,gv,across,early))
    across=flip(across,3)
    g_all=jnp.concatenate([jnp.concatenate([gq_near,gq_far],axis=0),gk,gv],axis=1)
    grad_wqkv=tn(jnp.concatenate(n1,axis=0),g_all).astype(bf16)
    grad_wqkv,hid,gq_near=lax.optimization_barrier((grad_wqkv,hid,gq_near))
    d=tokens.shape[1]
    sizes=(3*cols,db.shape[1],early.size)
    pad=(-sum(sizes))%(8*cols<<bits)
    small=jnp.concatenate([(bs0+bs1)[:3].reshape(-1),db[0],early.reshape(-1),jnp.zeros((pad,),f32)]).astype(bf16).reshape(-1,cols)
    tail_a=DpSum(jnp.concatenate([grad_wqkv[:,:cols],grad_wqkv[:,cols:2*cols]],axis=0),tuple(range(bits)))
    tail_b=DpSum(jnp.concatenate([grad_wqkv[:,2*cols:],grad_proj.reshape(-1,cols),small],axis=0),(1,0)+tuple(range(2,bits)))
    tails=(tail_a,tail_b)
    for t in tails: t.start(t.operand())
    *gots,across=lax.optimization_barrier((tail_a.got,tail_b.got,across))
    for t,got in zip(tails,gots): t.finish(got)
    r0,r1=back_rows(gq_near,gk,gv,w_qkv,0)
    mine=pair_sum(r0,r1)
    grad_x_norm,grad_gain_one,grad_shift_one=norm_one_back(mine+across.astype(f32))
    one=jnp.stack([grad_gain_one,grad_shift_one])
    o=[jnp.dot(hid[j*tok:(j+1)*tok],w_fc2,preferred_element_type=f32).astype(bf16) for j in range(ranks)]
    o_across=flip(pair_sum(o[3],o[2]).astype(bf16),3)
    for t in tails: t.start(t.operand())
    one,*gots=lax.optimization_barrier((one,tail_a.got,tail_b.got))
    for t,got in zip(tails,gots): t.finish(got)
    hops=[partial(dp_flip,bit=bit) for bit in range(bits)]+[partial(flip,bits=1),partial(flip,bits=2)]
    while hops or tail_a.at<len(tail_a.stages):
        busy=[t for t in tails if t.at<len(t.stages)]
        for t in busy: t.start(t.operand())
        hop=hops.pop(0) if hops else None
        other=hop(one) if hop else one
        third=bool(busy) and busy[0].at==bits-1
        gots=[t.got for t in busy]
        if third:
            other,o_across,wsum,*gots=lax.optimization_barrier((other,o_across,wsum,*gots))
        else:
            other,*gots=lax.optimization_barrier((other,*gots))
        for t,got in zip(busy,gots): t.finish(got)
        one=one+other if hop else one
    tail_a,tail_b=tail_a.cur,tail_b.cur
    output=(resid_one+pair_sum(o[0],o[1])+o_across.astype(f32)+shifts[3]).astype(bf16)
    grad_w1,grad_w2=wsum[:d],wsum[d:]
    grad_wqkv=jnp.stack([tail_a[:d],tail_a[d:],tail_b[:d]]).astype(f32)
    grad_wproj=tail_b[d:2*d].reshape(cols,d).astype(f32)
    small=tail_b[2*d:].reshape(-1).astype(f32)
    grad_bqkv=small[:sizes[0]].reshape(3,cols)
    grad_b1=small[sizes[0]:sizes[0]+sizes[1]]
    early=small[sizes[0]+sizes[1]:sum(sizes)].reshape(4,d)
    grad_tokens=(grad_resid_one+grad_x_norm).astype(bf16)
    return (output,grad_tokens,grad_wqkv,grad_bqkv,grad_wproj,grad_w1.astype(f32),grad_b1,grad_w2.astype(f32),
            jnp.stack([one[0],early[0]]),jnp.stack([one[1],early[1],early[2],early[3]]))


def solution(mesh):
    rows=P(("dp","tensor"),None)
    return jax.shard_map(shards,mesh=mesh,
        in_specs=(rows,rows,P("dp",None),P(None,"dp"),P(None,None,"tensor"),P(None,"tensor"),P("tensor",None),
                  P(None,"tensor"),P("tensor"),P("tensor",None),P(),P()),
        out_specs=(rows,rows,P(None,None,"tensor"),P(None,"tensor"),P("tensor",None),P(None,"tensor"),P("tensor"),
                   P("tensor",None),P(),P()),
        check_vma=False)
```

```python
from functools import partial

import jax
import jax.numpy as jnp
from jax import lax
from jax.experimental import pallas as pl
from jax.experimental.pallas import tpu as pltpu
from jax.sharding import PartitionSpec as P

HDIM=64
LOG2E=1.4426950408889634
LN2=0.6931471805599453
f32=jnp.float32; bf16=jnp.bfloat16
BLK=256
VROWS=80
NT=(((1,),(1,)),((),()))

def work(flops):
    return pl.CostEstimate(flops=flops,bytes_accessed=0,transcendentals=0)

def lane_half(shape, which):
    lane=lax.broadcasted_iota(jnp.int32, shape, 1)
    return (lane//HDIM)%2==which

def attn_fwd_kernel(codes, q_ref, k_ref, v_ref, segq_ref, segk_ref, o_ref, lse_ref, vt, qm, m_sc, acc, s_sc):
    step=pl.program_id(0)
    nkb=k_ref.shape[0]//BLK
    heads=q_ref.shape[1]//HDIM
    @pl.when(step==0)
    def _():
        for blk in range(nkb):
            rows=pl.ds(blk*BLK,BLK)
            vT=v_ref[rows,:].T
            for h in range(heads):
                vt[h*VROWS:h*VROWS+HDIM, rows]=vT[h*HDIM:(h+1)*HDIM,:]
        for h in range(heads):
            vt[h*VROWS+HDIM:(h+1)*VROWS,:]=jnp.ones((VROWS-HDIM,vt.shape[1]),bf16)
    for p in range(heads//2):
        qp=q_ref[:,p*128:(p+1)*128]
        for w in range(2):
            qm[2*p+w]=jnp.where(lane_half(qp.shape,w),qp,jnp.zeros_like(qp))
    m_sc[...]=jnp.full(m_sc.shape,-1e30,f32)
    acc[...]=jnp.zeros(acc.shape,f32)
    scale=HDIM**-0.5*LOG2E

    def tile(kb,masked):
        rows=pl.ds(pl.multiple_of(kb*BLK,BLK),BLK)
        if masked:
            allowed=segk_ref[rows,:][:,0:1]==segq_ref[0:1,:]
        tops=[]
        for h in range(heads):
            p=h//2
            s=lax.dot_general(k_ref[rows,p*128:(p+1)*128],qm[h],NT,preferred_element_type=f32)*scale
            if masked: s=jnp.where(allowed,s,-1e30)
            s_sc[h]=s
            tops.append(jnp.max(s,axis=0,keepdims=True))
        m_prev=m_sc[0:heads,:]
        m_new=jnp.maximum(m_prev,jnp.concatenate(tops,axis=0))
        alpha=jnp.exp2(m_prev-m_new)
        m_sc[0:heads,:]=m_new
        for h in range(heads):
            prob=jnp.exp2(s_sc[h]-m_new[h:h+1,:]).astype(bf16)
            arows=slice(h*VROWS,(h+1)*VROWS)
            acc[arows,:]=acc[arows,:]*alpha[h:h+1,:]+jnp.dot(vt[arows,rows],prob,preferred_element_type=f32)

    def body(kb,carry):
        code=codes[step,kb]
        @pl.when(code==1)
        def _(): tile(kb,False)
        @pl.when(code==2)
        def _(): tile(kb,True)
        return carry
    lax.fori_loop(0,nkb,body,0)
    outs=[]
    for h in range(heads):
        total=acc[h*VROWS+HDIM:h*VROWS+HDIM+1,:]
        outs.append(acc[h*VROWS:h*VROWS+HDIM,:]/total)
        lse_ref[h:h+1,:]=m_sc[h:h+1,:]+jnp.log2(total)
    for h in range(heads,8):
        lse_ref[h:h+1,:]=jnp.zeros((1,BLK),f32)
    o_ref[...]=jnp.concatenate(outs,axis=0).T.astype(bf16)

def attn_fwd(codes,q,k,v,segq,segk,block0,nblocks):
    rows,cols=k.shape
    heads=cols//HDIM
    full=lambda i,c:(0,0)
    return pl.pallas_call(
        attn_fwd_kernel,
        out_shape=(jax.ShapeDtypeStruct((nblocks*BLK,cols),bf16),jax.ShapeDtypeStruct((8,nblocks*BLK),f32)),
        grid_spec=pltpu.PrefetchScalarGridSpec(num_scalar_prefetch=1,grid=(nblocks,),
            in_specs=[pl.BlockSpec((BLK,cols),lambda i,c:(i+block0,0)),
                      pl.BlockSpec((rows,cols),full),pl.BlockSpec((rows,cols),full),
                      pl.BlockSpec((1,BLK),lambda i,c:(0,i+block0)),
                      pl.BlockSpec((rows,1),full)],
            out_specs=[pl.BlockSpec((BLK,cols),lambda i,c:(i,0)),pl.BlockSpec((8,BLK),lambda i,c:(0,i))],
            scratch_shapes=[pltpu.VMEM((heads*VROWS,rows),bf16),pltpu.VMEM((heads,BLK,128),bf16),
                            pltpu.VMEM((8,BLK),f32),pltpu.VMEM((heads*VROWS,BLK),f32),pltpu.VMEM((heads,BLK,BLK),f32)]),
        compiler_params=pltpu.CompilerParams(dimension_semantics=("arbitrary",)),
        name="attn_fwd",
        cost_estimate=work(64*nblocks*BLK*rows*cols),
    )(codes,q,k,v,segq,segk)

def swap_halves(x):
    n=x.shape[1]
    lane=lax.broadcasted_iota(jnp.int32,x.shape,1)
    up=pltpu.roll(x,n-HDIM//2,1)
    down=pltpu.roll(x,HDIM//2,1)
    return jnp.where(lane%HDIM<HDIM//2,up,down)

def attn_bwd_kernel(last, codes, q_ref,k_ref,v_ref,do_ref,o_ref,lse_ref,segq_ref,segk_ref,cos_ref,sin_ref,cosk_ref,sink_ref,*rest):
    if last:
        dk0_ref,dv0_ref,gq_ref,gk_ref,gv_ref,bsum_ref,kt,qm,dom,delta,dq,dk,dv,p_sc,low_sc,ds_sc=rest
    else:
        gq_ref,gk_ref,gv_ref,bsum_ref,kt,qm,dom,delta,dq,dk,dv,p_sc,low_sc,ds_sc=rest
    step=pl.program_id(0)
    nkb=pl.num_programs(0)
    nqb=q_ref.shape[0]//BLK
    heads=q_ref.shape[1]//HDIM
    scale=HDIM**-0.5
    def unrotate(x,cos,sin):
        out=[]
        for p in range(heads//2):
            xp=x[:,p*128:(p+1)*128]
            out.append(xp*cos-swap_halves(xp)*sin)
        return jnp.concatenate(out,axis=1)
    @pl.when(step==0)
    def _():
        def prep(blk,carry):
            rows=pl.ds(pl.multiple_of(blk*BLK,BLK),BLK)
            for p in range(heads//2):
                lanes=slice(p*128,(p+1)*128)
                qp=q_ref[rows,lanes]; dp=do_ref[rows,lanes]
                for w in range(2):
                    sel=lane_half(qp.shape,w)
                    qm[2*p+w,rows,:]=jnp.where(sel,qp,jnp.zeros_like(qp))
                    dom[2*p+w,rows,:]=jnp.where(sel,dp,jnp.zeros_like(dp))
            prod=(do_ref[rows,:].astype(f32)*o_ref[rows,:].astype(f32)).T
            for h in range(heads):
                delta[h:h+1,rows]=jnp.sum(prod[h*HDIM:(h+1)*HDIM,:],axis=0,keepdims=True)
            return carry
        lax.fori_loop(0,nqb,prep,0)
        dq[...]=jnp.zeros(dq.shape,f32)
        bsum_ref[...]=jnp.zeros(bsum_ref.shape,f32)
    kt[...]=k_ref[...].T
    if last:
        dk[...]=dk0_ref[...]
        dv[...]=dv0_ref[...]
    else:
        dk[...]=jnp.zeros(dk.shape,f32)
        dv[...]=jnp.zeros(dv.shape,f32)

    def tile(qb,masked):
        rows=pl.ds(pl.multiple_of(qb*BLK,BLK),BLK)
        if masked:
            allowed=segk_ref[:,0:1]==segq_ref[0:1,rows]
        for h in range(heads):
            lanes=slice(h//2*128,(h//2+1)*128)
            s=lax.dot_general(k_ref[:,lanes],qm[h,rows,:],NT,preferred_element_type=f32)*(scale*LOG2E)
            prob=jnp.exp2(s-lse_ref[h:h+1,rows])
            if masked: prob=jnp.where(allowed,prob,0.0)
            p_sc[h]=prob
        for h in range(heads):
            lanes=slice(h//2*128,(h//2+1)*128)
            side=slice(h%2*BLK,(h%2+1)*BLK)
            dp=lax.dot_general(v_ref[:,lanes],dom[h,rows,:],NT,preferred_element_type=f32)
            prob=p_sc[h]
            low_sc[h//2,:,side]=prob.astype(bf16)
            ds_sc[h//2,:,side]=(prob*(dp-delta[h:h+1,rows])).astype(bf16)
        for p in range(heads//2):
            lanes=slice(p*128,(p+1)*128)
            pair=slice(2*p,2*p+2)
            dv[:,lanes]+=jnp.dot(low_sc[p],dom[pair,rows,:].reshape(2*BLK,128),preferred_element_type=f32)
            dk[:,lanes]+=jnp.dot(ds_sc[p],qm[pair,rows,:].reshape(2*BLK,128),preferred_element_type=f32)
        for h in range(heads):
            hr=slice(h*HDIM,(h+1)*HDIM)
            side=slice(h%2*BLK,(h%2+1)*BLK)
            dq[hr,rows]+=jnp.dot(kt[hr,:],ds_sc[h//2,:,side],preferred_element_type=f32)

    def body(qb,carry):
        code=codes[qb,step]
        @pl.when(code==1)
        def _(): tile(qb,False)
        @pl.when(code==2)
        def _(): tile(qb,True)
        return carry
    lax.fori_loop(0,nqb,body,0)

    if last:
        gk=unrotate(dk[...]*scale,cosk_ref[...],sink_ref[...]).astype(bf16)
        gv=dv[...].astype(bf16)
        gk_ref[...]=gk
        gv_ref[...]=gv
        bsum_ref[1:2,:]+=jnp.sum(gk.astype(f32),axis=0,keepdims=True)
        bsum_ref[2:3,:]+=jnp.sum(gv.astype(f32),axis=0,keepdims=True)
    else:
        gk_ref[...]=dk[...]
        gv_ref[...]=dv[...]

    @pl.when(step==nkb-1)
    def _():
        def fin(blk,carry):
            rows=pl.ds(pl.multiple_of(blk*BLK,BLK),BLK)
            gq=unrotate(dq[:,rows].T*scale,cos_ref[rows,:],sin_ref[rows,:]).astype(bf16)
            gq_ref[rows,:]=gq
            bsum_ref[0:1,:]+=jnp.sum(gq.astype(f32),axis=0,keepdims=True)
            return carry
        lax.fori_loop(0,nqb,fin,0)

def attn_bwd(codes,q,k,v,do,o,lse,segq,segk,cos,sin,part,carried):
    rows,cols=k.shape
    half=do.shape[0]
    heads=cols//HDIM
    nb=rows//BLK
    last=carried is not None
    mine=lambda n: pl.BlockSpec((half,n),lambda i,c:(part,0))
    here=lambda n: pl.BlockSpec((half,n),lambda i,c:(0,0))
    blk=lambda n: pl.BlockSpec((BLK,n),lambda i,c:(i,0))
    kdtype=bf16 if last else f32
    return pl.pallas_call(
        partial(attn_bwd_kernel,last),
        out_shape=(jax.ShapeDtypeStruct((half,cols),bf16),jax.ShapeDtypeStruct((rows,cols),kdtype),
                   jax.ShapeDtypeStruct((rows,cols),kdtype),jax.ShapeDtypeStruct((8,cols),f32)),
        grid_spec=pltpu.PrefetchScalarGridSpec(num_scalar_prefetch=1,grid=(nb,),
            in_specs=[mine(cols),blk(cols),blk(cols),here(cols),here(cols),pl.BlockSpec((8,half),lambda i,c:(0,0)),
                      pl.BlockSpec((1,half),lambda i,c:(0,part)),blk(1),mine(128),mine(128),blk(128),blk(128)]
                     +([blk(cols),blk(cols)] if last else []),
            out_specs=[here(cols),blk(cols),blk(cols),pl.BlockSpec((8,cols),lambda i,c:(0,0))],
            scratch_shapes=[pltpu.VMEM((cols,BLK),bf16),pltpu.VMEM((heads,half,128),bf16),pltpu.VMEM((heads,half,128),bf16),
                            pltpu.VMEM((8,half),f32),pltpu.VMEM((cols,half),f32),pltpu.VMEM((BLK,cols),f32),pltpu.VMEM((BLK,cols),f32),
                            pltpu.VMEM((heads,BLK,BLK),f32),pltpu.VMEM((heads//2,BLK,2*BLK),bf16),pltpu.VMEM((heads//2,BLK,2*BLK),bf16)]),
        compiler_params=pltpu.CompilerParams(dimension_semantics=("arbitrary",)),
        name="attn_bwd",
        cost_estimate=work(1),
    )(codes,q,k,v,do,o,lse,segq,segk,cos,sin,cos,sin,*(carried or ()))

def block_codes(seg,pad_seg,skip_pad):
    sb=seg.reshape(-1,BLK)
    lo=jnp.min(sb,axis=1); hi=jnp.max(sb,axis=1)
    meet=(lo[:,None]<=hi[None,:])&(lo[None,:]<=hi[:,None])
    whole=(lo==hi)
    same=whole[:,None]&whole[None,:]&(lo[:,None]==lo[None,:])
    code=jnp.where(meet,jnp.where(same,1,2),0).astype(jnp.int32)
    if skip_pad:
        alive=lo<pad_seg
        code=jnp.where(alive[:,None]&alive[None,:],code,0)
    return code


def pick(i,n,a_ref,b_ref):
    return jnp.where(i<n,a_ref[...],b_ref[...])


def qkv_kernel(n, xa_ref, xb_ref, w_ref, b_ref, cos_ref, sin_ref, *rest):
    x=pick(pl.program_id(0),n,xa_ref,xb_ref)
    cos=cos_ref[...]; sin=sin_ref[...]
    for c,o_ref in enumerate(rest[-3:]):
        y=jnp.dot(x,w_ref[c],preferred_element_type=f32)+b_ref[c:c+1,:]
        if c<2:
            parts=[]
            for p in range(y.shape[1]//128):
                yp=y[:,p*128:(p+1)*128]
                parts.append(yp*cos+swap_halves(yp)*sin)
            y=jnp.concatenate(parts,axis=1)
        o_ref[...]=y.astype(bf16)


def two(tile,n,width):
    return [pl.BlockSpec((tile,width),lambda i:(jnp.minimum(i,n-1),0)),
            pl.BlockSpec((tile,width),lambda i:(jnp.maximum(i-n,0),0))]


def qkv_rows(xa,xb,w,b,cos,sin,part,full):
    rows,d=xa.shape
    cols=w.shape[2]
    tile=min(512,rows)
    n=rows//tile
    off=part*2*n
    row=lambda m: pl.BlockSpec((tile,m),lambda i:(i+off,0))
    kept=[] if full is None else list(full)
    return pl.pallas_call(
        partial(qkv_kernel,n),
        grid=(2*n,),
        out_shape=[jax.ShapeDtypeStruct((cos.shape[0],cols),bf16)]*3,
        in_specs=two(tile,n,d)+[pl.BlockSpec(w.shape,lambda i:(0,0,0)),pl.BlockSpec(b.shape,lambda i:(0,0)),
                  row(128),row(128)]+[pl.BlockSpec(memory_space=pl.ANY)]*len(kept),
        out_specs=[row(cols)]*3,
        input_output_aliases={6+i:i for i in range(len(kept))},
        compiler_params=pltpu.CompilerParams(dimension_semantics=("arbitrary",)),
        name="qkv",
        cost_estimate=work(20*rows*d*cols*2),
    )(xa,xb,w,b,cos,sin,*kept)


def mlp_kernel(n,xa_ref,xb_ref,ga_ref,gb_ref,w1_ref,b1_ref,w2_ref,*rest):
    hid_ref,gp_ref,na_ref,nb_ref,db_ref=rest[-5:]
    i=pl.program_id(0)
    @pl.when(i==0)
    def _():
        db_ref[...]=jnp.zeros(db_ref.shape,f32)
    pre=jnp.dot(pick(i,n,xa_ref,xb_ref),w1_ref[...],preferred_element_type=f32)+b1_ref[...]
    phi=0.5+0.5*lax.erf(pre*0.7071067811865476)
    hid_ref[...]=(pre*phi).astype(bf16)
    slope=phi+pre*(0.3989422804014327*jnp.exp2(pre*pre*(-0.5*LOG2E)))
    gh=lax.dot_general(pick(i,n,ga_ref,gb_ref),w2_ref[...],NT,preferred_element_type=f32)
    gp=(gh*slope).astype(bf16)
    gp_ref[...]=gp
    db_ref[...]+=jnp.sum(gp.astype(f32),axis=0,keepdims=True)
    gn=lax.dot_general(gp,w1_ref[...],NT,preferred_element_type=f32).astype(bf16)
    @pl.when(i<n)
    def _(): na_ref[...]=gn
    @pl.when(i>=n)
    def _(): nb_ref[...]=gn


def mlp_rows(xs,gs,w1,b1,w2,part,full):
    rows,d=xs[0].shape
    units=w1.shape[1]
    tile=min(256,rows)
    n=rows//tile
    off=part*2*n
    row=lambda m: pl.BlockSpec((tile,m),lambda i:(i+off,0))
    whole=lambda a: pl.BlockSpec(a.shape,lambda i:(0,0))
    kept=[] if full is None else list(full)
    return pl.pallas_call(
        partial(mlp_kernel,n),
        grid=(2*n,),
        out_shape=[jax.ShapeDtypeStruct((rows*4,units),bf16)]*2+[jax.ShapeDtypeStruct((rows,d),bf16)]*2+
                  [jax.ShapeDtypeStruct((1,units),f32)],
        in_specs=two(tile,n,d)+two(tile,n,d)+[whole(w1),whole(b1),whole(w2)]+[pl.BlockSpec(memory_space=pl.ANY)]*len(kept),
        out_specs=[row(units),row(units)]+two(tile,n,d)+[pl.BlockSpec((1,units),lambda i:(0,0))],
        input_output_aliases={7+i:i for i in range(len(kept))},
        compiler_params=pltpu.CompilerParams(dimension_semantics=("arbitrary",)),
        name="mlp",
        cost_estimate=work(12*rows*d*units),
    )(*xs,*gs,w1,b1,w2,*kept)


def back_kernel(n,gq_ref,gk_ref,gv_ref,w_ref,oa_ref,ob_ref):
    i=pl.program_id(0)
    y=lax.dot_general(gq_ref[...],w_ref[0],NT,preferred_element_type=f32)
    y=y+lax.dot_general(gk_ref[...],w_ref[1],NT,preferred_element_type=f32)
    y=(y+lax.dot_general(gv_ref[...],w_ref[2],NT,preferred_element_type=f32)).astype(bf16)
    @pl.when(i<n)
    def _(): oa_ref[...]=y
    @pl.when(i>=n)
    def _(): ob_ref[...]=y


def back_rows(gq,gk,gv,w,part):
    half,cols=gq.shape
    rows=half//2
    d=w.shape[1]
    tile=min(512,rows)
    n=rows//tile
    off=part*2*n
    row=pl.BlockSpec((tile,cols),lambda i:(i+off,0))
    return pl.pallas_call(
        partial(back_kernel,n),
        grid=(2*n,),
        out_shape=[jax.ShapeDtypeStruct((rows,d),bf16)]*2,
        in_specs=[pl.BlockSpec((tile,cols),lambda i:(i,0)),row,row,pl.BlockSpec(w.shape,lambda i:(0,0,0))],
        out_specs=two(tile,n,d),
        compiler_params=pltpu.CompilerParams(dimension_semantics=("arbitrary",)),
        name="back",
        cost_estimate=work(1),
    )(gq,gk,gv,w)


def norm_rows(values_in, gain_row, shift_row):
    row_mean = jnp.mean(values_in, axis=-1, keepdims=True)
    centred = values_in - row_mean
    variance = jnp.mean(centred * centred, axis=-1, keepdims=True)
    return centred * lax.rsqrt(variance + 1e-06) * gain_row + shift_row


def flip(x,bits):
    n=lax.axis_size("tensor")
    return lax.ppermute(x,"tensor",[(i,i^bits) for i in range(n)])


def pair_sum(mine,other):
    return mine.astype(f32)+flip(other,1).astype(f32)


def dp_flip(x,bit):
    n=lax.axis_size("dp")
    return lax.ppermute(x,"dp",[(i,i^(1<<bit)) for i in range(n)])


class DpSum:
    def __init__(self,x,order):
        self.cur=x
        self.stages=[(bit,True) for bit in order]+[(bit,False) for bit in reversed(order)]
        self.at=0

    def operand(self):
        bit,halving=self.stages[self.at]
        if not halving: return self.cur
        up=(lax.axis_index("dp")>>bit)&1
        halves=self.cur.reshape(2,-1,self.cur.shape[1])
        self.kept=lax.dynamic_index_in_dim(halves,up,0,False)
        return lax.dynamic_index_in_dim(halves,1-up,0,False)

    def start(self,operand):
        self.sent=operand
        self.got=dp_flip(operand,self.stages[self.at][0])

    def finish(self,got):
        bit,halving=self.stages[self.at]
        self.at+=1
        if halving:
            self.cur=(self.kept.astype(f32)+got.astype(f32)).astype(bf16)
        else:
            up=((lax.axis_index("dp")>>bit)&1)==1
            self.cur=jnp.concatenate([jnp.where(up,got,self.sent),jnp.where(up,self.sent,got)],axis=0)

    def rest(self):
        while self.at<len(self.stages):
            self.start(self.operand())
            self.finish(self.got)
        return self.cur


def begin(sums,value):
    value,*sends=lax.optimization_barrier((value,*[s.operand() for s in sums]))
    for s,x in zip(sums,sends): s.start(x)
    return value


def settle(sums,value):
    value,*gots=lax.optimization_barrier((value,*[s.got for s in sums]))
    for s,x in zip(sums,gots): s.finish(x)
    return value


def all_sum(x):
    for bits in (1,2):
        x=x+flip(x,bits)
    for bit in range(lax.axis_size("dp").bit_length()-1):
        x=x+dp_flip(x,bit)
    return x


def after(x,*others):
    return lax.optimization_barrier((x,)+others)[0]


def shards(tokens,grad_out,lengths,coords,w_qkv,b_qkv,w_proj,w_fc1,b_fc1,w_fc2,norm_gains,shift_biases):
    tok=tokens.shape[0]
    ranks=lax.axis_size("tensor")
    bits=lax.axis_size("dp").bit_length()-1
    me=lax.axis_index("tensor")
    rows_all=tok*ranks
    half=rows_all//2
    cols=w_qkv.shape[2]
    ends=jnp.cumsum(lengths[0])
    slots=lengths.shape[1]
    rel=jnp.arange(rows_all,dtype=jnp.int32)
    place=((rel//tok)^me)*tok+rel%tok
    seg=jnp.sum((place[:,None]>=ends[None,:]).astype(jnp.int32),axis=1)
    live=(place[:tok]<ends[-1]).astype(f32)[:,None]
    cgrp=jnp.concatenate([lax.dynamic_slice_in_dim(coords,(me^j)*tok,tok,1) for j in range(ranks)],axis=1).astype(f32)
    lane=jnp.arange(128,dtype=jnp.int32)
    pair=lane%(HDIM//2)
    freq=100.0**(-(pair//3).astype(f32)/(HDIM//2//3+1))
    angle=jnp.zeros((rows_all,128),f32)
    for a in range(3):
        angle=angle+cgrp[a][:,None]*jnp.where(pair%3==a,freq,0.0)[None,:]
    cos=jnp.cos(angle)
    sin=jnp.sin(angle)*jnp.where(lane%HDIM<HDIM//2,-1.0,1.0)[None,:]
    gains=norm_gains.astype(f32)
    shifts=shift_biases.astype(f32)
    x_rows=tokens.astype(f32)

    normed_one,norm_one_back=jax.vjp(norm_rows,x_rows,gains[0],shifts[0])
    low_one=normed_one.astype(bf16)
    far=flip(low_one,2)
    near=flip(low_one,1)
    grad_y=grad_out.astype(f32)*live
    grad_mlp=grad_y.astype(bf16)

    bq=b_qkv.astype(f32)
    qkv=qkv_rows(low_one,near,w_qkv,bq,cos,sin,0,None)
    far,*qkv=lax.optimization_barrier((far,*qkv))
    far_pair=flip(far,1)
    q,k,v=qkv_rows(far,far_pair,w_qkv,bq,cos,sin,1,qkv)
    n1=[low_one,near,far,far_pair]
    late,q,k,v=lax.optimization_barrier((grad_mlp,q,k,v))
    gm=[late,flip(late,1),flip(late,2)]
    segq=seg[None,:]; segk=seg[:,None]
    hb=half//BLK
    codes=block_codes(seg,slots,False)
    att_far,lse_far=attn_fwd(codes[hb:],q,k,v,segq,segk,hb,hb)
    att_far,g2=lax.optimization_barrier((att_far,gm[2]))
    proj=lambda a: jnp.dot(a,w_proj,preferred_element_type=f32).astype(bf16)
    across=pair_sum(proj(att_far[tok:]),proj(att_far[:tok])).astype(bf16)
    q_late,across=lax.optimization_barrier((q,across))
    gm=[gm[0],gm[1],g2,flip(g2,1)]
    across=flip(across,3)
    att_near,lse_near=attn_fwd(codes[:hb],q_late,k,v,segq,segk,0,hb)
    across,att_near=lax.optimization_barrier((across,att_near))
    mine=pair_sum(proj(att_near[:tok]),proj(att_near[tok:]))
    resid_one=x_rows+mine+across.astype(f32)+shifts[2]
    normed_two,norm_two_back=jax.vjp(norm_rows,resid_one,gains[1],shifts[1])
    low_two=normed_two.astype(bf16)
    far=flip(low_two,2)
    near=flip(low_two,1)
    b1=b_fc1.astype(f32)[None,:]
    hid,gp,gn0,gn1,db0=mlp_rows((low_two,near),(gm[0],gm[1]),w_fc1,b1,w_fc2,0,None)
    far,hid,gp=lax.optimization_barrier((far,hid,gp))
    far_pair=flip(far,1)
    hid,gp,gn2,gn3,db1=mlp_rows((far,far_pair),(gm[2],gm[3]),w_fc1,b1,w_fc2,1,(hid,gp))
    db=db0+db1
    across=pair_sum(gn3,gn2).astype(bf16)
    hid,gp,across=lax.optimization_barrier((hid,gp,across))
    across=flip(across,3)
    mine=pair_sum(gn0,gn1)
    tn=lambda a,b: lax.dot_general(a,b,(((0,),(0,)),((),())),preferred_element_type=f32)
    grad_w1=tn(jnp.concatenate([low_two,near,far,far_pair],axis=0),gp).astype(bf16)
    grad_w2=tn(hid,jnp.concatenate(gm,axis=0)).astype(bf16)
    across,grad_w1,grad_w2=lax.optimization_barrier((across,grad_w1,grad_w2))
    wsum=lax.psum_scatter(jnp.concatenate([grad_w1,grad_w2],axis=0),"dp",scatter_dimension=0,tiled=True)
    grad_resid_two,grad_gain_two,grad_shift_two=norm_two_back(mine+across.astype(f32))

    grad_resid_one=grad_y+grad_resid_two
    grad_attn=grad_resid_one.astype(bf16)
    far=flip(grad_attn,2)
    near=flip(grad_attn,1)
    ghead=lambda a: lax.dot_general(a,w_proj,NT,preferred_element_type=f32).astype(bf16)
    bcodes=block_codes(seg,slots,True)
    do_near=jnp.concatenate([ghead(grad_attn),ghead(near)],axis=0)
    gq_near,dk,dv,bs0=attn_bwd(bcodes[:hb],q,k,v,do_near,att_near,lse_near,segq,segk,cos,sin,0,None)
    early=jnp.stack([grad_gain_two,grad_shift_two,jnp.sum(grad_attn,axis=0,dtype=f32),jnp.sum(grad_mlp,axis=0,dtype=f32)])
    far,dk,dv,early=lax.optimization_barrier((far,dk,dv,early))
    early=early+flip(early,1)
    early=early+flip(early,2)
    far_pair=flip(far,1)
    do_far=jnp.concatenate([ghead(far),ghead(far_pair)],axis=0)
    alla=jnp.concatenate([grad_attn,near,far,far_pair],axis=0)
    grad_proj=tn(jnp.concatenate([att_near,att_far],axis=0),alla).astype(bf16)
    do_far,grad_proj,early=lax.optimization_barrier((do_far,grad_proj,early))
    gq_far,gk,gv,bs1=attn_bwd(bcodes[hb:],q,k,v,do_far,att_far,lse_far,segq,segk,cos,sin,1,(dk,dv))
    gk,wsum=lax.optimization_barrier((gk,wsum))
    wsum=lax.all_gather(wsum,"dp",axis=0,tiled=True)
    r2,r3=back_rows(gq_far,gk,gv,w_qkv,1)
    across=pair_sum(r3,r2).astype(bf16)
    gq_near,gk,gv,across,early=lax.optimization_barrier((gq_near,gk,gv,across,early))
    across=flip(across,3)
    g_all=jnp.concatenate([jnp.concatenate([gq_near,gq_far],axis=0),gk,gv],axis=1)
    grad_wqkv=tn(jnp.concatenate(n1,axis=0),g_all).astype(bf16)
    grad_wqkv,hid,gq_near=lax.optimization_barrier((grad_wqkv,hid,gq_near))
    d=tokens.shape[1]
    sizes=(3*cols,db.shape[1],early.size)
    pad=(-sum(sizes))%(8*cols<<bits)
    small=jnp.concatenate([(bs0+bs1)[:3].reshape(-1),db[0],early.reshape(-1),jnp.zeros((pad,),f32)]).astype(bf16).reshape(-1,cols)
    tail_a=DpSum(jnp.concatenate([grad_wqkv[:,:cols],grad_wqkv[:,cols:2*cols]],axis=0),tuple(range(bits)))
    tail_b=DpSum(jnp.concatenate([grad_wqkv[:,2*cols:],grad_proj.reshape(-1,cols),small],axis=0),(1,0)+tuple(range(2,bits)))
    tails=(tail_a,tail_b)
    for t in tails: t.start(t.operand())
    *gots,across=lax.optimization_barrier((tail_a.got,tail_b.got,across))
    for t,got in zip(tails,gots): t.finish(got)
    r0,r1=back_rows(gq_near,gk,gv,w_qkv,0)
    mine=pair_sum(r0,r1)
    grad_x_norm,grad_gain_one,grad_shift_one=norm_one_back(mine+across.astype(f32))
    one=jnp.stack([grad_gain_one,grad_shift_one])
    o=[jnp.dot(hid[j*tok:(j+1)*tok],w_fc2,preferred_element_type=f32).astype(bf16) for j in range(ranks)]
    o_across=flip(pair_sum(o[3],o[2]).astype(bf16),3)
    for t in tails: t.start(t.operand())
    one,*gots=lax.optimization_barrier((one,tail_a.got,tail_b.got))
    for t,got in zip(tails,gots): t.finish(got)
    hops=[partial(dp_flip,bit=bit) for bit in range(bits)]+[partial(flip,bits=1),partial(flip,bits=2)]
    while hops or tail_a.at<len(tail_a.stages):
        busy=[t for t in tails if t.at<len(t.stages)]
        for t in busy: t.start(t.operand())
        hop=hops.pop(0) if hops else None
        other=hop(one) if hop else one
        third=bool(busy) and busy[0].at==bits-1
        gots=[t.got for t in busy]
        if third:
            other,o_across,wsum,*gots=lax.optimization_barrier((other,o_across,wsum,*gots))
        else:
            other,*gots=lax.optimization_barrier((other,*gots))
        for t,got in zip(busy,gots): t.finish(got)
        one=one+other if hop else one
    tail_a,tail_b=tail_a.cur,tail_b.cur
    output=(resid_one+pair_sum(o[0],o[1])+o_across.astype(f32)+shifts[3]).astype(bf16)
    grad_w1,grad_w2=wsum[:d],wsum[d:]
    grad_wqkv=jnp.stack([tail_a[:d],tail_a[d:],tail_b[:d]]).astype(f32)
    grad_wproj=tail_b[d:2*d].reshape(cols,d).astype(f32)
    small=tail_b[2*d:].reshape(-1).astype(f32)
    grad_bqkv=small[:sizes[0]].reshape(3,cols)
    grad_b1=small[sizes[0]:sizes[0]+sizes[1]]
    early=small[sizes[0]+sizes[1]:sum(sizes)].reshape(4,d)
    grad_tokens=(grad_resid_one+grad_x_norm).astype(bf16)
    return (output,grad_tokens,grad_wqkv,grad_bqkv,grad_wproj,grad_w1.astype(f32),grad_b1,grad_w2.astype(f32),
            jnp.stack([one[0],early[0]]),jnp.stack([one[1],early[1],early[2],early[3]]))


def solution(mesh):
    rows=P(("dp","tensor"),None)
    return jax.shard_map(shards,mesh=mesh,
        in_specs=(rows,rows,P("dp",None),P(None,"dp"),P(None,None,"tensor"),P(None,"tensor"),P("tensor",None),
                  P(None,"tensor"),P("tensor"),P("tensor",None),P(),P()),
        out_specs=(rows,rows,P(None,None,"tensor"),P(None,"tensor"),P("tensor",None),P(None,"tensor"),P("tensor"),
                   P("tensor",None),P(),P()),
        check_vma=False)
```

```python
from functools import partial

import jax
import jax.numpy as jnp
from jax import lax
from jax.experimental import pallas as pl
from jax.experimental.pallas import tpu as pltpu
from jax.sharding import PartitionSpec as P

HDIM=64
LOG2E=1.4426950408889634
LN2=0.6931471805599453
f32=jnp.float32; bf16=jnp.bfloat16
BLK=256
VROWS=80
NT=(((1,),(1,)),((),()))

def work(flops):
    return pl.CostEstimate(flops=flops,bytes_accessed=0,transcendentals=0)

def lane_half(shape, which):
    lane=lax.broadcasted_iota(jnp.int32, shape, 1)
    return (lane//HDIM)%2==which

def attn_fwd_kernel(codes, q_ref, k_ref, v_ref, segq_ref, segk_ref, o_ref, lse_ref, vt, qm, m_sc, acc, s_sc):
    step=pl.program_id(0)
    nkb=k_ref.shape[0]//BLK
    heads=q_ref.shape[1]//HDIM
    @pl.when(step==0)
    def _():
        for blk in range(nkb):
            rows=pl.ds(blk*BLK,BLK)
            vT=v_ref[rows,:].T
            for h in range(heads):
                vt[h*VROWS:h*VROWS+HDIM, rows]=vT[h*HDIM:(h+1)*HDIM,:]
        for h in range(heads):
            vt[h*VROWS+HDIM:(h+1)*VROWS,:]=jnp.ones((VROWS-HDIM,vt.shape[1]),bf16)
    for p in range(heads//2):
        qp=q_ref[:,p*128:(p+1)*128]
        for w in range(2):
            qm[2*p+w]=jnp.where(lane_half(qp.shape,w),qp,jnp.zeros_like(qp))
    m_sc[...]=jnp.full(m_sc.shape,-1e30,f32)
    acc[...]=jnp.zeros(acc.shape,f32)
    scale=HDIM**-0.5*LOG2E

    def tile(kb,masked):
        rows=pl.ds(pl.multiple_of(kb*BLK,BLK),BLK)
        if masked:
            allowed=segk_ref[rows,:][:,0:1]==segq_ref[0:1,:]
        tops=[]
        for h in range(heads):
            p=h//2
            s=lax.dot_general(k_ref[rows,p*128:(p+1)*128],qm[h],NT,preferred_element_type=f32)*scale
            if masked: s=jnp.where(allowed,s,-1e30)
            s_sc[h]=s
            tops.append(jnp.max(s,axis=0,keepdims=True))
        m_prev=m_sc[0:heads,:]
        m_new=jnp.maximum(m_prev,jnp.concatenate(tops,axis=0))
        alpha=jnp.exp2(m_prev-m_new)
        m_sc[0:heads,:]=m_new
        for h in range(heads):
            prob=jnp.exp2(s_sc[h]-m_new[h:h+1,:]).astype(bf16)
            arows=slice(h*VROWS,(h+1)*VROWS)
            acc[arows,:]=acc[arows,:]*alpha[h:h+1,:]+jnp.dot(vt[arows,rows],prob,preferred_element_type=f32)

    def body(kb,carry):
        code=codes[step,kb]
        @pl.when(code==1)
        def _(): tile(kb,False)
        @pl.when(code==2)
        def _(): tile(kb,True)
        return carry
    lax.fori_loop(0,nkb,body,0)
    outs=[]
    for h in range(heads):
        total=acc[h*VROWS+HDIM:h*VROWS+HDIM+1,:]
        outs.append(acc[h*VROWS:h*VROWS+HDIM,:]/total)
        lse_ref[h:h+1,:]=m_sc[h:h+1,:]+jnp.log2(total)
    for h in range(heads,8):
        lse_ref[h:h+1,:]=jnp.zeros((1,BLK),f32)
    o_ref[...]=jnp.concatenate(outs,axis=0).T.astype(bf16)

def attn_fwd(codes,q,k,v,segq,segk,block0,nblocks):
    rows,cols=k.shape
    heads=cols//HDIM
    full=lambda i,c:(0,0)
    return pl.pallas_call(
        attn_fwd_kernel,
        out_shape=(jax.ShapeDtypeStruct((nblocks*BLK,cols),bf16),jax.ShapeDtypeStruct((8,nblocks*BLK),f32)),
        grid_spec=pltpu.PrefetchScalarGridSpec(num_scalar_prefetch=1,grid=(nblocks,),
            in_specs=[pl.BlockSpec((BLK,cols),lambda i,c:(i+block0,0)),
                      pl.BlockSpec((rows,cols),full),pl.BlockSpec((rows,cols),full),
                      pl.BlockSpec((1,BLK),lambda i,c:(0,i+block0)),
                      pl.BlockSpec((rows,1),full)],
            out_specs=[pl.BlockSpec((BLK,cols),lambda i,c:(i,0)),pl.BlockSpec((8,BLK),lambda i,c:(0,i))],
            scratch_shapes=[pltpu.VMEM((heads*VROWS,rows),bf16),pltpu.VMEM((heads,BLK,128),bf16),
                            pltpu.VMEM((8,BLK),f32),pltpu.VMEM((heads*VROWS,BLK),f32),pltpu.VMEM((heads,BLK,BLK),f32)]),
        compiler_params=pltpu.CompilerParams(dimension_semantics=("arbitrary",)),
        name="attn_fwd",
        cost_estimate=work((4 if block0 else 64)*nblocks*BLK*rows*cols),
    )(codes,q,k,v,segq,segk)

def swap_halves(x):
    n=x.shape[1]
    lane=lax.broadcasted_iota(jnp.int32,x.shape,1)
    up=pltpu.roll(x,n-HDIM//2,1)
    down=pltpu.roll(x,HDIM//2,1)
    return jnp.where(lane%HDIM<HDIM//2,up,down)

def attn_bwd_kernel(last, codes, q_ref,k_ref,v_ref,do_ref,o_ref,lse_ref,segq_ref,segk_ref,cos_ref,sin_ref,cosk_ref,sink_ref,*rest):
    if last:
        dk0_ref,dv0_ref,gq_ref,gk_ref,gv_ref,bsum_ref,kt,qm,dom,delta,dq,dk,dv,p_sc,low_sc,ds_sc=rest
    else:
        gq_ref,gk_ref,gv_ref,bsum_ref,kt,qm,dom,delta,dq,dk,dv,p_sc,low_sc,ds_sc=rest
    step=pl.program_id(0)
    nkb=pl.num_programs(0)
    nqb=q_ref.shape[0]//BLK
    heads=q_ref.shape[1]//HDIM
    scale=HDIM**-0.5
    def unrotate(x,cos,sin):
        out=[]
        for p in range(heads//2):
            xp=x[:,p*128:(p+1)*128]
            out.append(xp*cos-swap_halves(xp)*sin)
        return jnp.concatenate(out,axis=1)
    @pl.when(step==0)
    def _():
        def prep(blk,carry):
            rows=pl.ds(pl.multiple_of(blk*BLK,BLK),BLK)
            for p in range(heads//2):
                lanes=slice(p*128,(p+1)*128)
                qp=q_ref[rows,lanes]; dp=do_ref[rows,lanes]
                for w in range(2):
                    sel=lane_half(qp.shape,w)
                    qm[2*p+w,rows,:]=jnp.where(sel,qp,jnp.zeros_like(qp))
                    dom[2*p+w,rows,:]=jnp.where(sel,dp,jnp.zeros_like(dp))
            prod=(do_ref[rows,:].astype(f32)*o_ref[rows,:].astype(f32)).T
            for h in range(heads):
                delta[h:h+1,rows]=jnp.sum(prod[h*HDIM:(h+1)*HDIM,:],axis=0,keepdims=True)
            return carry
        lax.fori_loop(0,nqb,prep,0)
        dq[...]=jnp.zeros(dq.shape,f32)
        bsum_ref[...]=jnp.zeros(bsum_ref.shape,f32)
    kt[...]=k_ref[...].T
    if last:
        dk[...]=dk0_ref[...]
        dv[...]=dv0_ref[...]
    else:
        dk[...]=jnp.zeros(dk.shape,f32)
        dv[...]=jnp.zeros(dv.shape,f32)

    def tile(qb,masked):
        rows=pl.ds(pl.multiple_of(qb*BLK,BLK),BLK)
        if masked:
            allowed=segk_ref[:,0:1]==segq_ref[0:1,rows]
        for h in range(heads):
            lanes=slice(h//2*128,(h//2+1)*128)
            s=lax.dot_general(k_ref[:,lanes],qm[h,rows,:],NT,preferred_element_type=f32)*(scale*LOG2E)
            prob=jnp.exp2(s-lse_ref[h:h+1,rows])
            if masked: prob=jnp.where(allowed,prob,0.0)
            p_sc[h]=prob
        for h in range(heads):
            lanes=slice(h//2*128,(h//2+1)*128)
            side=slice(h%2*BLK,(h%2+1)*BLK)
            dp=lax.dot_general(v_ref[:,lanes],dom[h,rows,:],NT,preferred_element_type=f32)
            prob=p_sc[h]
            low_sc[h//2,:,side]=prob.astype(bf16)
            ds_sc[h//2,:,side]=(prob*(dp-delta[h:h+1,rows])).astype(bf16)
        for p in range(heads//2):
            lanes=slice(p*128,(p+1)*128)
            pair=slice(2*p,2*p+2)
            dv[:,lanes]+=jnp.dot(low_sc[p],dom[pair,rows,:].reshape(2*BLK,128),preferred_element_type=f32)
            dk[:,lanes]+=jnp.dot(ds_sc[p],qm[pair,rows,:].reshape(2*BLK,128),preferred_element_type=f32)
        for h in range(heads):
            hr=slice(h*HDIM,(h+1)*HDIM)
            side=slice(h%2*BLK,(h%2+1)*BLK)
            dq[hr,rows]+=jnp.dot(kt[hr,:],ds_sc[h//2,:,side],preferred_element_type=f32)

    def body(qb,carry):
        code=codes[qb,step]
        @pl.when(code==1)
        def _(): tile(qb,False)
        @pl.when(code==2)
        def _(): tile(qb,True)
        return carry
    lax.fori_loop(0,nqb,body,0)

    if last:
        gk=unrotate(dk[...]*scale,cosk_ref[...],sink_ref[...]).astype(bf16)
        gv=dv[...].astype(bf16)
        gk_ref[...]=gk
        gv_ref[...]=gv
        bsum_ref[1:2,:]+=jnp.sum(gk.astype(f32),axis=0,keepdims=True)
        bsum_ref[2:3,:]+=jnp.sum(gv.astype(f32),axis=0,keepdims=True)
    else:
        gk_ref[...]=dk[...]
        gv_ref[...]=dv[...]

    @pl.when(step==nkb-1)
    def _():
        def fin(blk,carry):
            rows=pl.ds(pl.multiple_of(blk*BLK,BLK),BLK)
            gq=unrotate(dq[:,rows].T*scale,cos_ref[rows,:],sin_ref[rows,:]).astype(bf16)
            gq_ref[rows,:]=gq
            bsum_ref[0:1,:]+=jnp.sum(gq.astype(f32),axis=0,keepdims=True)
            return carry
        lax.fori_loop(0,nqb,fin,0)

def attn_bwd(codes,q,k,v,do,o,lse,segq,segk,cos,sin,part,carried):
    rows,cols=k.shape
    half=do.shape[0]
    heads=cols//HDIM
    nb=rows//BLK
    last=carried is not None
    mine=lambda n: pl.BlockSpec((half,n),lambda i,c:(part,0))
    here=lambda n: pl.BlockSpec((half,n),lambda i,c:(0,0))
    blk=lambda n: pl.BlockSpec((BLK,n),lambda i,c:(i,0))
    kdtype=bf16 if last else f32
    return pl.pallas_call(
        partial(attn_bwd_kernel,last),
        out_shape=(jax.ShapeDtypeStruct((half,cols),bf16),jax.ShapeDtypeStruct((rows,cols),kdtype),
                   jax.ShapeDtypeStruct((rows,cols),kdtype),jax.ShapeDtypeStruct((8,cols),f32)),
        grid_spec=pltpu.PrefetchScalarGridSpec(num_scalar_prefetch=1,grid=(nb,),
            in_specs=[mine(cols),blk(cols),blk(cols),here(cols),here(cols),pl.BlockSpec((8,half),lambda i,c:(0,0)),
                      pl.BlockSpec((1,half),lambda i,c:(0,part)),blk(1),mine(128),mine(128),blk(128),blk(128)]
                     +([blk(cols),blk(cols)] if last else []),
            out_specs=[here(cols),blk(cols),blk(cols),pl.BlockSpec((8,cols),lambda i,c:(0,0))],
            scratch_shapes=[pltpu.VMEM((cols,BLK),bf16),pltpu.VMEM((heads,half,128),bf16),pltpu.VMEM((heads,half,128),bf16),
                            pltpu.VMEM((8,half),f32),pltpu.VMEM((cols,half),f32),pltpu.VMEM((BLK,cols),f32),pltpu.VMEM((BLK,cols),f32),
                            pltpu.VMEM((heads,BLK,BLK),f32),pltpu.VMEM((heads//2,BLK,2*BLK),bf16),pltpu.VMEM((heads//2,BLK,2*BLK),bf16)]),
        compiler_params=pltpu.CompilerParams(dimension_semantics=("arbitrary",)),
        name="attn_bwd",
        cost_estimate=work(1),
    )(codes,q,k,v,do,o,lse,segq,segk,cos,sin,cos,sin,*(carried or ()))

def block_codes(seg,pad_seg,skip_pad):
    sb=seg.reshape(-1,BLK)
    lo=jnp.min(sb,axis=1); hi=jnp.max(sb,axis=1)
    meet=(lo[:,None]<=hi[None,:])&(lo[None,:]<=hi[:,None])
    whole=(lo==hi)
    same=whole[:,None]&whole[None,:]&(lo[:,None]==lo[None,:])
    code=jnp.where(meet,jnp.where(same,1,2),0).astype(jnp.int32)
    if skip_pad:
        alive=lo<pad_seg
        code=jnp.where(alive[:,None]&alive[None,:],code,0)
    return code


def pick(i,n,a_ref,b_ref):
    return jnp.where(i<n,a_ref[...],b_ref[...])


def qkv_kernel(n, xa_ref, xb_ref, w_ref, b_ref, cos_ref, sin_ref, *rest):
    x=pick(pl.program_id(0),n,xa_ref,xb_ref)
    cos=cos_ref[...]; sin=sin_ref[...]
    for c,o_ref in enumerate(rest[-3:]):
        y=jnp.dot(x,w_ref[c],preferred_element_type=f32)+b_ref[c:c+1,:]
        if c<2:
            parts=[]
            for p in range(y.shape[1]//128):
                yp=y[:,p*128:(p+1)*128]
                parts.append(yp*cos+swap_halves(yp)*sin)
            y=jnp.concatenate(parts,axis=1)
        o_ref[...]=y.astype(bf16)


def two(tile,n,width):
    return [pl.BlockSpec((tile,width),lambda i:(jnp.minimum(i,n-1),0)),
            pl.BlockSpec((tile,width),lambda i:(jnp.maximum(i-n,0),0))]


def qkv_rows(xa,xb,w,b,cos,sin,part,full):
    rows,d=xa.shape
    cols=w.shape[2]
    tile=min(512,rows)
    n=rows//tile
    off=part*2*n
    row=lambda m: pl.BlockSpec((tile,m),lambda i:(i+off,0))
    kept=[] if full is None else list(full)
    return pl.pallas_call(
        partial(qkv_kernel,n),
        grid=(2*n,),
        out_shape=[jax.ShapeDtypeStruct((cos.shape[0],cols),bf16)]*3,
        in_specs=two(tile,n,d)+[pl.BlockSpec(w.shape,lambda i:(0,0,0)),pl.BlockSpec(b.shape,lambda i:(0,0)),
                  row(128),row(128)]+[pl.BlockSpec(memory_space=pl.ANY)]*len(kept),
        out_specs=[row(cols)]*3,
        input_output_aliases={6+i:i for i in range(len(kept))},
        compiler_params=pltpu.CompilerParams(dimension_semantics=("arbitrary",)),
        name="qkv",
        cost_estimate=work(20*rows*d*cols*2),
    )(xa,xb,w,b,cos,sin,*kept)


def mlp_kernel(n,xa_ref,xb_ref,ga_ref,gb_ref,w1_ref,b1_ref,w2_ref,*rest):
    hid_ref,gp_ref,na_ref,nb_ref,db_ref=rest[-5:]
    i=pl.program_id(0)
    @pl.when(i==0)
    def _():
        db_ref[...]=jnp.zeros(db_ref.shape,f32)
    pre=jnp.dot(pick(i,n,xa_ref,xb_ref),w1_ref[...],preferred_element_type=f32)+b1_ref[...]
    phi=0.5+0.5*lax.erf(pre*0.7071067811865476)
    hid_ref[...]=(pre*phi).astype(bf16)
    slope=phi+pre*(0.3989422804014327*jnp.exp2(pre*pre*(-0.5*LOG2E)))
    gh=lax.dot_general(pick(i,n,ga_ref,gb_ref),w2_ref[...],NT,preferred_element_type=f32)
    gp=(gh*slope).astype(bf16)
    gp_ref[...]=gp
    db_ref[...]+=jnp.sum(gp.astype(f32),axis=0,keepdims=True)
    gn=lax.dot_general(gp,w1_ref[...],NT,preferred_element_type=f32).astype(bf16)
    @pl.when(i<n)
    def _(): na_ref[...]=gn
    @pl.when(i>=n)
    def _(): nb_ref[...]=gn


def mlp_rows(xs,gs,w1,b1,w2,part,full):
    rows,d=xs[0].shape
    units=w1.shape[1]
    tile=min(256,rows)
    n=rows//tile
    off=part*2*n
    row=lambda m: pl.BlockSpec((tile,m),lambda i:(i+off,0))
    whole=lambda a: pl.BlockSpec(a.shape,lambda i:(0,0))
    kept=[] if full is None else list(full)
    return pl.pallas_call(
        partial(mlp_kernel,n),
        grid=(2*n,),
        out_shape=[jax.ShapeDtypeStruct((rows*4,units),bf16)]*2+[jax.ShapeDtypeStruct((rows,d),bf16)]*2+
                  [jax.ShapeDtypeStruct((1,units),f32)],
        in_specs=two(tile,n,d)+two(tile,n,d)+[whole(w1),whole(b1),whole(w2)]+[pl.BlockSpec(memory_space=pl.ANY)]*len(kept),
        out_specs=[row(units),row(units)]+two(tile,n,d)+[pl.BlockSpec((1,units),lambda i:(0,0))],
        input_output_aliases={7+i:i for i in range(len(kept))},
        compiler_params=pltpu.CompilerParams(dimension_semantics=("arbitrary",)),
        name="mlp",
        cost_estimate=work(12*rows*d*units),
    )(*xs,*gs,w1,b1,w2,*kept)


def back_kernel(n,gq_ref,gk_ref,gv_ref,w_ref,oa_ref,ob_ref):
    i=pl.program_id(0)
    y=lax.dot_general(gq_ref[...],w_ref[0],NT,preferred_element_type=f32)
    y=y+lax.dot_general(gk_ref[...],w_ref[1],NT,preferred_element_type=f32)
    y=(y+lax.dot_general(gv_ref[...],w_ref[2],NT,preferred_element_type=f32)).astype(bf16)
    @pl.when(i<n)
    def _(): oa_ref[...]=y
    @pl.when(i>=n)
    def _(): ob_ref[...]=y


def back_rows(gq,gk,gv,w,part):
    half,cols=gq.shape
    rows=half//2
    d=w.shape[1]
    tile=min(512,rows)
    n=rows//tile
    off=part*2*n
    row=pl.BlockSpec((tile,cols),lambda i:(i+off,0))
    return pl.pallas_call(
        partial(back_kernel,n),
        grid=(2*n,),
        out_shape=[jax.ShapeDtypeStruct((rows,d),bf16)]*2,
        in_specs=[pl.BlockSpec((tile,cols),lambda i:(i,0)),row,row,pl.BlockSpec(w.shape,lambda i:(0,0,0))],
        out_specs=two(tile,n,d),
        compiler_params=pltpu.CompilerParams(dimension_semantics=("arbitrary",)),
        name="back",
        cost_estimate=work(100*part*rows*d*cols+1),
    )(gq,gk,gv,w)


def norm_rows(values_in, gain_row, shift_row):
    row_mean = jnp.mean(values_in, axis=-1, keepdims=True)
    centred = values_in - row_mean
    variance = jnp.mean(centred * centred, axis=-1, keepdims=True)
    return centred * lax.rsqrt(variance + 1e-06) * gain_row + shift_row


def flip(x,bits):
    n=lax.axis_size("tensor")
    return lax.ppermute(x,"tensor",[(i,i^bits) for i in range(n)])


def pair_sum(mine,other):
    return mine.astype(f32)+flip(other,1).astype(f32)


def dp_flip(x,bit):
    n=lax.axis_size("dp")
    return lax.ppermute(x,"dp",[(i,i^(1<<bit)) for i in range(n)])


class DpSum:
    def __init__(self,x,order):
        self.cur=x
        self.stages=[(bit,True) for bit in order]+[(bit,False) for bit in reversed(order)]
        self.at=0

    def operand(self):
        bit,halving=self.stages[self.at]
        if not halving: return self.cur
        up=(lax.axis_index("dp")>>bit)&1
        halves=self.cur.reshape(2,-1,self.cur.shape[1])
        self.kept=lax.dynamic_index_in_dim(halves,up,0,False)
        return lax.dynamic_index_in_dim(halves,1-up,0,False)

    def start(self,operand):
        self.sent=operand
        self.got=dp_flip(operand,self.stages[self.at][0])

    def finish(self,got):
        bit,halving=self.stages[self.at]
        self.at+=1
        if halving:
            self.cur=(self.kept.astype(f32)+got.astype(f32)).astype(bf16)
        else:
            up=((lax.axis_index("dp")>>bit)&1)==1
            self.cur=jnp.concatenate([jnp.where(up,got,self.sent),jnp.where(up,self.sent,got)],axis=0)

    def rest(self):
        while self.at<len(self.stages):
            self.start(self.operand())
            self.finish(self.got)
        return self.cur


def begin(sums,value):
    value,*sends=lax.optimization_barrier((value,*[s.operand() for s in sums]))
    for s,x in zip(sums,sends): s.start(x)
    return value


def settle(sums,value):
    value,*gots=lax.optimization_barrier((value,*[s.got for s in sums]))
    for s,x in zip(sums,gots): s.finish(x)
    return value


def all_sum(x):
    for bits in (1,2):
        x=x+flip(x,bits)
    for bit in range(lax.axis_size("dp").bit_length()-1):
        x=x+dp_flip(x,bit)
    return x


def after(x,*others):
    return lax.optimization_barrier((x,)+others)[0]


def shards(tokens,grad_out,lengths,coords,w_qkv,b_qkv,w_proj,w_fc1,b_fc1,w_fc2,norm_gains,shift_biases):
    tok=tokens.shape[0]
    ranks=lax.axis_size("tensor")
    bits=lax.axis_size("dp").bit_length()-1
    me=lax.axis_index("tensor")
    rows_all=tok*ranks
    half=rows_all//2
    cols=w_qkv.shape[2]
    ends=jnp.cumsum(lengths[0])
    slots=lengths.shape[1]
    rel=jnp.arange(rows_all,dtype=jnp.int32)
    place=((rel//tok)^me)*tok+rel%tok
    seg=jnp.sum((place[:,None]>=ends[None,:]).astype(jnp.int32),axis=1)
    live=(place[:tok]<ends[-1]).astype(f32)[:,None]
    cgrp=jnp.concatenate([lax.dynamic_slice_in_dim(coords,(me^j)*tok,tok,1) for j in range(ranks)],axis=1).astype(f32)
    lane=jnp.arange(128,dtype=jnp.int32)
    pair=lane%(HDIM//2)
    freq=100.0**(-(pair//3).astype(f32)/(HDIM//2//3+1))
    angle=jnp.zeros((rows_all,128),f32)
    for a in range(3):
        angle=angle+cgrp[a][:,None]*jnp.where(pair%3==a,freq,0.0)[None,:]
    cos=jnp.cos(angle)
    sin=jnp.sin(angle)*jnp.where(lane%HDIM<HDIM//2,-1.0,1.0)[None,:]
    gains=norm_gains.astype(f32)
    shifts=shift_biases.astype(f32)
    x_rows=tokens.astype(f32)

    normed_one,norm_one_back=jax.vjp(norm_rows,x_rows,gains[0],shifts[0])
    low_one=normed_one.astype(bf16)
    far=flip(low_one,2)
    near=flip(low_one,1)
    grad_y=grad_out.astype(f32)*live
    grad_mlp=grad_y.astype(bf16)

    bq=b_qkv.astype(f32)
    qkv=qkv_rows(low_one,near,w_qkv,bq,cos,sin,0,None)
    far,*qkv=lax.optimization_barrier((far,*qkv))
    far_pair=flip(far,1)
    q,k,v=qkv_rows(far,far_pair,w_qkv,bq,cos,sin,1,qkv)
    n1=[low_one,near,far,far_pair]
    late=after(grad_mlp,far)
    gm=[late,flip(late,1),flip(late,2)]
    segq=seg[None,:]; segk=seg[:,None]
    hb=half//BLK
    codes=block_codes(seg,slots,False)
    att_far,lse_far=attn_fwd(codes[hb:],q,k,v,segq,segk,hb,hb)
    att_far,g2=lax.optimization_barrier((att_far,gm[2]))
    proj=lambda a: jnp.dot(a,w_proj,preferred_element_type=f32).astype(bf16)
    across=pair_sum(proj(att_far[tok:]),proj(att_far[:tok])).astype(bf16)
    q_late,across=lax.optimization_barrier((q,across))
    gm=[gm[0],gm[1],g2,flip(g2,1)]
    across=flip(across,3)
    att_near,lse_near=attn_fwd(codes[:hb],q_late,k,v,segq,segk,0,hb)
    across,att_near=lax.optimization_barrier((across,att_near))
    mine=pair_sum(proj(att_near[:tok]),proj(att_near[tok:]))
    resid_one=x_rows+mine+across.astype(f32)+shifts[2]
    normed_two,norm_two_back=jax.vjp(norm_rows,resid_one,gains[1],shifts[1])
    low_two=normed_two.astype(bf16)
    far=flip(low_two,2)
    near=flip(low_two,1)
    b1=b_fc1.astype(f32)[None,:]
    hid,gp,gn0,gn1,db0=mlp_rows((low_two,near),(gm[0],gm[1]),w_fc1,b1,w_fc2,0,None)
    far,hid,gp=lax.optimization_barrier((far,hid,gp))
    far_pair=flip(far,1)
    hid,gp,gn2,gn3,db1=mlp_rows((far,far_pair),(gm[2],gm[3]),w_fc1,b1,w_fc2,1,(hid,gp))
    db=db0+db1
    across=pair_sum(gn3,gn2).astype(bf16)
    hid,gp,across=lax.optimization_barrier((hid,gp,across))
    across=flip(across,3)
    mine=pair_sum(gn0,gn1)
    tn=lambda a,b: lax.dot_general(a,b,(((0,),(0,)),((),())),preferred_element_type=f32)
    grad_w1=tn(jnp.concatenate([low_two,near,far,far_pair],axis=0),gp).astype(bf16)
    grad_w2=tn(hid,jnp.concatenate(gm,axis=0)).astype(bf16)
    both=jnp.concatenate([grad_w1,grad_w2],axis=0)
    across=after(across,both)
    wsum=lax.psum_scatter(both,"dp",scatter_dimension=0,tiled=True)
    grad_resid_two,grad_gain_two,grad_shift_two=norm_two_back(mine+across.astype(f32))

    grad_resid_one=grad_y+grad_resid_two
    grad_attn=grad_resid_one.astype(bf16)
    far=flip(grad_attn,2)
    near=flip(grad_attn,1)
    ghead=lambda a: lax.dot_general(a,w_proj,NT,preferred_element_type=f32).astype(bf16)
    bcodes=block_codes(seg,slots,True)
    do_near=jnp.concatenate([ghead(grad_attn),ghead(near)],axis=0)
    gq_near,dk,dv,bs0=attn_bwd(bcodes[:hb],q,k,v,do_near,att_near,lse_near,segq,segk,cos,sin,0,None)
    early=jnp.stack([grad_gain_two,grad_shift_two,jnp.sum(grad_attn,axis=0,dtype=f32),jnp.sum(grad_mlp,axis=0,dtype=f32)])
    far,dk,dv,early=lax.optimization_barrier((far,dk,dv,early))
    early_pair=flip(early,1)
    far_pair=flip(far,1)
    do_far=jnp.concatenate([ghead(far),ghead(far_pair)],axis=0)
    alla=jnp.concatenate([grad_attn,near,far,far_pair],axis=0)
    grad_proj=tn(jnp.concatenate([att_near,att_far],axis=0),alla).astype(bf16)
    do_far,grad_proj=lax.optimization_barrier((do_far,grad_proj))
    gq_far,gk,gv,bs1=attn_bwd(bcodes[hb:],q,k,v,do_far,att_far,lse_far,segq,segk,cos,sin,1,(dk,dv))
    gk,wsum,early_pair=lax.optimization_barrier((gk,wsum,early_pair))
    wsum=lax.all_gather(wsum,"dp",axis=0,tiled=True)
    early=early+early_pair
    early=early+flip(early,2)
    g_all=jnp.concatenate([jnp.concatenate([gq_near,gq_far],axis=0),gk,gv],axis=1)
    grad_wqkv=tn(jnp.concatenate(n1,axis=0),g_all).astype(bf16)
    d=tokens.shape[1]
    sizes=(3*cols,db.shape[1],early.size)
    pad=(-sum(sizes))%(8*cols<<bits)
    small=jnp.concatenate([(bs0+bs1)[:3].reshape(-1),db[0],early.reshape(-1),jnp.zeros((pad,),f32)]).astype(bf16).reshape(-1,cols)
    tail_a=DpSum(jnp.concatenate([grad_wqkv[:,:cols],grad_wqkv[:,cols:2*cols]],axis=0),tuple(range(bits)))
    tail_b=DpSum(jnp.concatenate([grad_wqkv[:,2*cols:],grad_proj.reshape(-1,cols),small],axis=0),(1,0)+tuple(range(2,bits)))
    tails=(tail_a,tail_b)
    gq_far=begin(tails,gq_far)
    r2,r3=back_rows(gq_far,gk,gv,w_qkv,1)
    across=pair_sum(r3,r2).astype(bf16)
    gq_near,across,hid=lax.optimization_barrier((gq_near,across,hid))
    across=flip(across,3)
    gq_near=settle(tails,gq_near)
    r0,r1=back_rows(gq_near,gk,gv,w_qkv,0)
    mine=pair_sum(r0,r1)
    o=[jnp.dot(hid[j*tok:(j+1)*tok],w_fc2,preferred_element_type=f32).astype(bf16) for j in range(ranks)]
    o_across=flip(pair_sum(o[3],o[2]).astype(bf16),3)
    for t in tails: t.start(t.operand())
    across=settle(tails,across)
    grad_x_norm,grad_gain_one,grad_shift_one=norm_one_back(mine+across.astype(f32))
    one=jnp.stack([grad_gain_one,grad_shift_one])
    hops=[partial(dp_flip,bit=bit) for bit in range(bits)]+[partial(flip,bits=1),partial(flip,bits=2)]
    while hops or tail_a.at<len(tail_a.stages):
        busy=[t for t in tails if t.at<len(t.stages)]
        for t in busy: t.start(t.operand())
        hop=hops.pop(0) if hops else None
        other=hop(one) if hop else one
        third=bool(busy) and busy[0].at==max(2,bits-1)
        gots=[t.got for t in busy]
        if third:
            other,o_across,wsum,*gots=lax.optimization_barrier((other,o_across,wsum,*gots))
        else:
            other,*gots=lax.optimization_barrier((other,*gots))
        for t,got in zip(busy,gots): t.finish(got)
        one=one+other if hop else one
    tail_a,tail_b=tail_a.cur,tail_b.cur
    output=(resid_one+pair_sum(o[0],o[1])+o_across.astype(f32)+shifts[3]).astype(bf16)
    grad_w1,grad_w2=wsum[:d],wsum[d:]
    grad_wqkv=jnp.stack([tail_a[:d],tail_a[d:],tail_b[:d]]).astype(f32)
    grad_wproj=tail_b[d:2*d].reshape(cols,d).astype(f32)
    small=tail_b[2*d:].reshape(-1).astype(f32)
    grad_bqkv=small[:sizes[0]].reshape(3,cols)
    grad_b1=small[sizes[0]:sizes[0]+sizes[1]]
    early=small[sizes[0]+sizes[1]:sum(sizes)].reshape(4,d)
    grad_tokens=(grad_resid_one+grad_x_norm).astype(bf16)
    return (output,grad_tokens,grad_wqkv,grad_bqkv,grad_wproj,grad_w1.astype(f32),grad_b1,grad_w2.astype(f32),
            jnp.stack([one[0],early[0]]),jnp.stack([one[1],early[1],early[2],early[3]]))


def solution(mesh):
    rows=P(("dp","tensor"),None)
    return jax.shard_map(shards,mesh=mesh,
        in_specs=(rows,rows,P("dp",None),P(None,"dp"),P(None,None,"tensor"),P(None,"tensor"),P("tensor",None),
                  P(None,"tensor"),P("tensor"),P("tensor",None),P(),P()),
        out_specs=(rows,rows,P(None,None,"tensor"),P(None,"tensor"),P("tensor",None),P(None,"tensor"),P("tensor"),
                   P("tensor",None),P(),P()),
        check_vma=False)
```

```python
from functools import partial

import jax
import jax.numpy as jnp
from jax import lax
from jax.experimental import pallas as pl
from jax.experimental.pallas import tpu as pltpu
from jax.sharding import PartitionSpec as P

HDIM=64
LOG2E=1.4426950408889634
LN2=0.6931471805599453
f32=jnp.float32; bf16=jnp.bfloat16
BLK=256
VROWS=80
NT=(((1,),(1,)),((),()))

def work(flops):
    return pl.CostEstimate(flops=flops,bytes_accessed=0,transcendentals=0)

def lane_half(shape, which):
    lane=lax.broadcasted_iota(jnp.int32, shape, 1)
    return (lane//HDIM)%2==which

def attn_fwd_kernel(codes, q_ref, k_ref, v_ref, segq_ref, segk_ref, o_ref, lse_ref, vt, qm, m_sc, acc, s_sc):
    step=pl.program_id(0)
    nkb=k_ref.shape[0]//BLK
    heads=q_ref.shape[1]//HDIM
    @pl.when(step==0)
    def _():
        for blk in range(nkb):
            rows=pl.ds(blk*BLK,BLK)
            vT=v_ref[rows,:].T
            for h in range(heads):
                vt[h*VROWS:h*VROWS+HDIM, rows]=vT[h*HDIM:(h+1)*HDIM,:]
        for h in range(heads):
            vt[h*VROWS+HDIM:(h+1)*VROWS,:]=jnp.ones((VROWS-HDIM,vt.shape[1]),bf16)
    for p in range(heads//2):
        qp=q_ref[:,p*128:(p+1)*128]
        for w in range(2):
            qm[2*p+w]=jnp.where(lane_half(qp.shape,w),qp,jnp.zeros_like(qp))
    m_sc[...]=jnp.full(m_sc.shape,-1e30,f32)
    acc[...]=jnp.zeros(acc.shape,f32)
    scale=HDIM**-0.5*LOG2E

    def tile(kb,masked):
        rows=pl.ds(pl.multiple_of(kb*BLK,BLK),BLK)
        if masked:
            allowed=segk_ref[rows,:][:,0:1]==segq_ref[0:1,:]
        tops=[]
        for h in range(heads):
            p=h//2
            s=lax.dot_general(k_ref[rows,p*128:(p+1)*128],qm[h],NT,preferred_element_type=f32)*scale
            if masked: s=jnp.where(allowed,s,-1e30)
            s_sc[h]=s
            tops.append(jnp.max(s,axis=0,keepdims=True))
        m_prev=m_sc[0:heads,:]
        m_new=jnp.maximum(m_prev,jnp.concatenate(tops,axis=0))
        alpha=jnp.exp2(m_prev-m_new)
        m_sc[0:heads,:]=m_new
        for h in range(heads):
            prob=jnp.exp2(s_sc[h]-m_new[h:h+1,:]).astype(bf16)
            arows=slice(h*VROWS,(h+1)*VROWS)
            acc[arows,:]=acc[arows,:]*alpha[h:h+1,:]+jnp.dot(vt[arows,rows],prob,preferred_element_type=f32)

    def body(kb,carry):
        code=codes[step,kb]
        @pl.when(code==1)
        def _(): tile(kb,False)
        @pl.when(code==2)
        def _(): tile(kb,True)
        return carry
    lax.fori_loop(0,nkb,body,0)
    outs=[]
    for h in range(heads):
        total=acc[h*VROWS+HDIM:h*VROWS+HDIM+1,:]
        outs.append(acc[h*VROWS:h*VROWS+HDIM,:]/total)
        lse_ref[h:h+1,:]=m_sc[h:h+1,:]+jnp.log2(total)
    for h in range(heads,8):
        lse_ref[h:h+1,:]=jnp.zeros((1,BLK),f32)
    o_ref[...]=jnp.concatenate(outs,axis=0).T.astype(bf16)

def attn_fwd(codes,q,k,v,segq,segk,block0,nblocks):
    rows,cols=k.shape
    heads=cols//HDIM
    full=lambda i,c:(0,0)
    return pl.pallas_call(
        attn_fwd_kernel,
        out_shape=(jax.ShapeDtypeStruct((nblocks*BLK,cols),bf16),jax.ShapeDtypeStruct((8,nblocks*BLK),f32)),
        grid_spec=pltpu.PrefetchScalarGridSpec(num_scalar_prefetch=1,grid=(nblocks,),
            in_specs=[pl.BlockSpec((BLK,cols),lambda i,c:(i+block0,0)),
                      pl.BlockSpec((rows,cols),full),pl.BlockSpec((rows,cols),full),
                      pl.BlockSpec((1,BLK),lambda i,c:(0,i+block0)),
                      pl.BlockSpec((rows,1),full)],
            out_specs=[pl.BlockSpec((BLK,cols),lambda i,c:(i,0)),pl.BlockSpec((8,BLK),lambda i,c:(0,i))],
            scratch_shapes=[pltpu.VMEM((heads*VROWS,rows),bf16),pltpu.VMEM((heads,BLK,128),bf16),
                            pltpu.VMEM((8,BLK),f32),pltpu.VMEM((heads*VROWS,BLK),f32),pltpu.VMEM((heads,BLK,BLK),f32)]),
        compiler_params=pltpu.CompilerParams(dimension_semantics=("arbitrary",)),
        name="attn_fwd",
        cost_estimate=work((4 if block0 else 64)*nblocks*BLK*rows*cols),
    )(codes,q,k,v,segq,segk)

def swap_halves(x):
    n=x.shape[1]
    lane=lax.broadcasted_iota(jnp.int32,x.shape,1)
    up=pltpu.roll(x,n-HDIM//2,1)
    down=pltpu.roll(x,HDIM//2,1)
    return jnp.where(lane%HDIM<HDIM//2,up,down)

def attn_bwd_kernel(carries, first_head, codes, q_ref,k_ref,v_ref,do_ref,o_ref,lse_ref,segq_ref,segk_ref,cos_ref,sin_ref,cosk_ref,sink_ref,*rest):
    last=carries>0
    dk_refs,dv_refs,rest=rest[:carries],rest[carries:2*carries],rest[2*carries:]
    gq_ref,gk_ref,gv_ref,bsum_ref,kt,qm,dom,delta,dq,dk,dv,p_sc,low_sc,ds_sc=rest
    step=pl.program_id(0)
    nkb=pl.num_programs(0)
    nqb=q_ref.shape[0]//BLK
    heads=q_ref.shape[1]//HDIM
    scale=HDIM**-0.5
    def unrotate(x,cos,sin):
        out=[]
        for p in range(heads//2):
            xp=x[:,p*128:(p+1)*128]
            out.append(xp*cos-swap_halves(xp)*sin)
        return jnp.concatenate(out,axis=1)
    @pl.when(step==0)
    def _():
        def prep(blk,carry):
            rows=pl.ds(pl.multiple_of(blk*BLK,BLK),BLK)
            for p in range(heads//2):
                lanes=slice(p*128,(p+1)*128)
                qp=q_ref[rows,lanes]; dp=do_ref[rows,lanes]
                for w in range(2):
                    sel=lane_half(qp.shape,w)
                    qm[2*p+w,rows,:]=jnp.where(sel,qp,jnp.zeros_like(qp))
                    dom[2*p+w,rows,:]=jnp.where(sel,dp,jnp.zeros_like(dp))
            prod=(do_ref[rows,:].astype(f32)*o_ref[rows,:].astype(f32)).T
            for h in range(heads):
                delta[h:h+1,rows]=jnp.sum(prod[h*HDIM:(h+1)*HDIM,:],axis=0,keepdims=True)
            return carry
        lax.fori_loop(0,nqb,prep,0)
        dq[...]=jnp.zeros(dq.shape,f32)
        bsum_ref[...]=jnp.zeros(bsum_ref.shape,f32)
    kt[...]=k_ref[...].T
    if last:
        dk[...]=jnp.concatenate([r[...] for r in dk_refs],axis=1)
        dv[...]=jnp.concatenate([r[...] for r in dv_refs],axis=1)
    else:
        dk[...]=jnp.zeros(dk.shape,f32)
        dv[...]=jnp.zeros(dv.shape,f32)

    def tile(qb,masked):
        rows=pl.ds(pl.multiple_of(qb*BLK,BLK),BLK)
        if masked:
            allowed=segk_ref[:,0:1]==segq_ref[0:1,rows]
        for h in range(heads):
            lanes=slice(h//2*128,(h//2+1)*128)
            s=lax.dot_general(k_ref[:,lanes],qm[h,rows,:],NT,preferred_element_type=f32)*(scale*LOG2E)
            prob=jnp.exp2(s-lse_ref[first_head+h:first_head+h+1,rows])
            if masked: prob=jnp.where(allowed,prob,0.0)
            p_sc[h]=prob
        for h in range(heads):
            lanes=slice(h//2*128,(h//2+1)*128)
            side=slice(h%2*BLK,(h%2+1)*BLK)
            dp=lax.dot_general(v_ref[:,lanes],dom[h,rows,:],NT,preferred_element_type=f32)
            prob=p_sc[h]
            low_sc[h//2,:,side]=prob.astype(bf16)
            ds_sc[h//2,:,side]=(prob*(dp-delta[h:h+1,rows])).astype(bf16)
        for p in range(heads//2):
            lanes=slice(p*128,(p+1)*128)
            pair=slice(2*p,2*p+2)
            dv[:,lanes]+=jnp.dot(low_sc[p],dom[pair,rows,:].reshape(2*BLK,128),preferred_element_type=f32)
            dk[:,lanes]+=jnp.dot(ds_sc[p],qm[pair,rows,:].reshape(2*BLK,128),preferred_element_type=f32)
        for h in range(heads):
            hr=slice(h*HDIM,(h+1)*HDIM)
            side=slice(h%2*BLK,(h%2+1)*BLK)
            dq[hr,rows]+=jnp.dot(kt[hr,:],ds_sc[h//2,:,side],preferred_element_type=f32)

    def body(qb,carry):
        code=codes[qb,step]
        @pl.when(code==1)
        def _(): tile(qb,False)
        @pl.when(code==2)
        def _(): tile(qb,True)
        return carry
    lax.fori_loop(0,nqb,body,0)

    if last:
        gk=unrotate(dk[...]*scale,cosk_ref[...],sink_ref[...]).astype(bf16)
        gv=dv[...].astype(bf16)
        gk_ref[...]=gk
        gv_ref[...]=gv
        bsum_ref[1:2,:]+=jnp.sum(gk.astype(f32),axis=0,keepdims=True)
        bsum_ref[2:3,:]+=jnp.sum(gv.astype(f32),axis=0,keepdims=True)
    else:
        gk_ref[...]=dk[...]
        gv_ref[...]=dv[...]

    @pl.when(step==nkb-1)
    def _():
        def fin(blk,carry):
            rows=pl.ds(pl.multiple_of(blk*BLK,BLK),BLK)
            gq=unrotate(dq[:,rows].T*scale,cos_ref[rows,:],sin_ref[rows,:]).astype(bf16)
            gq_ref[rows,:]=gq
            bsum_ref[0:1,:]+=jnp.sum(gq.astype(f32),axis=0,keepdims=True)
            return carry
        lax.fori_loop(0,nqb,fin,0)

def attn_bwd(codes,q,k,v,do,o,lse,segq,segk,cos,sin,part,pair,carried):
    rows=k.shape[0]
    cols=k.shape[1] if pair is None else 2*HDIM
    at=0 if pair is None else pair
    half=do.shape[0]
    heads=cols//HDIM
    nb=rows//BLK
    carried=carried or ([],[])
    carries=len(carried[0])
    here=lambda n,col: pl.BlockSpec((half,n),lambda i,c:(0,col))
    mine=lambda n,col: pl.BlockSpec((half,n),lambda i,c:(part,col))
    blk=lambda n,col: pl.BlockSpec((BLK,n),lambda i,c:(i,col))
    kdtype=bf16 if carries else f32
    return pl.pallas_call(
        partial(attn_bwd_kernel,carries,2*at),
        out_shape=(jax.ShapeDtypeStruct((half,cols),bf16),jax.ShapeDtypeStruct((rows,cols),kdtype),
                   jax.ShapeDtypeStruct((rows,cols),kdtype),jax.ShapeDtypeStruct((8,cols),f32)),
        grid_spec=pltpu.PrefetchScalarGridSpec(num_scalar_prefetch=1,grid=(nb,),
            in_specs=[mine(cols,at),blk(cols,at),blk(cols,at),here(cols,at),here(cols,at),pl.BlockSpec((8,half),lambda i,c:(0,0)),
                      pl.BlockSpec((1,half),lambda i,c:(0,part)),blk(1,0),mine(128,0),mine(128,0),blk(128,0),blk(128,0)]
                     +[blk(2*HDIM,0)]*(2*carries),
            out_specs=[here(cols,0),blk(cols,0),blk(cols,0),pl.BlockSpec((8,cols),lambda i,c:(0,0))],
            scratch_shapes=[pltpu.VMEM((cols,BLK),bf16),pltpu.VMEM((heads,half,128),bf16),pltpu.VMEM((heads,half,128),bf16),
                            pltpu.VMEM((8,half),f32),pltpu.VMEM((cols,half),f32),pltpu.VMEM((BLK,cols),f32),pltpu.VMEM((BLK,cols),f32),
                            pltpu.VMEM((heads,BLK,BLK),f32),pltpu.VMEM((heads//2,BLK,2*BLK),bf16),pltpu.VMEM((heads//2,BLK,2*BLK),bf16)]),
        compiler_params=pltpu.CompilerParams(dimension_semantics=("arbitrary",)),
        name="attn_bwd",
        cost_estimate=work(1 if carries else 80*half*rows*cols),
    )(codes,q,k,v,do,o,lse,segq,segk,cos,sin,cos,sin,*carried[0],*carried[1])

def block_codes(seg,pad_seg,skip_pad):
    sb=seg.reshape(-1,BLK)
    lo=jnp.min(sb,axis=1); hi=jnp.max(sb,axis=1)
    meet=(lo[:,None]<=hi[None,:])&(lo[None,:]<=hi[:,None])
    whole=(lo==hi)
    same=whole[:,None]&whole[None,:]&(lo[:,None]==lo[None,:])
    code=jnp.where(meet,jnp.where(same,1,2),0).astype(jnp.int32)
    if skip_pad:
        alive=lo<pad_seg
        code=jnp.where(alive[:,None]&alive[None,:],code,0)
    return code


def pick(i,n,a_ref,b_ref):
    return jnp.where(i<n,a_ref[...],b_ref[...])


def qkv_kernel(n, xa_ref, xb_ref, w_ref, b_ref, cos_ref, sin_ref, *rest):
    x=pick(pl.program_id(0),n,xa_ref,xb_ref)
    cos=cos_ref[...]; sin=sin_ref[...]
    for c,o_ref in enumerate(rest[-3:]):
        y=jnp.dot(x,w_ref[c],preferred_element_type=f32)+b_ref[c:c+1,:]
        if c<2:
            parts=[]
            for p in range(y.shape[1]//128):
                yp=y[:,p*128:(p+1)*128]
                parts.append(yp*cos+swap_halves(yp)*sin)
            y=jnp.concatenate(parts,axis=1)
        o_ref[...]=y.astype(bf16)


def two(tile,n,width):
    return [pl.BlockSpec((tile,width),lambda i:(jnp.minimum(i,n-1),0)),
            pl.BlockSpec((tile,width),lambda i:(jnp.maximum(i-n,0),0))]


def qkv_rows(xa,xb,w,b,cos,sin,part,full):
    rows,d=xa.shape
    cols=w.shape[2]
    tile=min(512,rows)
    n=rows//tile
    off=part*2*n
    row=lambda m: pl.BlockSpec((tile,m),lambda i:(i+off,0))
    kept=[] if full is None else list(full)
    return pl.pallas_call(
        partial(qkv_kernel,n),
        grid=(2*n,),
        out_shape=[jax.ShapeDtypeStruct((cos.shape[0],cols),bf16)]*3,
        in_specs=two(tile,n,d)+[pl.BlockSpec(w.shape,lambda i:(0,0,0)),pl.BlockSpec(b.shape,lambda i:(0,0)),
                  row(128),row(128)]+[pl.BlockSpec(memory_space=pl.ANY)]*len(kept),
        out_specs=[row(cols)]*3,
        input_output_aliases={6+i:i for i in range(len(kept))},
        compiler_params=pltpu.CompilerParams(dimension_semantics=("arbitrary",)),
        name="qkv",
        cost_estimate=work(20*rows*d*cols*2),
    )(xa,xb,w,b,cos,sin,*kept)


def mlp_kernel(n,xa_ref,xb_ref,ga_ref,gb_ref,w1_ref,b1_ref,w2_ref,*rest):
    hid_ref,gp_ref,na_ref,nb_ref,db_ref=rest[-5:]
    i=pl.program_id(0)
    @pl.when(i==0)
    def _():
        db_ref[...]=jnp.zeros(db_ref.shape,f32)
    pre=jnp.dot(pick(i,n,xa_ref,xb_ref),w1_ref[...],preferred_element_type=f32)+b1_ref[...]
    phi=0.5+0.5*lax.erf(pre*0.7071067811865476)
    hid_ref[...]=(pre*phi).astype(bf16)
    slope=phi+pre*(0.3989422804014327*jnp.exp2(pre*pre*(-0.5*LOG2E)))
    gh=lax.dot_general(pick(i,n,ga_ref,gb_ref),w2_ref[...],NT,preferred_element_type=f32)
    gp=(gh*slope).astype(bf16)
    gp_ref[...]=gp
    db_ref[...]+=jnp.sum(gp.astype(f32),axis=0,keepdims=True)
    gn=lax.dot_general(gp,w1_ref[...],NT,preferred_element_type=f32).astype(bf16)
    @pl.when(i<n)
    def _(): na_ref[...]=gn
    @pl.when(i>=n)
    def _(): nb_ref[...]=gn


def mlp_rows(xs,gs,w1,b1,w2,part,full):
    rows,d=xs[0].shape
    units=w1.shape[1]
    tile=min(256,rows)
    n=rows//tile
    off=part*2*n
    row=lambda m: pl.BlockSpec((tile,m),lambda i:(i+off,0))
    whole=lambda a: pl.BlockSpec(a.shape,lambda i:(0,0))
    kept=[] if full is None else list(full)
    return pl.pallas_call(
        partial(mlp_kernel,n),
        grid=(2*n,),
        out_shape=[jax.ShapeDtypeStruct((rows*4,units),bf16)]*2+[jax.ShapeDtypeStruct((rows,d),bf16)]*2+
                  [jax.ShapeDtypeStruct((1,units),f32)],
        in_specs=two(tile,n,d)+two(tile,n,d)+[whole(w1),whole(b1),whole(w2)]+[pl.BlockSpec(memory_space=pl.ANY)]*len(kept),
        out_specs=[row(units),row(units)]+two(tile,n,d)+[pl.BlockSpec((1,units),lambda i:(0,0))],
        input_output_aliases={7+i:i for i in range(len(kept))},
        compiler_params=pltpu.CompilerParams(dimension_semantics=("arbitrary",)),
        name="mlp",
        cost_estimate=work(12*rows*d*units),
    )(*xs,*gs,w1,b1,w2,*kept)


def back_kernel(n,gq_ref,gk_ref,gv_ref,w_ref,oa_ref,ob_ref):
    i=pl.program_id(0)
    y=lax.dot_general(gq_ref[...],w_ref[0],NT,preferred_element_type=f32)
    y=y+lax.dot_general(gk_ref[...],w_ref[1],NT,preferred_element_type=f32)
    y=(y+lax.dot_general(gv_ref[...],w_ref[2],NT,preferred_element_type=f32)).astype(bf16)
    @pl.when(i<n)
    def _(): oa_ref[...]=y
    @pl.when(i>=n)
    def _(): ob_ref[...]=y


def back_rows(gq,gk,gv,w,part):
    half,cols=gq.shape
    rows=half//2
    d=w.shape[1]
    tile=min(512,rows)
    n=rows//tile
    off=part*2*n
    row=pl.BlockSpec((tile,cols),lambda i:(i+off,0))
    return pl.pallas_call(
        partial(back_kernel,n),
        grid=(2*n,),
        out_shape=[jax.ShapeDtypeStruct((rows,d),bf16)]*2,
        in_specs=[pl.BlockSpec((tile,cols),lambda i:(i,0)),row,row,pl.BlockSpec(w.shape,lambda i:(0,0,0))],
        out_specs=two(tile,n,d),
        compiler_params=pltpu.CompilerParams(dimension_semantics=("arbitrary",)),
        name="back",
        cost_estimate=work(1),
    )(gq,gk,gv,w)


def norm_rows(values_in, gain_row, shift_row):
    row_mean = jnp.mean(values_in, axis=-1, keepdims=True)
    centred = values_in - row_mean
    variance = jnp.mean(centred * centred, axis=-1, keepdims=True)
    return centred * lax.rsqrt(variance + 1e-06) * gain_row + shift_row


def flip(x,bits):
    n=lax.axis_size("tensor")
    return lax.ppermute(x,"tensor",[(i,i^bits) for i in range(n)])


def pair_sum(mine,other):
    return mine.astype(f32)+flip(other,1).astype(f32)


def dp_flip(x,bit):
    n=lax.axis_size("dp")
    return lax.ppermute(x,"dp",[(i,i^(1<<bit)) for i in range(n)])


class DpSum:
    def __init__(self,x,order):
        self.cur=x
        self.stages=[(bit,True) for bit in order]+[(bit,False) for bit in reversed(order)]
        self.at=0

    def operand(self):
        bit,halving=self.stages[self.at]
        if not halving: return self.cur
        up=(lax.axis_index("dp")>>bit)&1
        halves=self.cur.reshape(2,-1,self.cur.shape[1])
        self.kept=lax.dynamic_index_in_dim(halves,up,0,False)
        return lax.dynamic_index_in_dim(halves,1-up,0,False)

    def start(self,operand):
        self.sent=operand
        self.got=dp_flip(operand,self.stages[self.at][0])

    def finish(self,got):
        bit,halving=self.stages[self.at]
        self.at+=1
        if halving:
            self.cur=(self.kept.astype(f32)+got.astype(f32)).astype(bf16)
        else:
            up=((lax.axis_index("dp")>>bit)&1)==1
            self.cur=jnp.concatenate([jnp.where(up,got,self.sent),jnp.where(up,self.sent,got)],axis=0)

    def rest(self):
        while self.at<len(self.stages):
            self.start(self.operand())
            self.finish(self.got)
        return self.cur


def begin(sums,value):
    value,*sends=lax.optimization_barrier((value,*[s.operand() for s in sums]))
    for s,x in zip(sums,sends): s.start(x)
    return value


def settle(sums,value):
    value,*gots=lax.optimization_barrier((value,*[s.got for s in sums]))
    for s,x in zip(sums,gots): s.finish(x)
    return value


def all_sum(x):
    for bits in (1,2):
        x=x+flip(x,bits)
    for bit in range(lax.axis_size("dp").bit_length()-1):
        x=x+dp_flip(x,bit)
    return x


def after(x,*others):
    return lax.optimization_barrier((x,)+others)[0]


def shards(tokens,grad_out,lengths,coords,w_qkv,b_qkv,w_proj,w_fc1,b_fc1,w_fc2,norm_gains,shift_biases):
    tok=tokens.shape[0]
    ranks=lax.axis_size("tensor")
    bits=lax.axis_size("dp").bit_length()-1
    me=lax.axis_index("tensor")
    rows_all=tok*ranks
    half=rows_all//2
    cols=w_qkv.shape[2]
    ends=jnp.cumsum(lengths[0])
    slots=lengths.shape[1]
    rel=jnp.arange(rows_all,dtype=jnp.int32)
    place=((rel//tok)^me)*tok+rel%tok
    seg=jnp.sum((place[:,None]>=ends[None,:]).astype(jnp.int32),axis=1)
    live=(place[:tok]<ends[-1]).astype(f32)[:,None]
    cgrp=jnp.concatenate([lax.dynamic_slice_in_dim(coords,(me^j)*tok,tok,1) for j in range(ranks)],axis=1).astype(f32)
    lane=jnp.arange(128,dtype=jnp.int32)
    pair=lane%(HDIM//2)
    freq=100.0**(-(pair//3).astype(f32)/(HDIM//2//3+1))
    angle=jnp.zeros((rows_all,128),f32)
    for a in range(3):
        angle=angle+cgrp[a][:,None]*jnp.where(pair%3==a,freq,0.0)[None,:]
    cos=jnp.cos(angle)
    sin=jnp.sin(angle)*jnp.where(lane%HDIM<HDIM//2,-1.0,1.0)[None,:]
    gains=norm_gains.astype(f32)
    shifts=shift_biases.astype(f32)
    x_rows=tokens.astype(f32)

    normed_one,norm_one_back=jax.vjp(norm_rows,x_rows,gains[0],shifts[0])
    low_one=normed_one.astype(bf16)
    far=flip(low_one,2)
    near=flip(low_one,1)
    grad_y=grad_out.astype(f32)*live
    grad_mlp=grad_y.astype(bf16)

    bq=b_qkv.astype(f32)
    qkv=qkv_rows(low_one,near,w_qkv,bq,cos,sin,0,None)
    far,*qkv=lax.optimization_barrier((far,*qkv))
    far_pair=flip(far,1)
    q,k,v=qkv_rows(far,far_pair,w_qkv,bq,cos,sin,1,qkv)
    n1=[low_one,near,far,far_pair]
    late=after(grad_mlp,far)
    gm=[late,flip(late,1),flip(late,2)]
    segq=seg[None,:]; segk=seg[:,None]
    hb=half//BLK
    codes=block_codes(seg,slots,False)
    att_far,lse_far=attn_fwd(codes[hb:],q,k,v,segq,segk,hb,hb)
    att_far,g2=lax.optimization_barrier((att_far,gm[2]))
    proj=lambda a: jnp.dot(a,w_proj,preferred_element_type=f32).astype(bf16)
    across=pair_sum(proj(att_far[tok:]),proj(att_far[:tok])).astype(bf16)
    q_late,across=lax.optimization_barrier((q,across))
    gm=[gm[0],gm[1],g2,flip(g2,1)]
    across=flip(across,3)
    att_near,lse_near=attn_fwd(codes[:hb],q_late,k,v,segq,segk,0,hb)
    across,att_near=lax.optimization_barrier((across,att_near))
    mine=pair_sum(proj(att_near[:tok]),proj(att_near[tok:]))
    resid_one=x_rows+mine+across.astype(f32)+shifts[2]
    normed_two,norm_two_back=jax.vjp(norm_rows,resid_one,gains[1],shifts[1])
    low_two=normed_two.astype(bf16)
    far=flip(low_two,2)
    near=flip(low_two,1)
    b1=b_fc1.astype(f32)[None,:]
    hid,gp,gn0,gn1,db0=mlp_rows((low_two,near),(gm[0],gm[1]),w_fc1,b1,w_fc2,0,None)
    far,hid,gp=lax.optimization_barrier((far,hid,gp))
    far_pair=flip(far,1)
    hid,gp,gn2,gn3,db1=mlp_rows((far,far_pair),(gm[2],gm[3]),w_fc1,b1,w_fc2,1,(hid,gp))
    db=db0+db1
    across=pair_sum(gn3,gn2).astype(bf16)
    hid,gp,across=lax.optimization_barrier((hid,gp,across))
    across=flip(across,3)
    mine=pair_sum(gn0,gn1)
    tn=lambda a,b: lax.dot_general(a,b,(((0,),(0,)),((),())),preferred_element_type=f32)
    grad_w1=tn(jnp.concatenate([low_two,near,far,far_pair],axis=0),gp).astype(bf16)
    grad_w2=tn(hid,jnp.concatenate(gm,axis=0)).astype(bf16)
    low_order=tuple(range(bits))
    swapped=(1,0)+tuple(range(2,bits))
    wsums=(DpSum(grad_w1,low_order),DpSum(grad_w2,swapped))
    sends=[t.operand() for t in wsums]
    across=after(across,*sends)
    for t,x in zip(wsums,sends): t.start(x)
    grad_resid_two,grad_gain_two,grad_shift_two=norm_two_back(mine+across.astype(f32))

    grad_resid_one=grad_y+grad_resid_two
    grad_attn=grad_resid_one.astype(bf16)
    grad_attn=settle(wsums,grad_attn)
    far=flip(grad_attn,2)
    near=flip(grad_attn,1)
    ghead=lambda a: lax.dot_general(a,w_proj,NT,preferred_element_type=f32).astype(bf16)
    bcodes=block_codes(seg,slots,True)
    do_near=jnp.concatenate([ghead(grad_attn),ghead(near)],axis=0)
    do_near=begin(wsums,do_near)
    bwd_near=lambda pair,do: attn_bwd(bcodes[:hb],q,k,v,do,att_near,lse_near,segq,segk,cos,sin,0,pair,None)
    gq0,dk0,dv0,bs0=bwd_near(0,do_near)
    dk0=settle(wsums,dk0)
    do_near,dk0=lax.optimization_barrier((do_near,dk0))
    do_near=begin(wsums,do_near)
    gq1,dk,dv1,bs1=bwd_near(1,do_near)
    gq_near=jnp.concatenate([gq0,gq1],axis=1)
    bs0=jnp.concatenate([bs0,bs1],axis=1)
    dk=settle(wsums,dk)
    for step in range(3,bits):
        for t in wsums: t.start(t.operand()); t.finish(t.got)
    early=jnp.stack([grad_gain_two,grad_shift_two,jnp.sum(grad_attn,axis=0,dtype=f32),jnp.sum(grad_mlp,axis=0,dtype=f32)])
    far,dk,early=lax.optimization_barrier((far,dk,early))
    early_pair=flip(early,1)
    far_pair=flip(far,1)
    do_far=jnp.concatenate([ghead(far),ghead(far_pair)],axis=0)
    alla=jnp.concatenate([grad_attn,near,far,far_pair],axis=0)
    grad_proj=tn(jnp.concatenate([att_near,att_far],axis=0),alla).astype(bf16)
    wpart=jnp.concatenate([t.cur for t in wsums],axis=0)
    do_far,grad_proj,wpart=lax.optimization_barrier((do_far,grad_proj,wpart))
    wsum=lax.all_gather(wpart,"dp",axis=0,tiled=True)
    gq_far,gk,gv,bs1=attn_bwd(bcodes[hb:],q,k,v,do_far,att_far,lse_far,segq,segk,cos,sin,1,None,([dk0,dk],[dv0,dv1]))
    gk,early_pair=lax.optimization_barrier((gk,early_pair))
    early=early+early_pair
    early=early+flip(early,2)
    r2,r3=back_rows(gq_far,gk,gv,w_qkv,1)
    across=pair_sum(r3,r2).astype(bf16)
    gq_near,gk,gv,across,early=lax.optimization_barrier((gq_near,gk,gv,across,early))
    across=flip(across,3)
    g_all=jnp.concatenate([jnp.concatenate([gq_near,gq_far],axis=0),gk,gv],axis=1)
    grad_wqkv=tn(jnp.concatenate(n1,axis=0),g_all).astype(bf16)
    grad_wqkv,hid,gq_near=lax.optimization_barrier((grad_wqkv,hid,gq_near))
    d=tokens.shape[1]
    sizes=(3*cols,db.shape[1],early.size)
    pad=(-sum(sizes))%(8*cols<<bits)
    small=jnp.concatenate([(bs0+bs1)[:3].reshape(-1),db[0],early.reshape(-1),jnp.zeros((pad,),f32)]).astype(bf16).reshape(-1,cols)
    tail_a=DpSum(jnp.concatenate([grad_wqkv[:,:cols],grad_wqkv[:,cols:2*cols]],axis=0),tuple(range(bits)))
    tail_b=DpSum(jnp.concatenate([grad_wqkv[:,2*cols:],grad_proj.reshape(-1,cols),small],axis=0),(1,0)+tuple(range(2,bits)))
    tails=(tail_a,tail_b)
    for t in tails: t.start(t.operand())
    *gots,across,wsum=lax.optimization_barrier((tail_a.got,tail_b.got,across,wsum))
    for t,got in zip(tails,gots): t.finish(got)
    r0,r1=back_rows(gq_near,gk,gv,w_qkv,0)
    mine=pair_sum(r0,r1)
    grad_x_norm,grad_gain_one,grad_shift_one=norm_one_back(mine+across.astype(f32))
    one=jnp.stack([grad_gain_one,grad_shift_one])
    o=[jnp.dot(hid[j*tok:(j+1)*tok],w_fc2,preferred_element_type=f32).astype(bf16) for j in range(ranks)]
    o_across=flip(pair_sum(o[3],o[2]).astype(bf16),3)
    for t in tails: t.start(t.operand())
    one,*gots=lax.optimization_barrier((one,tail_a.got,tail_b.got))
    for t,got in zip(tails,gots): t.finish(got)
    hops=[partial(dp_flip,bit=bit) for bit in range(bits)]+[partial(flip,bits=1),partial(flip,bits=2)]
    while hops or tail_a.at<len(tail_a.stages):
        busy=[t for t in tails if t.at<len(t.stages)]
        for t in busy: t.start(t.operand())
        hop=hops.pop(0) if hops else None
        other=hop(one) if hop else one
        gots=[t.got for t in busy]
        other,o_across,*gots=lax.optimization_barrier((other,o_across,*gots))
        for t,got in zip(busy,gots): t.finish(got)
        one=one+other if hop else one
    tail_a,tail_b=tail_a.cur,tail_b.cur
    output=(resid_one+pair_sum(o[0],o[1])+o_across.astype(f32)+shifts[3]).astype(bf16)
    def whole(which,order):
        parts=wsum.reshape((2,)*bits+(2,-1,wsum.shape[1]))[(slice(None),)*bits+(which,)]
        return parts.transpose(tuple(bits-1-bit for bit in order)+(bits,bits+1)).reshape(-1,wsum.shape[1])
    grad_w1,grad_w2=whole(0,low_order),whole(1,swapped)
    grad_wqkv=jnp.stack([tail_a[:d],tail_a[d:],tail_b[:d]]).astype(f32)
    grad_wproj=tail_b[d:2*d].reshape(cols,d).astype(f32)
    small=tail_b[2*d:].reshape(-1).astype(f32)
    grad_bqkv=small[:sizes[0]].reshape(3,cols)
    grad_b1=small[sizes[0]:sizes[0]+sizes[1]]
    early=small[sizes[0]+sizes[1]:sum(sizes)].reshape(4,d)
    grad_tokens=(grad_resid_one+grad_x_norm).astype(bf16)
    return (output,grad_tokens,grad_wqkv,grad_bqkv,grad_wproj,grad_w1.astype(f32),grad_b1,grad_w2.astype(f32),
            jnp.stack([one[0],early[0]]),jnp.stack([one[1],early[1],early[2],early[3]]))


def solution(mesh):
    rows=P(("dp","tensor"),None)
    return jax.shard_map(shards,mesh=mesh,
        in_specs=(rows,rows,P("dp",None),P(None,"dp"),P(None,None,"tensor"),P(None,"tensor"),P("tensor",None),
                  P(None,"tensor"),P("tensor"),P("tensor",None),P(),P()),
        out_specs=(rows,rows,P(None,None,"tensor"),P(None,"tensor"),P("tensor",None),P(None,"tensor"),P("tensor"),
                   P("tensor",None),P(),P()),
        check_vma=False)
```

```python
from functools import partial

import jax
import jax.numpy as jnp
from jax import lax
from jax.experimental import pallas as pl
from jax.experimental.pallas import tpu as pltpu
from jax.sharding import PartitionSpec as P

HDIM=64
LOG2E=1.4426950408889634
LN2=0.6931471805599453
f32=jnp.float32; bf16=jnp.bfloat16
BLK=256
VROWS=80
NT=(((1,),(1,)),((),()))

def work(flops):
    return pl.CostEstimate(flops=flops,bytes_accessed=0,transcendentals=0)

def lane_half(shape, which):
    lane=lax.broadcasted_iota(jnp.int32, shape, 1)
    return (lane//HDIM)%2==which

def attn_fwd_kernel(codes, q_ref, k_ref, v_ref, segq_ref, segk_ref, o_ref, lse_ref, vt, qm, m_sc, acc, s_sc):
    step=pl.program_id(0)
    nkb=k_ref.shape[0]//BLK
    heads=q_ref.shape[1]//HDIM
    @pl.when(step==0)
    def _():
        for blk in range(nkb):
            rows=pl.ds(blk*BLK,BLK)
            vT=v_ref[rows,:].T
            for h in range(heads):
                vt[h*VROWS:h*VROWS+HDIM, rows]=vT[h*HDIM:(h+1)*HDIM,:]
        for h in range(heads):
            vt[h*VROWS+HDIM:(h+1)*VROWS,:]=jnp.ones((VROWS-HDIM,vt.shape[1]),bf16)
    for p in range(heads//2):
        qp=q_ref[:,p*128:(p+1)*128]
        for w in range(2):
            qm[2*p+w]=jnp.where(lane_half(qp.shape,w),qp,jnp.zeros_like(qp))
    m_sc[...]=jnp.full(m_sc.shape,-1e30,f32)
    acc[...]=jnp.zeros(acc.shape,f32)
    scale=HDIM**-0.5*LOG2E

    def tile(kb,masked):
        rows=pl.ds(pl.multiple_of(kb*BLK,BLK),BLK)
        if masked:
            allowed=segk_ref[rows,:][:,0:1]==segq_ref[0:1,:]
        tops=[]
        for h in range(heads):
            p=h//2
            s=lax.dot_general(k_ref[rows,p*128:(p+1)*128],qm[h],NT,preferred_element_type=f32)*scale
            if masked: s=jnp.where(allowed,s,-1e30)
            s_sc[h]=s
            tops.append(jnp.max(s,axis=0,keepdims=True))
        m_prev=m_sc[0:heads,:]
        m_new=jnp.maximum(m_prev,jnp.concatenate(tops,axis=0))
        alpha=jnp.exp2(m_prev-m_new)
        m_sc[0:heads,:]=m_new
        for h in range(heads):
            prob=jnp.exp2(s_sc[h]-m_new[h:h+1,:]).astype(bf16)
            arows=slice(h*VROWS,(h+1)*VROWS)
            acc[arows,:]=acc[arows,:]*alpha[h:h+1,:]+jnp.dot(vt[arows,rows],prob,preferred_element_type=f32)

    def body(kb,carry):
        code=codes[step,kb]
        @pl.when(code==1)
        def _(): tile(kb,False)
        @pl.when(code==2)
        def _(): tile(kb,True)
        return carry
    lax.fori_loop(0,nkb,body,0)
    outs=[]
    for h in range(heads):
        total=acc[h*VROWS+HDIM:h*VROWS+HDIM+1,:]
        outs.append(acc[h*VROWS:h*VROWS+HDIM,:]/total)
        lse_ref[h:h+1,:]=m_sc[h:h+1,:]+jnp.log2(total)
    for h in range(heads,8):
        lse_ref[h:h+1,:]=jnp.zeros((1,BLK),f32)
    o_ref[...]=jnp.concatenate(outs,axis=0).T.astype(bf16)

def attn_fwd(codes,q,k,v,segq,segk,block0,nblocks):
    rows,cols=k.shape
    heads=cols//HDIM
    full=lambda i,c:(0,0)
    return pl.pallas_call(
        attn_fwd_kernel,
        out_shape=(jax.ShapeDtypeStruct((nblocks*BLK,cols),bf16),jax.ShapeDtypeStruct((8,nblocks*BLK),f32)),
        grid_spec=pltpu.PrefetchScalarGridSpec(num_scalar_prefetch=1,grid=(nblocks,),
            in_specs=[pl.BlockSpec((BLK,cols),lambda i,c:(i+block0,0)),
                      pl.BlockSpec((rows,cols),full),pl.BlockSpec((rows,cols),full),
                      pl.BlockSpec((1,BLK),lambda i,c:(0,i+block0)),
                      pl.BlockSpec((rows,1),full)],
            out_specs=[pl.BlockSpec((BLK,cols),lambda i,c:(i,0)),pl.BlockSpec((8,BLK),lambda i,c:(0,i))],
            scratch_shapes=[pltpu.VMEM((heads*VROWS,rows),bf16),pltpu.VMEM((heads,BLK,128),bf16),
                            pltpu.VMEM((8,BLK),f32),pltpu.VMEM((heads*VROWS,BLK),f32),pltpu.VMEM((heads,BLK,BLK),f32)]),
        compiler_params=pltpu.CompilerParams(dimension_semantics=("arbitrary",)),
        name="attn_fwd",
        cost_estimate=work((4 if block0 else 64)*nblocks*BLK*rows*cols),
    )(codes,q,k,v,segq,segk)

def swap_halves(x):
    n=x.shape[1]
    lane=lax.broadcasted_iota(jnp.int32,x.shape,1)
    up=pltpu.roll(x,n-HDIM//2,1)
    down=pltpu.roll(x,HDIM//2,1)
    return jnp.where(lane%HDIM<HDIM//2,up,down)

def attn_bwd_kernel(carries, first_head, codes, q_ref,k_ref,v_ref,do_ref,o_ref,lse_ref,segq_ref,segk_ref,cos_ref,sin_ref,cosk_ref,sink_ref,*rest):
    last=carries>0
    dk_refs,dv_refs,rest=rest[:carries],rest[carries:2*carries],rest[2*carries:]
    gq_ref,gk_ref,gv_ref,bsum_ref,kt,qm,dom,delta,dq,dk,dv,p_sc,low_sc,ds_sc=rest
    step=pl.program_id(0)
    nkb=pl.num_programs(0)
    nqb=q_ref.shape[0]//BLK
    heads=q_ref.shape[1]//HDIM
    scale=HDIM**-0.5
    def unrotate(x,cos,sin):
        out=[]
        for p in range(heads//2):
            xp=x[:,p*128:(p+1)*128]
            out.append(xp*cos-swap_halves(xp)*sin)
        return jnp.concatenate(out,axis=1)
    @pl.when(step==0)
    def _():
        def prep(blk,carry):
            rows=pl.ds(pl.multiple_of(blk*BLK,BLK),BLK)
            for p in range(heads//2):
                lanes=slice(p*128,(p+1)*128)
                qp=q_ref[rows,lanes]; dp=do_ref[rows,lanes]
                for w in range(2):
                    sel=lane_half(qp.shape,w)
                    qm[2*p+w,rows,:]=jnp.where(sel,qp,jnp.zeros_like(qp))
                    dom[2*p+w,rows,:]=jnp.where(sel,dp,jnp.zeros_like(dp))
            prod=(do_ref[rows,:].astype(f32)*o_ref[rows,:].astype(f32)).T
            for h in range(heads):
                delta[h:h+1,rows]=jnp.sum(prod[h*HDIM:(h+1)*HDIM,:],axis=0,keepdims=True)
            return carry
        lax.fori_loop(0,nqb,prep,0)
        dq[...]=jnp.zeros(dq.shape,f32)
        bsum_ref[...]=jnp.zeros(bsum_ref.shape,f32)
    kt[...]=k_ref[...].T
    if last:
        dk[...]=jnp.concatenate([r[...] for r in dk_refs],axis=1)
        dv[...]=jnp.concatenate([r[...] for r in dv_refs],axis=1)
    else:
        dk[...]=jnp.zeros(dk.shape,f32)
        dv[...]=jnp.zeros(dv.shape,f32)

    def tile(qb,masked):
        rows=pl.ds(pl.multiple_of(qb*BLK,BLK),BLK)
        if masked:
            allowed=segk_ref[:,0:1]==segq_ref[0:1,rows]
        for h in range(heads):
            lanes=slice(h//2*128,(h//2+1)*128)
            s=lax.dot_general(k_ref[:,lanes],qm[h,rows,:],NT,preferred_element_type=f32)*(scale*LOG2E)
            prob=jnp.exp2(s-lse_ref[first_head+h:first_head+h+1,rows])
            if masked: prob=jnp.where(allowed,prob,0.0)
            p_sc[h]=prob
        for h in range(heads):
            lanes=slice(h//2*128,(h//2+1)*128)
            side=slice(h%2*BLK,(h%2+1)*BLK)
            dp=lax.dot_general(v_ref[:,lanes],dom[h,rows,:],NT,preferred_element_type=f32)
            prob=p_sc[h]
            low_sc[h//2,:,side]=prob.astype(bf16)
            ds_sc[h//2,:,side]=(prob*(dp-delta[h:h+1,rows])).astype(bf16)
        for p in range(heads//2):
            lanes=slice(p*128,(p+1)*128)
            pair=slice(2*p,2*p+2)
            dv[:,lanes]+=jnp.dot(low_sc[p],dom[pair,rows,:].reshape(2*BLK,128),preferred_element_type=f32)
            dk[:,lanes]+=jnp.dot(ds_sc[p],qm[pair,rows,:].reshape(2*BLK,128),preferred_element_type=f32)
        for h in range(heads):
            hr=slice(h*HDIM,(h+1)*HDIM)
            side=slice(h%2*BLK,(h%2+1)*BLK)
            dq[hr,rows]+=jnp.dot(kt[hr,:],ds_sc[h//2,:,side],preferred_element_type=f32)

    def body(qb,carry):
        code=codes[qb,step]
        @pl.when(code==1)
        def _(): tile(qb,False)
        @pl.when(code==2)
        def _(): tile(qb,True)
        return carry
    lax.fori_loop(0,nqb,body,0)

    if last:
        gk=unrotate(dk[...]*scale,cosk_ref[...],sink_ref[...]).astype(bf16)
        gv=dv[...].astype(bf16)
        gk_ref[...]=gk
        gv_ref[...]=gv
        bsum_ref[1:2,:]+=jnp.sum(gk.astype(f32),axis=0,keepdims=True)
        bsum_ref[2:3,:]+=jnp.sum(gv.astype(f32),axis=0,keepdims=True)
    else:
        gk_ref[...]=dk[...]
        gv_ref[...]=dv[...]

    @pl.when(step==nkb-1)
    def _():
        def fin(blk,carry):
            rows=pl.ds(pl.multiple_of(blk*BLK,BLK),BLK)
            gq=unrotate(dq[:,rows].T*scale,cos_ref[rows,:],sin_ref[rows,:]).astype(bf16)
            gq_ref[rows,:]=gq
            bsum_ref[0:1,:]+=jnp.sum(gq.astype(f32),axis=0,keepdims=True)
            return carry
        lax.fori_loop(0,nqb,fin,0)

def attn_bwd(codes,q,k,v,do,o,lse,segq,segk,cos,sin,part,pair,carried):
    rows=k.shape[0]
    cols=k.shape[1] if pair is None else 2*HDIM
    at=0 if pair is None else pair
    half=do.shape[0]
    heads=cols//HDIM
    nb=rows//BLK
    carried=carried or ([],[])
    carries=len(carried[0])
    here=lambda n,col: pl.BlockSpec((half,n),lambda i,c:(0,col))
    mine=lambda n,col: pl.BlockSpec((half,n),lambda i,c:(part,col))
    blk=lambda n,col: pl.BlockSpec((BLK,n),lambda i,c:(i,col))
    kdtype=bf16 if carries else f32
    return pl.pallas_call(
        partial(attn_bwd_kernel,carries,2*at),
        out_shape=(jax.ShapeDtypeStruct((half,cols),bf16),jax.ShapeDtypeStruct((rows,cols),kdtype),
                   jax.ShapeDtypeStruct((rows,cols),kdtype),jax.ShapeDtypeStruct((8,cols),f32)),
        grid_spec=pltpu.PrefetchScalarGridSpec(num_scalar_prefetch=1,grid=(nb,),
            in_specs=[mine(cols,at),blk(cols,at),blk(cols,at),here(cols,at),here(cols,at),pl.BlockSpec((8,half),lambda i,c:(0,0)),
                      pl.BlockSpec((1,half),lambda i,c:(0,part)),blk(1,0),mine(128,0),mine(128,0),blk(128,0),blk(128,0)]
                     +[blk(2*HDIM,0)]*(2*carries),
            out_specs=[here(cols,0),blk(cols,0),blk(cols,0),pl.BlockSpec((8,cols),lambda i,c:(0,0))],
            scratch_shapes=[pltpu.VMEM((cols,BLK),bf16),pltpu.VMEM((heads,half,128),bf16),pltpu.VMEM((heads,half,128),bf16),
                            pltpu.VMEM((8,half),f32),pltpu.VMEM((cols,half),f32),pltpu.VMEM((BLK,cols),f32),pltpu.VMEM((BLK,cols),f32),
                            pltpu.VMEM((heads,BLK,BLK),f32),pltpu.VMEM((heads//2,BLK,2*BLK),bf16),pltpu.VMEM((heads//2,BLK,2*BLK),bf16)]),
        compiler_params=pltpu.CompilerParams(dimension_semantics=("arbitrary",)),
        name="attn_bwd",
        cost_estimate=work(1 if carries else 80*half*rows*cols),
    )(codes,q,k,v,do,o,lse,segq,segk,cos,sin,cos,sin,*carried[0],*carried[1])

def block_codes(seg,pad_seg,skip_pad):
    sb=seg.reshape(-1,BLK)
    lo=jnp.min(sb,axis=1); hi=jnp.max(sb,axis=1)
    meet=(lo[:,None]<=hi[None,:])&(lo[None,:]<=hi[:,None])
    whole=(lo==hi)
    same=whole[:,None]&whole[None,:]&(lo[:,None]==lo[None,:])
    code=jnp.where(meet,jnp.where(same,1,2),0).astype(jnp.int32)
    if skip_pad:
        alive=lo<pad_seg
        code=jnp.where(alive[:,None]&alive[None,:],code,0)
    return code


def pick(i,n,a_ref,b_ref):
    return jnp.where(i<n,a_ref[...],b_ref[...])


def qkv_kernel(n, xa_ref, xb_ref, w_ref, b_ref, cos_ref, sin_ref, *rest):
    x=pick(pl.program_id(0),n,xa_ref,xb_ref)
    cos=cos_ref[...]; sin=sin_ref[...]
    for c,o_ref in enumerate(rest[-3:]):
        y=jnp.dot(x,w_ref[c],preferred_element_type=f32)+b_ref[c:c+1,:]
        if c<2:
            parts=[]
            for p in range(y.shape[1]//128):
                yp=y[:,p*128:(p+1)*128]
                parts.append(yp*cos+swap_halves(yp)*sin)
            y=jnp.concatenate(parts,axis=1)
        o_ref[...]=y.astype(bf16)


def two(tile,n,width):
    return [pl.BlockSpec((tile,width),lambda i:(jnp.minimum(i,n-1),0)),
            pl.BlockSpec((tile,width),lambda i:(jnp.maximum(i-n,0),0))]


def qkv_rows(xa,xb,w,b,cos,sin,part,full):
    rows,d=xa.shape
    cols=w.shape[2]
    tile=min(512,rows)
    n=rows//tile
    off=part*2*n
    row=lambda m: pl.BlockSpec((tile,m),lambda i:(i+off,0))
    kept=[] if full is None else list(full)
    return pl.pallas_call(
        partial(qkv_kernel,n),
        grid=(2*n,),
        out_shape=[jax.ShapeDtypeStruct((cos.shape[0],cols),bf16)]*3,
        in_specs=two(tile,n,d)+[pl.BlockSpec(w.shape,lambda i:(0,0,0)),pl.BlockSpec(b.shape,lambda i:(0,0)),
                  row(128),row(128)]+[pl.BlockSpec(memory_space=pl.ANY)]*len(kept),
        out_specs=[row(cols)]*3,
        input_output_aliases={6+i:i for i in range(len(kept))},
        compiler_params=pltpu.CompilerParams(dimension_semantics=("arbitrary",)),
        name="qkv",
        cost_estimate=work(20*rows*d*cols*2),
    )(xa,xb,w,b,cos,sin,*kept)


def mlp_kernel(n,xa_ref,xb_ref,ga_ref,gb_ref,w1_ref,b1_ref,w2_ref,*rest):
    hid_ref,gp_ref,na_ref,nb_ref,db_ref=rest[-5:]
    i=pl.program_id(0)
    @pl.when(i==0)
    def _():
        db_ref[...]=jnp.zeros(db_ref.shape,f32)
    pre=jnp.dot(pick(i,n,xa_ref,xb_ref),w1_ref[...],preferred_element_type=f32)+b1_ref[...]
    phi=0.5+0.5*lax.erf(pre*0.7071067811865476)
    hid_ref[...]=(pre*phi).astype(bf16)
    slope=phi+pre*(0.3989422804014327*jnp.exp2(pre*pre*(-0.5*LOG2E)))
    gh=lax.dot_general(pick(i,n,ga_ref,gb_ref),w2_ref[...],NT,preferred_element_type=f32)
    gp=(gh*slope).astype(bf16)
    gp_ref[...]=gp
    db_ref[...]+=jnp.sum(gp.astype(f32),axis=0,keepdims=True)
    gn=lax.dot_general(gp,w1_ref[...],NT,preferred_element_type=f32).astype(bf16)
    @pl.when(i<n)
    def _(): na_ref[...]=gn
    @pl.when(i>=n)
    def _(): nb_ref[...]=gn


def mlp_rows(xs,gs,w1,b1,w2,part,full):
    rows,d=xs[0].shape
    units=w1.shape[1]
    tile=min(256,rows)
    n=rows//tile
    off=part*2*n
    row=lambda m: pl.BlockSpec((tile,m),lambda i:(i+off,0))
    whole=lambda a: pl.BlockSpec(a.shape,lambda i:(0,0))
    kept=[] if full is None else list(full)
    return pl.pallas_call(
        partial(mlp_kernel,n),
        grid=(2*n,),
        out_shape=[jax.ShapeDtypeStruct((rows*4,units),bf16)]*2+[jax.ShapeDtypeStruct((rows,d),bf16)]*2+
                  [jax.ShapeDtypeStruct((1,units),f32)],
        in_specs=two(tile,n,d)+two(tile,n,d)+[whole(w1),whole(b1),whole(w2)]+[pl.BlockSpec(memory_space=pl.ANY)]*len(kept),
        out_specs=[row(units),row(units)]+two(tile,n,d)+[pl.BlockSpec((1,units),lambda i:(0,0))],
        input_output_aliases={7+i:i for i in range(len(kept))},
        compiler_params=pltpu.CompilerParams(dimension_semantics=("arbitrary",)),
        name="mlp",
        cost_estimate=work(12*rows*d*units),
    )(*xs,*gs,w1,b1,w2,*kept)


def back_kernel(n,gq_ref,gk_ref,gv_ref,w_ref,oa_ref,ob_ref):
    i=pl.program_id(0)
    y=lax.dot_general(gq_ref[...],w_ref[0],NT,preferred_element_type=f32)
    y=y+lax.dot_general(gk_ref[...],w_ref[1],NT,preferred_element_type=f32)
    y=(y+lax.dot_general(gv_ref[...],w_ref[2],NT,preferred_element_type=f32)).astype(bf16)
    @pl.when(i<n)
    def _(): oa_ref[...]=y
    @pl.when(i>=n)
    def _(): ob_ref[...]=y


def back_rows(gq,gk,gv,w,part):
    half,cols=gq.shape
    rows=half//2
    d=w.shape[1]
    tile=min(512,rows)
    n=rows//tile
    off=part*2*n
    row=pl.BlockSpec((tile,cols),lambda i:(i+off,0))
    return pl.pallas_call(
        partial(back_kernel,n),
        grid=(2*n,),
        out_shape=[jax.ShapeDtypeStruct((rows,d),bf16)]*2,
        in_specs=[pl.BlockSpec((tile,cols),lambda i:(i,0)),row,row,pl.BlockSpec(w.shape,lambda i:(0,0,0))],
        out_specs=two(tile,n,d),
        compiler_params=pltpu.CompilerParams(dimension_semantics=("arbitrary",)),
        name="back",
        cost_estimate=work(1),
    )(gq,gk,gv,w)


def norm_rows(values_in, gain_row, shift_row):
    row_mean = jnp.mean(values_in, axis=-1, keepdims=True)
    centred = values_in - row_mean
    variance = jnp.mean(centred * centred, axis=-1, keepdims=True)
    return centred * lax.rsqrt(variance + 1e-06) * gain_row + shift_row


def flip(x,bits):
    n=lax.axis_size("tensor")
    return lax.ppermute(x,"tensor",[(i,i^bits) for i in range(n)])


def pair_sum(mine,other):
    return mine.astype(f32)+flip(other,1).astype(f32)


def dp_flip(x,bit):
    n=lax.axis_size("dp")
    return lax.ppermute(x,"dp",[(i,i^(1<<bit)) for i in range(n)])


class DpSum:
    def __init__(self,x,order):
        self.cur=x
        self.stages=[(bit,True) for bit in order]+[(bit,False) for bit in reversed(order)]
        self.at=0

    def operand(self):
        bit,halving=self.stages[self.at]
        if not halving: return self.cur
        up=(lax.axis_index("dp")>>bit)&1
        halves=self.cur.reshape(2,-1,self.cur.shape[1])
        self.kept=lax.dynamic_index_in_dim(halves,up,0,False)
        return lax.dynamic_index_in_dim(halves,1-up,0,False)

    def start(self,operand):
        self.sent=operand
        self.got=dp_flip(operand,self.stages[self.at][0])

    def finish(self,got):
        bit,halving=self.stages[self.at]
        self.at+=1
        if halving:
            self.cur=(self.kept.astype(f32)+got.astype(f32)).astype(bf16)
        else:
            up=((lax.axis_index("dp")>>bit)&1)==1
            self.cur=jnp.concatenate([jnp.where(up,got,self.sent),jnp.where(up,self.sent,got)],axis=0)

    def rest(self):
        while self.at<len(self.stages):
            self.start(self.operand())
            self.finish(self.got)
        return self.cur


def begin(sums,value):
    value,*sends=lax.optimization_barrier((value,*[s.operand() for s in sums]))
    for s,x in zip(sums,sends): s.start(x)
    return value


def settle(sums,value):
    value,*gots=lax.optimization_barrier((value,*[s.got for s in sums]))
    for s,x in zip(sums,gots): s.finish(x)
    return value


def all_sum(x):
    for bits in (1,2):
        x=x+flip(x,bits)
    for bit in range(lax.axis_size("dp").bit_length()-1):
        x=x+dp_flip(x,bit)
    return x


def after(x,*others):
    return lax.optimization_barrier((x,)+others)[0]


def shards(tokens,grad_out,lengths,coords,w_qkv,b_qkv,w_proj,w_fc1,b_fc1,w_fc2,norm_gains,shift_biases):
    tok=tokens.shape[0]
    ranks=lax.axis_size("tensor")
    bits=lax.axis_size("dp").bit_length()-1
    me=lax.axis_index("tensor")
    rows_all=tok*ranks
    half=rows_all//2
    cols=w_qkv.shape[2]
    ends=jnp.cumsum(lengths[0])
    slots=lengths.shape[1]
    rel=jnp.arange(rows_all,dtype=jnp.int32)
    place=((rel//tok)^me)*tok+rel%tok
    seg=jnp.sum((place[:,None]>=ends[None,:]).astype(jnp.int32),axis=1)
    live=(place[:tok]<ends[-1]).astype(f32)[:,None]
    cgrp=jnp.concatenate([lax.dynamic_slice_in_dim(coords,(me^j)*tok,tok,1) for j in range(ranks)],axis=1).astype(f32)
    lane=jnp.arange(128,dtype=jnp.int32)
    pair=lane%(HDIM//2)
    freq=100.0**(-(pair//3).astype(f32)/(HDIM//2//3+1))
    angle=jnp.zeros((rows_all,128),f32)
    for a in range(3):
        angle=angle+cgrp[a][:,None]*jnp.where(pair%3==a,freq,0.0)[None,:]
    cos=jnp.cos(angle)
    sin=jnp.sin(angle)*jnp.where(lane%HDIM<HDIM//2,-1.0,1.0)[None,:]
    gains=norm_gains.astype(f32)
    shifts=shift_biases.astype(f32)
    x_rows=tokens.astype(f32)

    normed_one,norm_one_back=jax.vjp(norm_rows,x_rows,gains[0],shifts[0])
    low_one=normed_one.astype(bf16)
    far=flip(low_one,2)
    near=flip(low_one,1)
    grad_y=grad_out.astype(f32)*live
    grad_mlp=grad_y.astype(bf16)

    bq=b_qkv.astype(f32)
    qkv=qkv_rows(low_one,near,w_qkv,bq,cos,sin,0,None)
    far,*qkv=lax.optimization_barrier((far,*qkv))
    far_pair=flip(far,1)
    q,k,v=qkv_rows(far,far_pair,w_qkv,bq,cos,sin,1,qkv)
    n1=[low_one,near,far,far_pair]
    late=after(grad_mlp,far)
    gm=[late,flip(late,1),flip(late,2)]
    segq=seg[None,:]; segk=seg[:,None]
    hb=half//BLK
    codes=block_codes(seg,slots,False)
    att_far,lse_far=attn_fwd(codes[hb:],q,k,v,segq,segk,hb,hb)
    att_far,g2=lax.optimization_barrier((att_far,gm[2]))
    proj=lambda a: jnp.dot(a,w_proj,preferred_element_type=f32).astype(bf16)
    across=pair_sum(proj(att_far[tok:]),proj(att_far[:tok])).astype(bf16)
    q_late,across=lax.optimization_barrier((q,across))
    gm=[gm[0],gm[1],g2,flip(g2,1)]
    across=flip(across,3)
    att_near,lse_near=attn_fwd(codes[:hb],q_late,k,v,segq,segk,0,hb)
    across,att_near=lax.optimization_barrier((across,att_near))
    mine=pair_sum(proj(att_near[:tok]),proj(att_near[tok:]))
    resid_one=x_rows+mine+across.astype(f32)+shifts[2]
    normed_two,norm_two_back=jax.vjp(norm_rows,resid_one,gains[1],shifts[1])
    low_two=normed_two.astype(bf16)
    far=flip(low_two,2)
    near=flip(low_two,1)
    b1=b_fc1.astype(f32)[None,:]
    hid,gp,gn0,gn1,db0=mlp_rows((low_two,near),(gm[0],gm[1]),w_fc1,b1,w_fc2,0,None)
    far,hid,gp=lax.optimization_barrier((far,hid,gp))
    far_pair=flip(far,1)
    hid,gp,gn2,gn3,db1=mlp_rows((far,far_pair),(gm[2],gm[3]),w_fc1,b1,w_fc2,1,(hid,gp))
    db=db0+db1
    across=pair_sum(gn3,gn2).astype(bf16)
    hid,gp,across=lax.optimization_barrier((hid,gp,across))
    across=flip(across,3)
    mine=pair_sum(gn0,gn1)
    tn=lambda a,b: lax.dot_general(a,b,(((0,),(0,)),((),())),preferred_element_type=f32)
    grad_w1=tn(jnp.concatenate([low_two,near,far,far_pair],axis=0),gp).astype(bf16)
    grad_w2=tn(hid,jnp.concatenate(gm,axis=0)).astype(bf16)
    low_order=tuple(range(bits))
    swapped=(1,0)+tuple(range(2,bits))
    wsums=(DpSum(grad_w1,low_order),DpSum(grad_w2,swapped))
    sends=[t.operand() for t in wsums]
    across=after(across,*sends)
    for t,x in zip(wsums,sends): t.start(x)
    grad_resid_two,grad_gain_two,grad_shift_two=norm_two_back(mine+across.astype(f32))

    grad_resid_one=grad_y+grad_resid_two
    grad_attn=grad_resid_one.astype(bf16)
    grad_attn=settle(wsums,grad_attn)
    far=flip(grad_attn,2)
    near=flip(grad_attn,1)
    ghead=lambda a: lax.dot_general(a,w_proj,NT,preferred_element_type=f32).astype(bf16)
    bcodes=block_codes(seg,slots,True)
    do_near=jnp.concatenate([ghead(grad_attn),ghead(near)],axis=0)
    do_near=begin(wsums,do_near)
    bwd_near=lambda pair,do: attn_bwd(bcodes[:hb],q,k,v,do,att_near,lse_near,segq,segk,cos,sin,0,pair,None)
    gq0,dk0,dv0,bs0=bwd_near(0,do_near)
    dk0=settle(wsums,dk0)
    do_near,dk0=lax.optimization_barrier((do_near,dk0))
    do_near=begin(wsums,do_near)
    gq1,dk,dv1,bs1=bwd_near(1,do_near)
    gq_near=jnp.concatenate([gq0,gq1],axis=1)
    bs0=jnp.concatenate([bs0,bs1],axis=1)
    dk=settle(wsums,dk)
    for step in range(3,bits):
        for t in wsums: t.start(t.operand()); t.finish(t.got)
    early=jnp.stack([grad_gain_two,grad_shift_two,jnp.sum(grad_attn,axis=0,dtype=f32),jnp.sum(grad_mlp,axis=0,dtype=f32)])
    far,dk,early=lax.optimization_barrier((far,dk,early))
    far_pair=flip(far,1)
    do_far=jnp.concatenate([ghead(far),ghead(far_pair)],axis=0)
    alla=jnp.concatenate([grad_attn,near,far,far_pair],axis=0)
    grad_proj=tn(jnp.concatenate([att_near,att_far],axis=0),alla).astype(bf16)
    wpart=jnp.concatenate([t.cur for t in wsums],axis=0)
    do_far,grad_proj,wpart=lax.optimization_barrier((do_far,grad_proj,wpart))
    wsum=lax.all_gather(wpart,"dp",axis=0,tiled=True)
    gq_far,gk,gv,bs1=attn_bwd(bcodes[hb:],q,k,v,do_far,att_far,lse_far,segq,segk,cos,sin,1,None,([dk0,dk],[dv0,dv1]))
    r2,r3=back_rows(gq_far,gk,gv,w_qkv,1)
    across=pair_sum(r3,r2).astype(bf16)
    gq_near,gk,gv,across=lax.optimization_barrier((gq_near,gk,gv,across))
    across=flip(across,3)
    g_all=jnp.concatenate([jnp.concatenate([gq_near,gq_far],axis=0),gk,gv],axis=1)
    grad_wqkv=tn(jnp.concatenate(n1,axis=0),g_all).astype(bf16)
    grad_wqkv,hid,gq_near=lax.optimization_barrier((grad_wqkv,hid,gq_near))
    d=tokens.shape[1]
    sizes=(3*cols,db.shape[1])
    pad=(-sum(sizes))%(8*cols<<bits)
    small=jnp.concatenate([(bs0+bs1)[:3].reshape(-1),db[0],jnp.zeros((pad,),f32)]).astype(bf16).reshape(-1,cols)
    tail_a=DpSum(jnp.concatenate([grad_wqkv[:,:cols],grad_wqkv[:,cols:2*cols]],axis=0),tuple(range(bits)))
    tail_b=DpSum(jnp.concatenate([grad_wqkv[:,2*cols:],grad_proj.reshape(-1,cols),small],axis=0),(1,0)+tuple(range(2,bits)))
    tails=(tail_a,tail_b)
    for t in tails: t.start(t.operand())
    gq_near=settle(tails,gq_near)
    r0,r1=back_rows(gq_near,gk,gv,w_qkv,0)
    mine=pair_sum(r0,r1)
    o=[jnp.dot(hid[j*tok:(j+1)*tok],w_fc2,preferred_element_type=f32).astype(bf16) for j in range(ranks)]
    o_across=flip(pair_sum(o[3],o[2]).astype(bf16),3)
    for t in tails: t.start(t.operand())
    *gots,across,wsum=lax.optimization_barrier((tail_a.got,tail_b.got,across,wsum))
    for t,got in zip(tails,gots): t.finish(got)
    grad_x_norm,grad_gain_one,grad_shift_one=norm_one_back(mine+across.astype(f32))
    one=jnp.concatenate([jnp.stack([grad_gain_one,grad_shift_one]),early],axis=0)
    hops=[partial(dp_flip,bit=bit) for bit in range(bits)]+[partial(flip,bits=1),partial(flip,bits=2)]
    def whole(which,order):
        parts=wsum.reshape((2,)*bits+(2,-1,wsum.shape[1]))[(slice(None),)*bits+(which,)]
        return parts.transpose(tuple(bits-1-bit for bit in order)+(bits,bits+1)).reshape(-1,wsum.shape[1]).astype(f32)
    grad_w1,grad_w2=whole(0,low_order),whole(1,swapped)
    mine_out=resid_one+pair_sum(o[0],o[1])
    while hops or tail_a.at<len(tail_a.stages):
        busy=[t for t in tails if t.at<len(t.stages)]
        for t in busy: t.start(t.operand())
        hop=hops.pop(0) if hops else None
        other=hop(one) if hop else one
        gots=[t.got for t in busy]
        other,o_across,*gots=lax.optimization_barrier((other,o_across,*gots))
        if busy and busy[0].at==len(busy[0].stages)-2:
            output=(mine_out+o_across.astype(f32)+shifts[3]).astype(bf16)
        if busy and busy[0].at==len(busy[0].stages)-1:
            output,grad_w1,grad_w2,*gots=lax.optimization_barrier((output,grad_w1,grad_w2,*gots))
        for t,got in zip(busy,gots): t.finish(got)
        one=one+other if hop else one
    tail_a,tail_b=tail_a.cur,tail_b.cur
    grad_wqkv=jnp.stack([tail_a[:d],tail_a[d:],tail_b[:d]]).astype(f32)
    grad_wproj=tail_b[d:2*d].reshape(cols,d).astype(f32)
    small=tail_b[2*d:].reshape(-1).astype(f32)
    grad_bqkv=small[:sizes[0]].reshape(3,cols)
    grad_b1=small[sizes[0]:sizes[0]+sizes[1]]
    grad_tokens=(grad_resid_one+grad_x_norm).astype(bf16)
    return (output,grad_tokens,grad_wqkv,grad_bqkv,grad_wproj,grad_w1,grad_b1,grad_w2,
            jnp.stack([one[0],one[2]]),jnp.stack([one[1],one[3],one[4],one[5]]))


def solution(mesh):
    rows=P(("dp","tensor"),None)
    return jax.shard_map(shards,mesh=mesh,
        in_specs=(rows,rows,P("dp",None),P(None,"dp"),P(None,None,"tensor"),P(None,"tensor"),P("tensor",None),
                  P(None,"tensor"),P("tensor"),P("tensor",None),P(),P()),
        out_specs=(rows,rows,P(None,None,"tensor"),P(None,"tensor"),P("tensor",None),P(None,"tensor"),P("tensor"),
                   P("tensor",None),P(),P()),
        check_vma=False)
```

```python
from functools import partial

import jax
import jax.numpy as jnp
from jax import lax
from jax.experimental import pallas as pl
from jax.experimental.pallas import tpu as pltpu
from jax.sharding import PartitionSpec as P

HDIM=64
LOG2E=1.4426950408889634
LN2=0.6931471805599453
f32=jnp.float32; bf16=jnp.bfloat16
BLK=256
VROWS=80
NT=(((1,),(1,)),((),()))

def work(flops):
    return pl.CostEstimate(flops=flops,bytes_accessed=0,transcendentals=0)

def lane_half(shape, which):
    lane=lax.broadcasted_iota(jnp.int32, shape, 1)
    return (lane//HDIM)%2==which

def attn_fwd_kernel(codes, q_ref, k_ref, v_ref, segq_ref, segk_ref, o_ref, lse_ref, vt, qm, m_sc, acc, s_sc):
    step=pl.program_id(0)
    nkb=k_ref.shape[0]//BLK
    heads=q_ref.shape[1]//HDIM
    @pl.when(step==0)
    def _():
        for blk in range(nkb):
            rows=pl.ds(blk*BLK,BLK)
            vT=v_ref[rows,:].T
            for h in range(heads):
                vt[h*VROWS:h*VROWS+HDIM, rows]=vT[h*HDIM:(h+1)*HDIM,:]
        for h in range(heads):
            vt[h*VROWS+HDIM:(h+1)*VROWS,:]=jnp.ones((VROWS-HDIM,vt.shape[1]),bf16)
    for p in range(heads//2):
        qp=q_ref[:,p*128:(p+1)*128]
        for w in range(2):
            qm[2*p+w]=jnp.where(lane_half(qp.shape,w),qp,jnp.zeros_like(qp))
    m_sc[...]=jnp.full(m_sc.shape,-1e30,f32)
    acc[...]=jnp.zeros(acc.shape,f32)
    scale=HDIM**-0.5*LOG2E

    def tile(kb,masked):
        rows=pl.ds(pl.multiple_of(kb*BLK,BLK),BLK)
        if masked:
            allowed=segk_ref[rows,:][:,0:1]==segq_ref[0:1,:]
        tops=[]
        for h in range(heads):
            p=h//2
            s=lax.dot_general(k_ref[rows,p*128:(p+1)*128],qm[h],NT,preferred_element_type=f32)*scale
            if masked: s=jnp.where(allowed,s,-1e30)
            s_sc[h]=s
            tops.append(jnp.max(s,axis=0,keepdims=True))
        m_prev=m_sc[0:heads,:]
        m_new=jnp.maximum(m_prev,jnp.concatenate(tops,axis=0))
        alpha=jnp.exp2(m_prev-m_new)
        m_sc[0:heads,:]=m_new
        for h in range(heads):
            prob=jnp.exp2(s_sc[h]-m_new[h:h+1,:]).astype(bf16)
            arows=slice(h*VROWS,(h+1)*VROWS)
            acc[arows,:]=acc[arows,:]*alpha[h:h+1,:]+jnp.dot(vt[arows,rows],prob,preferred_element_type=f32)

    def body(kb,carry):
        code=codes[step,kb]
        @pl.when(code==1)
        def _(): tile(kb,False)
        @pl.when(code==2)
        def _(): tile(kb,True)
        return carry
    lax.fori_loop(0,nkb,body,0)
    outs=[]
    for h in range(heads):
        total=acc[h*VROWS+HDIM:h*VROWS+HDIM+1,:]
        outs.append(acc[h*VROWS:h*VROWS+HDIM,:]/total)
        lse_ref[h:h+1,:]=m_sc[h:h+1,:]+jnp.log2(total)
    for h in range(heads,8):
        lse_ref[h:h+1,:]=jnp.zeros((1,BLK),f32)
    o_ref[...]=jnp.concatenate(outs,axis=0).T.astype(bf16)

def attn_fwd(codes,q,k,v,segq,segk,block0,nblocks):
    rows,cols=k.shape
    heads=cols//HDIM
    full=lambda i,c:(0,0)
    return pl.pallas_call(
        attn_fwd_kernel,
        out_shape=(jax.ShapeDtypeStruct((nblocks*BLK,cols),bf16),jax.ShapeDtypeStruct((8,nblocks*BLK),f32)),
        grid_spec=pltpu.PrefetchScalarGridSpec(num_scalar_prefetch=1,grid=(nblocks,),
            in_specs=[pl.BlockSpec((BLK,cols),lambda i,c:(i+block0,0)),
                      pl.BlockSpec((rows,cols),full),pl.BlockSpec((rows,cols),full),
                      pl.BlockSpec((1,BLK),lambda i,c:(0,i+block0)),
                      pl.BlockSpec((rows,1),full)],
            out_specs=[pl.BlockSpec((BLK,cols),lambda i,c:(i,0)),pl.BlockSpec((8,BLK),lambda i,c:(0,i))],
            scratch_shapes=[pltpu.VMEM((heads*VROWS,rows),bf16),pltpu.VMEM((heads,BLK,128),bf16),
                            pltpu.VMEM((8,BLK),f32),pltpu.VMEM((heads*VROWS,BLK),f32),pltpu.VMEM((heads,BLK,BLK),f32)]),
        compiler_params=pltpu.CompilerParams(dimension_semantics=("arbitrary",)),
        name="attn_fwd",
        cost_estimate=work((4 if block0 else 64)*nblocks*BLK*rows*cols),
    )(codes,q,k,v,segq,segk)

def swap_halves(x):
    n=x.shape[1]
    lane=lax.broadcasted_iota(jnp.int32,x.shape,1)
    up=pltpu.roll(x,n-HDIM//2,1)
    down=pltpu.roll(x,HDIM//2,1)
    return jnp.where(lane%HDIM<HDIM//2,up,down)

def attn_bwd_kernel(last, codes, q_ref,k_ref,v_ref,do_ref,o_ref,lse_ref,segq_ref,segk_ref,cos_ref,sin_ref,cosk_ref,sink_ref,*rest):
    if last:
        dk0_ref,dv0_ref,gq_ref,gk_ref,gv_ref,bsum_ref,kt,qm,dom,delta,dq,dk,dv,p_sc,low_sc,ds_sc=rest
    else:
        gq_ref,gk_ref,gv_ref,bsum_ref,kt,qm,dom,delta,dq,dk,dv,p_sc,low_sc,ds_sc=rest
    step=pl.program_id(0)
    nkb=pl.num_programs(0)
    nqb=q_ref.shape[0]//BLK
    heads=q_ref.shape[1]//HDIM
    scale=HDIM**-0.5
    def unrotate(x,cos,sin):
        out=[]
        for p in range(heads//2):
            xp=x[:,p*128:(p+1)*128]
            out.append(xp*cos-swap_halves(xp)*sin)
        return jnp.concatenate(out,axis=1)
    @pl.when(step==0)
    def _():
        def prep(blk,carry):
            rows=pl.ds(pl.multiple_of(blk*BLK,BLK),BLK)
            for p in range(heads//2):
                lanes=slice(p*128,(p+1)*128)
                qp=q_ref[rows,lanes]; dp=do_ref[rows,lanes]
                for w in range(2):
                    sel=lane_half(qp.shape,w)
                    qm[2*p+w,rows,:]=jnp.where(sel,qp,jnp.zeros_like(qp))
                    dom[2*p+w,rows,:]=jnp.where(sel,dp,jnp.zeros_like(dp))
            prod=(do_ref[rows,:].astype(f32)*o_ref[rows,:].astype(f32)).T
            for h in range(heads):
                delta[h:h+1,rows]=jnp.sum(prod[h*HDIM:(h+1)*HDIM,:],axis=0,keepdims=True)
            return carry
        lax.fori_loop(0,nqb,prep,0)
        dq[...]=jnp.zeros(dq.shape,f32)
        bsum_ref[...]=jnp.zeros(bsum_ref.shape,f32)
    kt[...]=k_ref[...].T
    if last:
        dk[...]=dk0_ref[...]
        dv[...]=dv0_ref[...]
    else:
        dk[...]=jnp.zeros(dk.shape,f32)
        dv[...]=jnp.zeros(dv.shape,f32)

    def tile(qb,masked):
        rows=pl.ds(pl.multiple_of(qb*BLK,BLK),BLK)
        if masked:
            allowed=segk_ref[:,0:1]==segq_ref[0:1,rows]
        for h in range(heads):
            lanes=slice(h//2*128,(h//2+1)*128)
            s=lax.dot_general(k_ref[:,lanes],qm[h,rows,:],NT,preferred_element_type=f32)*(scale*LOG2E)
            prob=jnp.exp2(s-lse_ref[h:h+1,rows])
            if masked: prob=jnp.where(allowed,prob,0.0)
            p_sc[h]=prob
        for h in range(heads):
            lanes=slice(h//2*128,(h//2+1)*128)
            side=slice(h%2*BLK,(h%2+1)*BLK)
            dp=lax.dot_general(v_ref[:,lanes],dom[h,rows,:],NT,preferred_element_type=f32)
            prob=p_sc[h]
            low_sc[h//2,:,side]=prob.astype(bf16)
            ds_sc[h//2,:,side]=(prob*(dp-delta[h:h+1,rows])).astype(bf16)
        for p in range(heads//2):
            lanes=slice(p*128,(p+1)*128)
            pair=slice(2*p,2*p+2)
            dv[:,lanes]+=jnp.dot(low_sc[p],dom[pair,rows,:].reshape(2*BLK,128),preferred_element_type=f32)
            dk[:,lanes]+=jnp.dot(ds_sc[p],qm[pair,rows,:].reshape(2*BLK,128),preferred_element_type=f32)
        for h in range(heads):
            hr=slice(h*HDIM,(h+1)*HDIM)
            side=slice(h%2*BLK,(h%2+1)*BLK)
            dq[hr,rows]+=jnp.dot(kt[hr,:],ds_sc[h//2,:,side],preferred_element_type=f32)

    def body(qb,carry):
        code=codes[qb,step]
        @pl.when(code==1)
        def _(): tile(qb,False)
        @pl.when(code==2)
        def _(): tile(qb,True)
        return carry
    lax.fori_loop(0,nqb,body,0)

    if last:
        gk=unrotate(dk[...]*scale,cosk_ref[...],sink_ref[...]).astype(bf16)
        gv=dv[...].astype(bf16)
        gk_ref[...]=gk
        gv_ref[...]=gv
        bsum_ref[1:2,:]+=jnp.sum(gk.astype(f32),axis=0,keepdims=True)
        bsum_ref[2:3,:]+=jnp.sum(gv.astype(f32),axis=0,keepdims=True)
    else:
        gk_ref[...]=dk[...]
        gv_ref[...]=dv[...]

    @pl.when(step==nkb-1)
    def _():
        def fin(blk,carry):
            rows=pl.ds(pl.multiple_of(blk*BLK,BLK),BLK)
            gq=unrotate(dq[:,rows].T*scale,cos_ref[rows,:],sin_ref[rows,:]).astype(bf16)
            gq_ref[rows,:]=gq
            bsum_ref[0:1,:]+=jnp.sum(gq.astype(f32),axis=0,keepdims=True)
            return carry
        lax.fori_loop(0,nqb,fin,0)

def attn_bwd(codes,q,k,v,do,o,lse,segq,segk,cos,sin,part,carried):
    rows,cols=k.shape
    half=do.shape[0]
    heads=cols//HDIM
    nb=rows//BLK
    last=carried is not None
    mine=lambda n: pl.BlockSpec((half,n),lambda i,c:(part,0))
    here=lambda n: pl.BlockSpec((half,n),lambda i,c:(0,0))
    blk=lambda n: pl.BlockSpec((BLK,n),lambda i,c:(i,0))
    kdtype=bf16 if last else f32
    return pl.pallas_call(
        partial(attn_bwd_kernel,last),
        out_shape=(jax.ShapeDtypeStruct((half,cols),bf16),jax.ShapeDtypeStruct((rows,cols),kdtype),
                   jax.ShapeDtypeStruct((rows,cols),kdtype),jax.ShapeDtypeStruct((8,cols),f32)),
        grid_spec=pltpu.PrefetchScalarGridSpec(num_scalar_prefetch=1,grid=(nb,),
            in_specs=[mine(cols),blk(cols),blk(cols),here(cols),here(cols),pl.BlockSpec((8,half),lambda i,c:(0,0)),
                      pl.BlockSpec((1,half),lambda i,c:(0,part)),blk(1),mine(128),mine(128),blk(128),blk(128)]
                     +([blk(cols),blk(cols)] if last else []),
            out_specs=[here(cols),blk(cols),blk(cols),pl.BlockSpec((8,cols),lambda i,c:(0,0))],
            scratch_shapes=[pltpu.VMEM((cols,BLK),bf16),pltpu.VMEM((heads,half,128),bf16),pltpu.VMEM((heads,half,128),bf16),
                            pltpu.VMEM((8,half),f32),pltpu.VMEM((cols,half),f32),pltpu.VMEM((BLK,cols),f32),pltpu.VMEM((BLK,cols),f32),
                            pltpu.VMEM((heads,BLK,BLK),f32),pltpu.VMEM((heads//2,BLK,2*BLK),bf16),pltpu.VMEM((heads//2,BLK,2*BLK),bf16)]),
        compiler_params=pltpu.CompilerParams(dimension_semantics=("arbitrary",)),
        name="attn_bwd",
        cost_estimate=work(45*half*rows*cols),
    )(codes,q,k,v,do,o,lse,segq,segk,cos,sin,cos,sin,*(carried or ()))

def block_codes(seg,pad_seg,skip_pad):
    sb=seg.reshape(-1,BLK)
    lo=jnp.min(sb,axis=1); hi=jnp.max(sb,axis=1)
    meet=(lo[:,None]<=hi[None,:])&(lo[None,:]<=hi[:,None])
    whole=(lo==hi)
    same=whole[:,None]&whole[None,:]&(lo[:,None]==lo[None,:])
    code=jnp.where(meet,jnp.where(same,1,2),0).astype(jnp.int32)
    if skip_pad:
        alive=lo<pad_seg
        code=jnp.where(alive[:,None]&alive[None,:],code,0)
    return code


def pick(i,n,a_ref,b_ref):
    return jnp.where(i<n,a_ref[...],b_ref[...])


def qkv_kernel(n, xa_ref, xb_ref, w_ref, b_ref, cos_ref, sin_ref, *rest):
    x=pick(pl.program_id(0),n,xa_ref,xb_ref)
    cos=cos_ref[...]; sin=sin_ref[...]
    for c,o_ref in enumerate(rest[-3:]):
        y=jnp.dot(x,w_ref[c],preferred_element_type=f32)+b_ref[c:c+1,:]
        if c<2:
            parts=[]
            for p in range(y.shape[1]//128):
                yp=y[:,p*128:(p+1)*128]
                parts.append(yp*cos+swap_halves(yp)*sin)
            y=jnp.concatenate(parts,axis=1)
        o_ref[...]=y.astype(bf16)


def two(tile,n,width):
    return [pl.BlockSpec((tile,width),lambda i:(jnp.minimum(i,n-1),0)),
            pl.BlockSpec((tile,width),lambda i:(jnp.maximum(i-n,0),0))]


def qkv_rows(xa,xb,w,b,cos,sin,part,full):
    rows,d=xa.shape
    cols=w.shape[2]
    tile=min(512,rows)
    n=rows//tile
    off=part*2*n
    row=lambda m: pl.BlockSpec((tile,m),lambda i:(i+off,0))
    kept=[] if full is None else list(full)
    return pl.pallas_call(
        partial(qkv_kernel,n),
        grid=(2*n,),
        out_shape=[jax.ShapeDtypeStruct((cos.shape[0],cols),bf16)]*3,
        in_specs=two(tile,n,d)+[pl.BlockSpec(w.shape,lambda i:(0,0,0)),pl.BlockSpec(b.shape,lambda i:(0,0)),
                  row(128),row(128)]+[pl.BlockSpec(memory_space=pl.ANY)]*len(kept),
        out_specs=[row(cols)]*3,
        input_output_aliases={6+i:i for i in range(len(kept))},
        compiler_params=pltpu.CompilerParams(dimension_semantics=("arbitrary",)),
        name="qkv",
        cost_estimate=work(20*rows*d*cols*2),
    )(xa,xb,w,b,cos,sin,*kept)


def mlp_kernel(n,xa_ref,xb_ref,ga_ref,gb_ref,w1_ref,b1_ref,w2_ref,*rest):
    hid_ref,gp_ref,na_ref,nb_ref,db_ref=rest[-5:]
    i=pl.program_id(0)
    @pl.when(i==0)
    def _():
        db_ref[...]=jnp.zeros(db_ref.shape,f32)
    pre=jnp.dot(pick(i,n,xa_ref,xb_ref),w1_ref[...],preferred_element_type=f32)+b1_ref[...]
    phi=0.5+0.5*lax.erf(pre*0.7071067811865476)
    hid_ref[...]=(pre*phi).astype(bf16)
    slope=phi+pre*(0.3989422804014327*jnp.exp2(pre*pre*(-0.5*LOG2E)))
    gh=lax.dot_general(pick(i,n,ga_ref,gb_ref),w2_ref[...],NT,preferred_element_type=f32)
    gp=(gh*slope).astype(bf16)
    gp_ref[...]=gp
    db_ref[...]+=jnp.sum(gp.astype(f32),axis=0,keepdims=True)
    gn=lax.dot_general(gp,w1_ref[...],NT,preferred_element_type=f32).astype(bf16)
    @pl.when(i<n)
    def _(): na_ref[...]=gn
    @pl.when(i>=n)
    def _(): nb_ref[...]=gn


def mlp_rows(xs,gs,w1,b1,w2,part,full):
    rows,d=xs[0].shape
    units=w1.shape[1]
    tile=min(256,rows)
    n=rows//tile
    off=part*2*n
    row=lambda m: pl.BlockSpec((tile,m),lambda i:(i+off,0))
    whole=lambda a: pl.BlockSpec(a.shape,lambda i:(0,0))
    kept=[] if full is None else list(full)
    return pl.pallas_call(
        partial(mlp_kernel,n),
        grid=(2*n,),
        out_shape=[jax.ShapeDtypeStruct((rows*4,units),bf16)]*2+[jax.ShapeDtypeStruct((rows,d),bf16)]*2+
                  [jax.ShapeDtypeStruct((1,units),f32)],
        in_specs=two(tile,n,d)+two(tile,n,d)+[whole(w1),whole(b1),whole(w2)]+[pl.BlockSpec(memory_space=pl.ANY)]*len(kept),
        out_specs=[row(units),row(units)]+two(tile,n,d)+[pl.BlockSpec((1,units),lambda i:(0,0))],
        input_output_aliases={7+i:i for i in range(len(kept))},
        compiler_params=pltpu.CompilerParams(dimension_semantics=("arbitrary",)),
        name="mlp",
        cost_estimate=work(12*rows*d*units),
    )(*xs,*gs,w1,b1,w2,*kept)


def back_kernel(n,gq_ref,gk_ref,gv_ref,w_ref,oa_ref,ob_ref):
    i=pl.program_id(0)
    y=lax.dot_general(gq_ref[...],w_ref[0],NT,preferred_element_type=f32)
    y=y+lax.dot_general(gk_ref[...],w_ref[1],NT,preferred_element_type=f32)
    y=(y+lax.dot_general(gv_ref[...],w_ref[2],NT,preferred_element_type=f32)).astype(bf16)
    @pl.when(i<n)
    def _(): oa_ref[...]=y
    @pl.when(i>=n)
    def _(): ob_ref[...]=y


def back_rows(gq,gk,gv,w,part):
    half,cols=gq.shape
    rows=half//2
    d=w.shape[1]
    tile=min(512,rows)
    n=rows//tile
    off=part*2*n
    row=pl.BlockSpec((tile,cols),lambda i:(i+off,0))
    return pl.pallas_call(
        partial(back_kernel,n),
        grid=(2*n,),
        out_shape=[jax.ShapeDtypeStruct((rows,d),bf16)]*2,
        in_specs=[pl.BlockSpec((tile,cols),lambda i:(i,0)),row,row,pl.BlockSpec(w.shape,lambda i:(0,0,0))],
        out_specs=two(tile,n,d),
        compiler_params=pltpu.CompilerParams(dimension_semantics=("arbitrary",)),
        name="back",
        cost_estimate=work(1),
    )(gq,gk,gv,w)


def norm_rows(values_in, gain_row, shift_row):
    row_mean = jnp.mean(values_in, axis=-1, keepdims=True)
    centred = values_in - row_mean
    variance = jnp.mean(centred * centred, axis=-1, keepdims=True)
    return centred * lax.rsqrt(variance + 1e-06) * gain_row + shift_row


def flip(x,bits):
    n=lax.axis_size("tensor")
    return lax.ppermute(x,"tensor",[(i,i^bits) for i in range(n)])


def pair_sum(mine,other):
    return mine.astype(f32)+flip(other,1).astype(f32)


def dp_flip(x,bit):
    n=lax.axis_size("dp")
    return lax.ppermute(x,"dp",[(i,i^(1<<bit)) for i in range(n)])


class DpSum:
    def __init__(self,x,order):
        self.cur=x
        self.stages=[(bit,True) for bit in order]+[(bit,False) for bit in reversed(order)]
        self.at=0

    def operand(self):
        bit,halving=self.stages[self.at]
        if not halving: return self.cur
        up=(lax.axis_index("dp")>>bit)&1
        halves=self.cur.reshape(2,-1,self.cur.shape[1])
        self.kept=lax.dynamic_index_in_dim(halves,up,0,False)
        return lax.dynamic_index_in_dim(halves,1-up,0,False)

    def start(self,operand):
        self.sent=operand
        self.got=dp_flip(operand,self.stages[self.at][0])

    def finish(self,got):
        bit,halving=self.stages[self.at]
        self.at+=1
        if halving:
            self.cur=(self.kept.astype(f32)+got.astype(f32)).astype(bf16)
        else:
            up=((lax.axis_index("dp")>>bit)&1)==1
            self.cur=jnp.concatenate([jnp.where(up,got,self.sent),jnp.where(up,self.sent,got)],axis=0)

    def rest(self):
        while self.at<len(self.stages):
            self.start(self.operand())
            self.finish(self.got)
        return self.cur


def begin(sums,value):
    value,*sends=lax.optimization_barrier((value,*[s.operand() for s in sums]))
    for s,x in zip(sums,sends): s.start(x)
    return value


def settle(sums,value):
    value,*gots=lax.optimization_barrier((value,*[s.got for s in sums]))
    for s,x in zip(sums,gots): s.finish(x)
    return value


def all_sum(x):
    for bits in (1,2):
        x=x+flip(x,bits)
    for bit in range(lax.axis_size("dp").bit_length()-1):
        x=x+dp_flip(x,bit)
    return x


def after(x,*others):
    return lax.optimization_barrier((x,)+others)[0]


def shards(tokens,grad_out,lengths,coords,w_qkv,b_qkv,w_proj,w_fc1,b_fc1,w_fc2,norm_gains,shift_biases):
    tok=tokens.shape[0]
    ranks=lax.axis_size("tensor")
    bits=lax.axis_size("dp").bit_length()-1
    me=lax.axis_index("tensor")
    rows_all=tok*ranks
    half=rows_all//2
    cols=w_qkv.shape[2]
    ends=jnp.cumsum(lengths[0])
    slots=lengths.shape[1]
    rel=jnp.arange(rows_all,dtype=jnp.int32)
    place=((rel//tok)^me)*tok+rel%tok
    seg=jnp.sum((place[:,None]>=ends[None,:]).astype(jnp.int32),axis=1)
    live=(place[:tok]<ends[-1]).astype(f32)[:,None]
    cgrp=jnp.concatenate([lax.dynamic_slice_in_dim(coords,(me^j)*tok,tok,1) for j in range(ranks)],axis=1).astype(f32)
    lane=jnp.arange(128,dtype=jnp.int32)
    pair=lane%(HDIM//2)
    freq=100.0**(-(pair//3).astype(f32)/(HDIM//2//3+1))
    angle=jnp.zeros((rows_all,128),f32)
    for a in range(3):
        angle=angle+cgrp[a][:,None]*jnp.where(pair%3==a,freq,0.0)[None,:]
    cos=jnp.cos(angle)
    sin=jnp.sin(angle)*jnp.where(lane%HDIM<HDIM//2,-1.0,1.0)[None,:]
    gains=norm_gains.astype(f32)
    shifts=shift_biases.astype(f32)
    x_rows=tokens.astype(f32)

    normed_one,norm_one_back=jax.vjp(norm_rows,x_rows,gains[0],shifts[0])
    low_one=normed_one.astype(bf16)
    far=flip(low_one,2)
    near=flip(low_one,1)
    grad_y=grad_out.astype(f32)*live
    grad_mlp=grad_y.astype(bf16)

    bq=b_qkv.astype(f32)
    qkv=qkv_rows(low_one,near,w_qkv,bq,cos,sin,0,None)
    far,*qkv=lax.optimization_barrier((far,*qkv))
    far_pair=flip(far,1)
    q,k,v=qkv_rows(far,far_pair,w_qkv,bq,cos,sin,1,qkv)
    n1=[low_one,near,far,far_pair]
    late=after(grad_mlp,far)
    gm=[late,flip(late,1),flip(late,2)]
    segq=seg[None,:]; segk=seg[:,None]
    hb=half//BLK
    codes=block_codes(seg,slots,False)
    att_far,lse_far=attn_fwd(codes[hb:],q,k,v,segq,segk,hb,hb)
    att_far,g2=lax.optimization_barrier((att_far,gm[2]))
    proj=lambda a: jnp.dot(a,w_proj,preferred_element_type=f32).astype(bf16)
    across=pair_sum(proj(att_far[tok:]),proj(att_far[:tok])).astype(bf16)
    q_late,across=lax.optimization_barrier((q,across))
    gm=[gm[0],gm[1],g2,flip(g2,1)]
    across=flip(across,3)
    att_near,lse_near=attn_fwd(codes[:hb],q_late,k,v,segq,segk,0,hb)
    across,att_near=lax.optimization_barrier((across,att_near))
    mine=pair_sum(proj(att_near[:tok]),proj(att_near[tok:]))
    resid_one=x_rows+mine+across.astype(f32)+shifts[2]
    normed_two,norm_two_back=jax.vjp(norm_rows,resid_one,gains[1],shifts[1])
    low_two=normed_two.astype(bf16)
    far=flip(low_two,2)
    near=flip(low_two,1)
    b1=b_fc1.astype(f32)[None,:]
    hid,gp,gn0,gn1,db0=mlp_rows((low_two,near),(gm[0],gm[1]),w_fc1,b1,w_fc2,0,None)
    far,hid,gp=lax.optimization_barrier((far,hid,gp))
    far_pair=flip(far,1)
    hid,gp,gn2,gn3,db1=mlp_rows((far,far_pair),(gm[2],gm[3]),w_fc1,b1,w_fc2,1,(hid,gp))
    db=db0+db1
    across=pair_sum(gn3,gn2).astype(bf16)
    hid,gp,across=lax.optimization_barrier((hid,gp,across))
    across=flip(across,3)
    mine=pair_sum(gn0,gn1)
    tn=lambda a,b: lax.dot_general(a,b,(((0,),(0,)),((),())),preferred_element_type=f32)
    grad_w1=tn(jnp.concatenate([low_two,near,far,far_pair],axis=0),gp).astype(bf16)
    grad_w2=tn(hid,jnp.concatenate(gm,axis=0)).astype(bf16)
    both=jnp.concatenate([grad_w1,grad_w2],axis=0)
    across=after(across,both)
    wsum=lax.psum_scatter(both,"dp",scatter_dimension=0,tiled=True)
    grad_resid_two,grad_gain_two,grad_shift_two=norm_two_back(mine+across.astype(f32))

    grad_resid_one=grad_y+grad_resid_two
    grad_attn=grad_resid_one.astype(bf16)
    far=flip(grad_attn,2)
    near=flip(grad_attn,1)
    ghead=lambda a: lax.dot_general(a,w_proj,NT,preferred_element_type=f32).astype(bf16)
    bcodes=block_codes(seg,slots,True)
    do_near=jnp.concatenate([ghead(grad_attn),ghead(near)],axis=0)
    gq_near,dk,dv,bs0=attn_bwd(bcodes[:hb],q,k,v,do_near,att_near,lse_near,segq,segk,cos,sin,0,None)
    early=jnp.stack([grad_gain_two,grad_shift_two,jnp.sum(grad_attn,axis=0,dtype=f32),jnp.sum(grad_mlp,axis=0,dtype=f32)])
    far,dk,dv,early=lax.optimization_barrier((far,dk,dv,early))
    far_pair=flip(far,1)
    do_far=jnp.concatenate([ghead(far),ghead(far_pair)],axis=0)
    alla=jnp.concatenate([grad_attn,near,far,far_pair],axis=0)
    grad_proj=tn(jnp.concatenate([att_near,att_far],axis=0),alla).astype(bf16)
    do_far,grad_proj=lax.optimization_barrier((do_far,grad_proj))
    gq_far,gk,gv,bs1=attn_bwd(bcodes[hb:],q,k,v,do_far,att_far,lse_far,segq,segk,cos,sin,1,(dk,dv))
    gk,wsum=lax.optimization_barrier((gk,wsum))
    wsum=lax.all_gather(wsum,"dp",axis=0,tiled=True)
    r2,r3=back_rows(gq_far,gk,gv,w_qkv,1)
    across=pair_sum(r3,r2).astype(bf16)
    gq_near,gk,gv,across=lax.optimization_barrier((gq_near,gk,gv,across))
    across=flip(across,3)
    g_all=jnp.concatenate([jnp.concatenate([gq_near,gq_far],axis=0),gk,gv],axis=1)
    grad_wqkv=tn(jnp.concatenate(n1,axis=0),g_all).astype(bf16)
    grad_wqkv,hid,gq_near=lax.optimization_barrier((grad_wqkv,hid,gq_near))
    d=tokens.shape[1]
    sizes=(3*cols,db.shape[1])
    pad=(-sum(sizes))%(8*cols<<bits)
    small=jnp.concatenate([(bs0+bs1)[:3].reshape(-1),db[0],jnp.zeros((pad,),f32)]).astype(bf16).reshape(-1,cols)
    tail_a=DpSum(jnp.concatenate([grad_wqkv[:,:cols],grad_wqkv[:,cols:2*cols]],axis=0),tuple(range(bits)))
    tail_b=DpSum(jnp.concatenate([grad_wqkv[:,2*cols:],grad_proj.reshape(-1,cols),small],axis=0),(1,0)+tuple(range(2,bits)))
    tails=(tail_a,tail_b)
    for t in tails: t.start(t.operand())
    *gots,across=lax.optimization_barrier((tail_a.got,tail_b.got,across))
    for t,got in zip(tails,gots): t.finish(got)
    r0,r1=back_rows(gq_near,gk,gv,w_qkv,0)
    mine=pair_sum(r0,r1)
    grad_x_norm,grad_gain_one,grad_shift_one=norm_one_back(mine+across.astype(f32))
    one=jnp.concatenate([jnp.stack([grad_gain_one,grad_shift_one]),early],axis=0)
    o=[jnp.dot(hid[j*tok:(j+1)*tok],w_fc2,preferred_element_type=f32).astype(bf16) for j in range(ranks)]
    o_across=flip(pair_sum(o[3],o[2]).astype(bf16),3)
    for t in tails: t.start(t.operand())
    one,*gots=lax.optimization_barrier((one,tail_a.got,tail_b.got))
    for t,got in zip(tails,gots): t.finish(got)
    hops=[partial(dp_flip,bit=bit) for bit in range(bits)]+[partial(flip,bits=1),partial(flip,bits=2)]
    while hops or tail_a.at<len(tail_a.stages):
        busy=[t for t in tails if t.at<len(t.stages)]
        for t in busy: t.start(t.operand())
        hop=hops.pop(0) if hops else None
        other=hop(one) if hop else one
        third=bool(busy) and busy[0].at==bits-1
        gots=[t.got for t in busy]
        if third:
            other,o_across,wsum,*gots=lax.optimization_barrier((other,o_across,wsum,*gots))
        else:
            other,*gots=lax.optimization_barrier((other,*gots))
        for t,got in zip(busy,gots): t.finish(got)
        one=one+other if hop else one
    tail_a,tail_b=tail_a.cur,tail_b.cur
    output=(resid_one+pair_sum(o[0],o[1])+o_across.astype(f32)+shifts[3]).astype(bf16)
    grad_w1,grad_w2=wsum[:d],wsum[d:]
    grad_wqkv=jnp.stack([tail_a[:d],tail_a[d:],tail_b[:d]]).astype(f32)
    grad_wproj=tail_b[d:2*d].reshape(cols,d).astype(f32)
    small=tail_b[2*d:].reshape(-1).astype(f32)
    grad_bqkv=small[:sizes[0]].reshape(3,cols)
    grad_b1=small[sizes[0]:sizes[0]+sizes[1]]
    grad_tokens=(grad_resid_one+grad_x_norm).astype(bf16)
    return (output,grad_tokens,grad_wqkv,grad_bqkv,grad_wproj,grad_w1.astype(f32),grad_b1,grad_w2.astype(f32),
            jnp.stack([one[0],one[2]]),jnp.stack([one[1],one[3],one[4],one[5]]))


def solution(mesh):
    rows=P(("dp","tensor"),None)
    return jax.shard_map(shards,mesh=mesh,
        in_specs=(rows,rows,P("dp",None),P(None,"dp"),P(None,None,"tensor"),P(None,"tensor"),P("tensor",None),
                  P(None,"tensor"),P("tensor"),P("tensor",None),P(),P()),
        out_specs=(rows,rows,P(None,None,"tensor"),P(None,"tensor"),P("tensor",None),P(None,"tensor"),P("tensor"),
                   P("tensor",None),P(),P()),
        check_vma=False)
```

```python
from functools import partial

import jax
import jax.numpy as jnp
from jax import lax
from jax.experimental import pallas as pl
from jax.experimental.pallas import tpu as pltpu
from jax.sharding import PartitionSpec as P

HDIM=64
LOG2E=1.4426950408889634
LN2=0.6931471805599453
f32=jnp.float32; bf16=jnp.bfloat16
BLK=256
VROWS=80
NT=(((1,),(1,)),((),()))

def work(flops):
    return pl.CostEstimate(flops=flops,bytes_accessed=0,transcendentals=0)

def lane_half(shape, which):
    lane=lax.broadcasted_iota(jnp.int32, shape, 1)
    return (lane//HDIM)%2==which

def attn_fwd_kernel(codes, q_ref, k_ref, v_ref, segq_ref, segk_ref, o_ref, lse_ref, vt, qm, m_sc, acc, s_sc):
    step=pl.program_id(0)
    nkb=k_ref.shape[0]//BLK
    heads=q_ref.shape[1]//HDIM
    @pl.when(step==0)
    def _():
        for blk in range(nkb):
            rows=pl.ds(blk*BLK,BLK)
            vT=v_ref[rows,:].T
            for h in range(heads):
                vt[h*VROWS:h*VROWS+HDIM, rows]=vT[h*HDIM:(h+1)*HDIM,:]
        for h in range(heads):
            vt[h*VROWS+HDIM:(h+1)*VROWS,:]=jnp.ones((VROWS-HDIM,vt.shape[1]),bf16)
    for p in range(heads//2):
        qp=q_ref[:,p*128:(p+1)*128]
        for w in range(2):
            qm[2*p+w]=jnp.where(lane_half(qp.shape,w),qp,jnp.zeros_like(qp))
    m_sc[...]=jnp.full(m_sc.shape,-1e30,f32)
    acc[...]=jnp.zeros(acc.shape,f32)
    scale=HDIM**-0.5*LOG2E

    def tile(kb,masked):
        rows=pl.ds(pl.multiple_of(kb*BLK,BLK),BLK)
        if masked:
            allowed=segk_ref[rows,:][:,0:1]==segq_ref[0:1,:]
        tops=[]
        for h in range(heads):
            p=h//2
            s=lax.dot_general(k_ref[rows,p*128:(p+1)*128],qm[h],NT,preferred_element_type=f32)*scale
            if masked: s=jnp.where(allowed,s,-1e30)
            s_sc[h]=s
            tops.append(jnp.max(s,axis=0,keepdims=True))
        m_prev=m_sc[0:heads,:]
        m_new=jnp.maximum(m_prev,jnp.concatenate(tops,axis=0))
        alpha=jnp.exp2(m_prev-m_new)
        m_sc[0:heads,:]=m_new
        for h in range(heads):
            prob=jnp.exp2(s_sc[h]-m_new[h:h+1,:]).astype(bf16)
            arows=slice(h*VROWS,(h+1)*VROWS)
            acc[arows,:]=acc[arows,:]*alpha[h:h+1,:]+jnp.dot(vt[arows,rows],prob,preferred_element_type=f32)

    def body(kb,carry):
        code=codes[step,kb]
        @pl.when(code==1)
        def _(): tile(kb,False)
        @pl.when(code==2)
        def _(): tile(kb,True)
        return carry
    lax.fori_loop(0,nkb,body,0)
    outs=[]
    for h in range(heads):
        total=acc[h*VROWS+HDIM:h*VROWS+HDIM+1,:]
        outs.append(acc[h*VROWS:h*VROWS+HDIM,:]/total)
        lse_ref[h:h+1,:]=m_sc[h:h+1,:]+jnp.log2(total)
    for h in range(heads,8):
        lse_ref[h:h+1,:]=jnp.zeros((1,BLK),f32)
    o_ref[...]=jnp.concatenate(outs,axis=0).T.astype(bf16)

def attn_fwd(codes,q,k,v,segq,segk,block0,nblocks):
    rows,cols=k.shape
    heads=cols//HDIM
    full=lambda i,c:(0,0)
    return pl.pallas_call(
        attn_fwd_kernel,
        out_shape=(jax.ShapeDtypeStruct((nblocks*BLK,cols),bf16),jax.ShapeDtypeStruct((8,nblocks*BLK),f32)),
        grid_spec=pltpu.PrefetchScalarGridSpec(num_scalar_prefetch=1,grid=(nblocks,),
            in_specs=[pl.BlockSpec((BLK,cols),lambda i,c:(i+block0,0)),
                      pl.BlockSpec((rows,cols),full),pl.BlockSpec((rows,cols),full),
                      pl.BlockSpec((1,BLK),lambda i,c:(0,i+block0)),
                      pl.BlockSpec((rows,1),full)],
            out_specs=[pl.BlockSpec((BLK,cols),lambda i,c:(i,0)),pl.BlockSpec((8,BLK),lambda i,c:(0,i))],
            scratch_shapes=[pltpu.VMEM((heads*VROWS,rows),bf16),pltpu.VMEM((heads,BLK,128),bf16),
                            pltpu.VMEM((8,BLK),f32),pltpu.VMEM((heads*VROWS,BLK),f32),pltpu.VMEM((heads,BLK,BLK),f32)]),
        compiler_params=pltpu.CompilerParams(dimension_semantics=("arbitrary",)),
        name="attn_fwd",
        cost_estimate=work((4 if block0 else 64)*nblocks*BLK*rows*cols),
    )(codes,q,k,v,segq,segk)

def swap_halves(x):
    n=x.shape[1]
    lane=lax.broadcasted_iota(jnp.int32,x.shape,1)
    up=pltpu.roll(x,n-HDIM//2,1)
    down=pltpu.roll(x,HDIM//2,1)
    return jnp.where(lane%HDIM<HDIM//2,up,down)

def attn_bwd_kernel(last, codes, q_ref,k_ref,v_ref,do_ref,o_ref,lse_ref,segq_ref,segk_ref,cos_ref,sin_ref,cosk_ref,sink_ref,*rest):
    if last:
        dk0_ref,dv0_ref,gq_ref,gk_ref,gv_ref,bsum_ref,kt,qm,dom,delta,dq,dk,dv,p_sc,low_sc,ds_sc=rest
    else:
        gq_ref,gk_ref,gv_ref,bsum_ref,kt,qm,dom,delta,dq,dk,dv,p_sc,low_sc,ds_sc=rest
    step=pl.program_id(0)
    nkb=pl.num_programs(0)
    nqb=q_ref.shape[0]//BLK
    heads=q_ref.shape[1]//HDIM
    scale=HDIM**-0.5
    def unrotate(x,cos,sin):
        out=[]
        for p in range(heads//2):
            xp=x[:,p*128:(p+1)*128]
            out.append(xp*cos-swap_halves(xp)*sin)
        return jnp.concatenate(out,axis=1)
    @pl.when(step==0)
    def _():
        def prep(blk,carry):
            rows=pl.ds(pl.multiple_of(blk*BLK,BLK),BLK)
            for p in range(heads//2):
                lanes=slice(p*128,(p+1)*128)
                qp=q_ref[rows,lanes]; dp=do_ref[rows,lanes]
                for w in range(2):
                    sel=lane_half(qp.shape,w)
                    qm[2*p+w,rows,:]=jnp.where(sel,qp,jnp.zeros_like(qp))
                    dom[2*p+w,rows,:]=jnp.where(sel,dp,jnp.zeros_like(dp))
            prod=(do_ref[rows,:].astype(f32)*o_ref[rows,:].astype(f32)).T
            for h in range(heads):
                delta[h:h+1,rows]=jnp.sum(prod[h*HDIM:(h+1)*HDIM,:],axis=0,keepdims=True)
            return carry
        lax.fori_loop(0,nqb,prep,0)
        dq[...]=jnp.zeros(dq.shape,f32)
        bsum_ref[...]=jnp.zeros(bsum_ref.shape,f32)
    kt[...]=k_ref[...].T
    if last:
        dk[...]=dk0_ref[...]
        dv[...]=dv0_ref[...]
    else:
        dk[...]=jnp.zeros(dk.shape,f32)
        dv[...]=jnp.zeros(dv.shape,f32)

    def tile(qb,masked):
        rows=pl.ds(pl.multiple_of(qb*BLK,BLK),BLK)
        if masked:
            allowed=segk_ref[:,0:1]==segq_ref[0:1,rows]
        for h in range(heads):
            lanes=slice(h//2*128,(h//2+1)*128)
            s=lax.dot_general(k_ref[:,lanes],qm[h,rows,:],NT,preferred_element_type=f32)*(scale*LOG2E)
            prob=jnp.exp2(s-lse_ref[h:h+1,rows])
            if masked: prob=jnp.where(allowed,prob,0.0)
            p_sc[h]=prob
        for h in range(heads):
            lanes=slice(h//2*128,(h//2+1)*128)
            side=slice(h%2*BLK,(h%2+1)*BLK)
            dp=lax.dot_general(v_ref[:,lanes],dom[h,rows,:],NT,preferred_element_type=f32)
            prob=p_sc[h]
            low_sc[h//2,:,side]=prob.astype(bf16)
            ds_sc[h//2,:,side]=(prob*(dp-delta[h:h+1,rows])).astype(bf16)
        for p in range(heads//2):
            lanes=slice(p*128,(p+1)*128)
            pair=slice(2*p,2*p+2)
            dv[:,lanes]+=jnp.dot(low_sc[p],dom[pair,rows,:].reshape(2*BLK,128),preferred_element_type=f32)
            dk[:,lanes]+=jnp.dot(ds_sc[p],qm[pair,rows,:].reshape(2*BLK,128),preferred_element_type=f32)
        for h in range(heads):
            hr=slice(h*HDIM,(h+1)*HDIM)
            side=slice(h%2*BLK,(h%2+1)*BLK)
            dq[hr,rows]+=jnp.dot(kt[hr,:],ds_sc[h//2,:,side],preferred_element_type=f32)

    def body(qb,carry):
        code=codes[qb,step]
        @pl.when(code==1)
        def _(): tile(qb,False)
        @pl.when(code==2)
        def _(): tile(qb,True)
        return carry
    lax.fori_loop(0,nqb,body,0)

    if last:
        gk=unrotate(dk[...]*scale,cosk_ref[...],sink_ref[...]).astype(bf16)
        gv=dv[...].astype(bf16)
        gk_ref[...]=gk
        gv_ref[...]=gv
        bsum_ref[1:2,:]+=jnp.sum(gk.astype(f32),axis=0,keepdims=True)
        bsum_ref[2:3,:]+=jnp.sum(gv.astype(f32),axis=0,keepdims=True)
    else:
        gk_ref[...]=dk[...]
        gv_ref[...]=dv[...]

    @pl.when(step==nkb-1)
    def _():
        def fin(blk,carry):
            rows=pl.ds(pl.multiple_of(blk*BLK,BLK),BLK)
            gq=unrotate(dq[:,rows].T*scale,cos_ref[rows,:],sin_ref[rows,:]).astype(bf16)
            gq_ref[rows,:]=gq
            bsum_ref[0:1,:]+=jnp.sum(gq.astype(f32),axis=0,keepdims=True)
            return carry
        lax.fori_loop(0,nqb,fin,0)

def attn_bwd(codes,q,k,v,do,o,lse,segq,segk,cos,sin,part,carried):
    rows,cols=k.shape
    half=do.shape[0]
    heads=cols//HDIM
    nb=rows//BLK
    last=carried is not None
    mine=lambda n: pl.BlockSpec((half,n),lambda i,c:(part,0))
    here=lambda n: pl.BlockSpec((half,n),lambda i,c:(0,0))
    blk=lambda n: pl.BlockSpec((BLK,n),lambda i,c:(i,0))
    kdtype=bf16 if last else f32
    return pl.pallas_call(
        partial(attn_bwd_kernel,last),
        out_shape=(jax.ShapeDtypeStruct((half,cols),bf16),jax.ShapeDtypeStruct((rows,cols),kdtype),
                   jax.ShapeDtypeStruct((rows,cols),kdtype),jax.ShapeDtypeStruct((8,cols),f32)),
        grid_spec=pltpu.PrefetchScalarGridSpec(num_scalar_prefetch=1,grid=(nb,),
            in_specs=[mine(cols),blk(cols),blk(cols),here(cols),here(cols),pl.BlockSpec((8,half),lambda i,c:(0,0)),
                      pl.BlockSpec((1,half),lambda i,c:(0,part)),blk(1),mine(128),mine(128),blk(128),blk(128)]
                     +([blk(cols),blk(cols)] if last else []),
            out_specs=[here(cols),blk(cols),blk(cols),pl.BlockSpec((8,cols),lambda i,c:(0,0))],
            scratch_shapes=[pltpu.VMEM((cols,BLK),bf16),pltpu.VMEM((heads,half,128),bf16),pltpu.VMEM((heads,half,128),bf16),
                            pltpu.VMEM((8,half),f32),pltpu.VMEM((cols,half),f32),pltpu.VMEM((BLK,cols),f32),pltpu.VMEM((BLK,cols),f32),
                            pltpu.VMEM((heads,BLK,BLK),f32),pltpu.VMEM((heads//2,BLK,2*BLK),bf16),pltpu.VMEM((heads//2,BLK,2*BLK),bf16)]),
        compiler_params=pltpu.CompilerParams(dimension_semantics=("arbitrary",)),
        name="attn_bwd",
        cost_estimate=work(45*half*rows*cols),
    )(codes,q,k,v,do,o,lse,segq,segk,cos,sin,cos,sin,*(carried or ()))

def block_codes(seg,pad_seg,skip_pad):
    sb=seg.reshape(-1,BLK)
    lo=jnp.min(sb,axis=1); hi=jnp.max(sb,axis=1)
    meet=(lo[:,None]<=hi[None,:])&(lo[None,:]<=hi[:,None])
    whole=(lo==hi)
    same=whole[:,None]&whole[None,:]&(lo[:,None]==lo[None,:])
    code=jnp.where(meet,jnp.where(same,1,2),0).astype(jnp.int32)
    if skip_pad:
        alive=lo<pad_seg
        code=jnp.where(alive[:,None]&alive[None,:],code,0)
    return code


def pick(i,n,a_ref,b_ref):
    return jnp.where(i<n,a_ref[...],b_ref[...])


def qkv_kernel(n, xa_ref, xb_ref, w_ref, b_ref, cos_ref, sin_ref, *rest):
    x=pick(pl.program_id(0),n,xa_ref,xb_ref)
    cos=cos_ref[...]; sin=sin_ref[...]
    for c,o_ref in enumerate(rest[-3:]):
        y=jnp.dot(x,w_ref[c],preferred_element_type=f32)+b_ref[c:c+1,:]
        if c<2:
            parts=[]
            for p in range(y.shape[1]//128):
                yp=y[:,p*128:(p+1)*128]
                parts.append(yp*cos+swap_halves(yp)*sin)
            y=jnp.concatenate(parts,axis=1)
        o_ref[...]=y.astype(bf16)


def two(tile,n,width):
    return [pl.BlockSpec((tile,width),lambda i:(jnp.minimum(i,n-1),0)),
            pl.BlockSpec((tile,width),lambda i:(jnp.maximum(i-n,0),0))]


def qkv_rows(xa,xb,w,b,cos,sin,part,full):
    rows,d=xa.shape
    cols=w.shape[2]
    tile=min(512,rows)
    n=rows//tile
    off=part*2*n
    row=lambda m: pl.BlockSpec((tile,m),lambda i:(i+off,0))
    kept=[] if full is None else list(full)
    return pl.pallas_call(
        partial(qkv_kernel,n),
        grid=(2*n,),
        out_shape=[jax.ShapeDtypeStruct((cos.shape[0],cols),bf16)]*3,
        in_specs=two(tile,n,d)+[pl.BlockSpec(w.shape,lambda i:(0,0,0)),pl.BlockSpec(b.shape,lambda i:(0,0)),
                  row(128),row(128)]+[pl.BlockSpec(memory_space=pl.ANY)]*len(kept),
        out_specs=[row(cols)]*3,
        input_output_aliases={6+i:i for i in range(len(kept))},
        compiler_params=pltpu.CompilerParams(dimension_semantics=("arbitrary",)),
        name="qkv",
        cost_estimate=work(20*rows*d*cols*2),
    )(xa,xb,w,b,cos,sin,*kept)


def mlp_kernel(n,xa_ref,xb_ref,ga_ref,gb_ref,w1_ref,b1_ref,w2_ref,*rest):
    hid_ref,gp_ref,na_ref,nb_ref,db_ref=rest[-5:]
    i=pl.program_id(0)
    @pl.when(i==0)
    def _():
        db_ref[...]=jnp.zeros(db_ref.shape,f32)
    pre=jnp.dot(pick(i,n,xa_ref,xb_ref),w1_ref[...],preferred_element_type=f32)+b1_ref[...]
    phi=0.5+0.5*lax.erf(pre*0.7071067811865476)
    hid_ref[...]=(pre*phi).astype(bf16)
    slope=phi+pre*(0.3989422804014327*jnp.exp2(pre*pre*(-0.5*LOG2E)))
    gh=lax.dot_general(pick(i,n,ga_ref,gb_ref),w2_ref[...],NT,preferred_element_type=f32)
    gp=(gh*slope).astype(bf16)
    gp_ref[...]=gp
    db_ref[...]+=jnp.sum(gp.astype(f32),axis=0,keepdims=True)
    gn=lax.dot_general(gp,w1_ref[...],NT,preferred_element_type=f32).astype(bf16)
    @pl.when(i<n)
    def _(): na_ref[...]=gn
    @pl.when(i>=n)
    def _(): nb_ref[...]=gn


def mlp_rows(xs,gs,w1,b1,w2,first,total,full):
    rows,d=xs[0].shape
    units=w1.shape[1]
    tile=min(256,rows)
    n=rows//tile
    off=first//tile
    row=lambda m: pl.BlockSpec((tile,m),lambda i:(i+off,0))
    whole=lambda a: pl.BlockSpec(a.shape,lambda i:(0,0))
    kept=[] if full is None else list(full)
    return pl.pallas_call(
        partial(mlp_kernel,n),
        grid=(2*n,),
        out_shape=[jax.ShapeDtypeStruct((total,units),bf16)]*2+[jax.ShapeDtypeStruct((rows,d),bf16)]*2+
                  [jax.ShapeDtypeStruct((1,units),f32)],
        in_specs=two(tile,n,d)+two(tile,n,d)+[whole(w1),whole(b1),whole(w2)]+[pl.BlockSpec(memory_space=pl.ANY)]*len(kept),
        out_specs=[row(units),row(units)]+two(tile,n,d)+[pl.BlockSpec((1,units),lambda i:(0,0))],
        input_output_aliases={7+i:i for i in range(len(kept))},
        compiler_params=pltpu.CompilerParams(dimension_semantics=("arbitrary",)),
        name="mlp",
        cost_estimate=work((2 if first else 40)*rows*d*units),
    )(*xs,*gs,w1,b1,w2,*kept)


def back_kernel(n,gq_ref,gk_ref,gv_ref,w_ref,oa_ref,ob_ref):
    i=pl.program_id(0)
    y=lax.dot_general(gq_ref[...],w_ref[0],NT,preferred_element_type=f32)
    y=y+lax.dot_general(gk_ref[...],w_ref[1],NT,preferred_element_type=f32)
    y=(y+lax.dot_general(gv_ref[...],w_ref[2],NT,preferred_element_type=f32)).astype(bf16)
    @pl.when(i<n)
    def _(): oa_ref[...]=y
    @pl.when(i>=n)
    def _(): ob_ref[...]=y


def back_rows(gq,gk,gv,w,part):
    half,cols=gq.shape
    rows=half//2
    d=w.shape[1]
    tile=min(512,rows)
    n=rows//tile
    off=part*2*n
    row=pl.BlockSpec((tile,cols),lambda i:(i+off,0))
    return pl.pallas_call(
        partial(back_kernel,n),
        grid=(2*n,),
        out_shape=[jax.ShapeDtypeStruct((rows,d),bf16)]*2,
        in_specs=[pl.BlockSpec((tile,cols),lambda i:(i,0)),row,row,pl.BlockSpec(w.shape,lambda i:(0,0,0))],
        out_specs=two(tile,n,d),
        compiler_params=pltpu.CompilerParams(dimension_semantics=("arbitrary",)),
        name="back",
        cost_estimate=work(1),
    )(gq,gk,gv,w)


def norm_rows(values_in, gain_row, shift_row):
    row_mean = jnp.mean(values_in, axis=-1, keepdims=True)
    centred = values_in - row_mean
    variance = jnp.mean(centred * centred, axis=-1, keepdims=True)
    return centred * lax.rsqrt(variance + 1e-06) * gain_row + shift_row


def flip(x,bits):
    n=lax.axis_size("tensor")
    return lax.ppermute(x,"tensor",[(i,i^bits) for i in range(n)])


def pair_sum(mine,other):
    return mine.astype(f32)+flip(other,1).astype(f32)


def dp_flip(x,bit):
    n=lax.axis_size("dp")
    return lax.ppermute(x,"dp",[(i,i^(1<<bit)) for i in range(n)])


class DpSum:
    def __init__(self,x,order):
        self.cur=x
        self.stages=[(bit,True) for bit in order]+[(bit,False) for bit in reversed(order)]
        self.at=0

    def operand(self):
        bit,halving=self.stages[self.at]
        if not halving: return self.cur
        up=(lax.axis_index("dp")>>bit)&1
        halves=self.cur.reshape(2,-1,self.cur.shape[1])
        self.kept=lax.dynamic_index_in_dim(halves,up,0,False)
        return lax.dynamic_index_in_dim(halves,1-up,0,False)

    def start(self,operand):
        self.sent=operand
        self.got=dp_flip(operand,self.stages[self.at][0])

    def finish(self,got):
        bit,halving=self.stages[self.at]
        self.at+=1
        if halving:
            self.cur=(self.kept.astype(f32)+got.astype(f32)).astype(bf16)
        else:
            up=((lax.axis_index("dp")>>bit)&1)==1
            self.cur=jnp.concatenate([jnp.where(up,got,self.sent),jnp.where(up,self.sent,got)],axis=0)

    def rest(self):
        while self.at<len(self.stages):
            self.start(self.operand())
            self.finish(self.got)
        return self.cur


def begin(sums,value):
    value,*sends=lax.optimization_barrier((value,*[s.operand() for s in sums]))
    for s,x in zip(sums,sends): s.start(x)
    return value


def settle(sums,value):
    value,*gots=lax.optimization_barrier((value,*[s.got for s in sums]))
    for s,x in zip(sums,gots): s.finish(x)
    return value


def all_sum(x):
    for bits in (1,2):
        x=x+flip(x,bits)
    for bit in range(lax.axis_size("dp").bit_length()-1):
        x=x+dp_flip(x,bit)
    return x


def after(x,*others):
    return lax.optimization_barrier((x,)+others)[0]


def shards(tokens,grad_out,lengths,coords,w_qkv,b_qkv,w_proj,w_fc1,b_fc1,w_fc2,norm_gains,shift_biases):
    tok=tokens.shape[0]
    ranks=lax.axis_size("tensor")
    bits=lax.axis_size("dp").bit_length()-1
    me=lax.axis_index("tensor")
    rows_all=tok*ranks
    half=rows_all//2
    cols=w_qkv.shape[2]
    ends=jnp.cumsum(lengths[0])
    slots=lengths.shape[1]
    rel=jnp.arange(rows_all,dtype=jnp.int32)
    place=((rel//tok)^me)*tok+rel%tok
    seg=jnp.sum((place[:,None]>=ends[None,:]).astype(jnp.int32),axis=1)
    live=(place[:tok]<ends[-1]).astype(f32)[:,None]
    cgrp=jnp.concatenate([lax.dynamic_slice_in_dim(coords,(me^j)*tok,tok,1) for j in range(ranks)],axis=1).astype(f32)
    lane=jnp.arange(128,dtype=jnp.int32)
    pair=lane%(HDIM//2)
    freq=100.0**(-(pair//3).astype(f32)/(HDIM//2//3+1))
    angle=jnp.zeros((rows_all,128),f32)
    for a in range(3):
        angle=angle+cgrp[a][:,None]*jnp.where(pair%3==a,freq,0.0)[None,:]
    cos=jnp.cos(angle)
    sin=jnp.sin(angle)*jnp.where(lane%HDIM<HDIM//2,-1.0,1.0)[None,:]
    gains=norm_gains.astype(f32)
    shifts=shift_biases.astype(f32)
    x_rows=tokens.astype(f32)

    normed_one,norm_one_back=jax.vjp(norm_rows,x_rows,gains[0],shifts[0])
    low_one=normed_one.astype(bf16)
    far=flip(low_one,2)
    near=flip(low_one,1)
    grad_y=grad_out.astype(f32)*live
    grad_mlp=grad_y.astype(bf16)

    bq=b_qkv.astype(f32)
    qkv=qkv_rows(low_one,near,w_qkv,bq,cos,sin,0,None)
    far,*qkv=lax.optimization_barrier((far,*qkv))
    far_pair=flip(far,1)
    q,k,v=qkv_rows(far,far_pair,w_qkv,bq,cos,sin,1,qkv)
    n1=[low_one,near,far,far_pair]
    late=after(grad_mlp,far)
    gm=[late,flip(late,1),flip(late,2)]
    segq=seg[None,:]; segk=seg[:,None]
    hb=half//BLK
    codes=block_codes(seg,slots,False)
    att_far,lse_far=attn_fwd(codes[hb:],q,k,v,segq,segk,hb,hb)
    att_far,g2=lax.optimization_barrier((att_far,gm[2]))
    proj=lambda a: jnp.dot(a,w_proj,preferred_element_type=f32).astype(bf16)
    across=pair_sum(proj(att_far[tok:]),proj(att_far[:tok])).astype(bf16)
    q_late,across=lax.optimization_barrier((q,across))
    gm=[gm[0],gm[1],g2,flip(g2,1)]
    across=flip(across,3)
    att_near,lse_near=attn_fwd(codes[:hb],q_late,k,v,segq,segk,0,hb)
    across,att_near=lax.optimization_barrier((across,att_near))
    mine=pair_sum(proj(att_near[:tok]),proj(att_near[tok:]))
    resid_one=x_rows+mine+across.astype(f32)+shifts[2]
    normed_two,norm_two_back=jax.vjp(norm_rows,resid_one,gains[1],shifts[1])
    low_two=normed_two.astype(bf16)
    piece=tok//2
    far=[flip(low_two[:piece],2),flip(low_two[piece:],2)]
    near=flip(low_two,1)
    b1=b_fc1.astype(f32)[None,:]
    hid,gp,gn0,gn1,db=mlp_rows((low_two,near),(gm[0],gm[1]),w_fc1,b1,w_fc2,0,rows_all,None)
    ordered=[low_two,near]
    gorder=[gm[0],gm[1]]
    across=[]
    for c in range(2):
        f,hid,gp,*ordered=lax.optimization_barrier((far[c],hid,gp,*ordered))
        if across:
            hid,gp,sent=lax.optimization_barrier((hid,gp,across[0]))
            across=[flip(sent,3)]
        pair=(f,flip(f,1))
        gpair=tuple(g[c*piece:(c+1)*piece] for g in (gm[2],gm[3]))
        ordered+=pair
        gorder+=gpair
        hid,gp,gn2,gn3,db_c=mlp_rows(pair,gpair,w_fc1,b1,w_fc2,half+c*tok,rows_all,(hid,gp))
        db=db+db_c
        across.append(pair_sum(gn3,gn2).astype(bf16))
    hid,gp,last,*gorder=lax.optimization_barrier((hid,gp,across[1],*gorder))
    across=jnp.concatenate([across[0],flip(last,3)],axis=0)
    mine=pair_sum(gn0,gn1)
    tn=lambda a,b: lax.dot_general(a,b,(((0,),(0,)),((),())),preferred_element_type=f32)
    grad_w1=tn(jnp.concatenate(ordered,axis=0),gp).astype(bf16)
    grad_w2=tn(hid,jnp.concatenate(gorder,axis=0)).astype(bf16)
    both=jnp.concatenate([grad_w1,grad_w2],axis=0)
    across=after(across,both)
    wsum=lax.psum_scatter(both,"dp",scatter_dimension=0,tiled=True)
    grad_resid_two,grad_gain_two,grad_shift_two=norm_two_back(mine+across.astype(f32))

    grad_resid_one=grad_y+grad_resid_two
    grad_attn=grad_resid_one.astype(bf16)
    far=flip(grad_attn,2)
    near=flip(grad_attn,1)
    ghead=lambda a: lax.dot_general(a,w_proj,NT,preferred_element_type=f32).astype(bf16)
    bcodes=block_codes(seg,slots,True)
    do_near=jnp.concatenate([ghead(grad_attn),ghead(near)],axis=0)
    gq_near,dk,dv,bs0=attn_bwd(bcodes[:hb],q,k,v,do_near,att_near,lse_near,segq,segk,cos,sin,0,None)
    early=jnp.stack([grad_gain_two,grad_shift_two,jnp.sum(grad_attn,axis=0,dtype=f32),jnp.sum(grad_mlp,axis=0,dtype=f32)])
    far,dk,dv,early=lax.optimization_barrier((far,dk,dv,early))
    far_pair=flip(far,1)
    do_far=jnp.concatenate([ghead(far),ghead(far_pair)],axis=0)
    alla=jnp.concatenate([grad_attn,near,far,far_pair],axis=0)
    grad_proj=tn(jnp.concatenate([att_near,att_far],axis=0),alla).astype(bf16)
    do_far,grad_proj=lax.optimization_barrier((do_far,grad_proj))
    gq_far,gk,gv,bs1=attn_bwd(bcodes[hb:],q,k,v,do_far,att_far,lse_far,segq,segk,cos,sin,1,(dk,dv))
    gk,wsum=lax.optimization_barrier((gk,wsum))
    wsum=lax.all_gather(wsum,"dp",axis=0,tiled=True)
    r2,r3=back_rows(gq_far,gk,gv,w_qkv,1)
    across=pair_sum(r3,r2).astype(bf16)
    gq_near,gk,gv,across=lax.optimization_barrier((gq_near,gk,gv,across))
    across=flip(across,3)
    g_all=jnp.concatenate([jnp.concatenate([gq_near,gq_far],axis=0),gk,gv],axis=1)
    grad_wqkv=tn(jnp.concatenate(n1,axis=0),g_all).astype(bf16)
    grad_wqkv,hid,gq_near=lax.optimization_barrier((grad_wqkv,hid,gq_near))
    d=tokens.shape[1]
    sizes=(3*cols,db.shape[1])
    pad=(-sum(sizes))%(8*cols<<bits)
    small=jnp.concatenate([(bs0+bs1)[:3].reshape(-1),db[0],jnp.zeros((pad,),f32)]).astype(bf16).reshape(-1,cols)
    tail_a=DpSum(jnp.concatenate([grad_wqkv[:,:cols],grad_wqkv[:,cols:2*cols]],axis=0),tuple(range(bits)))
    tail_b=DpSum(jnp.concatenate([grad_wqkv[:,2*cols:],grad_proj.reshape(-1,cols),small],axis=0),(1,0)+tuple(range(2,bits)))
    tails=(tail_a,tail_b)
    for t in tails: t.start(t.operand())
    *gots,across=lax.optimization_barrier((tail_a.got,tail_b.got,across))
    for t,got in zip(tails,gots): t.finish(got)
    r0,r1=back_rows(gq_near,gk,gv,w_qkv,0)
    mine=pair_sum(r0,r1)
    grad_x_norm,grad_gain_one,grad_shift_one=norm_one_back(mine+across.astype(f32))
    one=jnp.concatenate([jnp.stack([grad_gain_one,grad_shift_one]),early],axis=0)
    o=jnp.dot(hid,w_fc2,preferred_element_type=f32).astype(bf16)
    fars=o[half:].reshape(2,2,piece,d)
    o=[o[:tok],o[tok:half],fars[:,0].reshape(tok,d),fars[:,1].reshape(tok,d)]
    o_across=flip(pair_sum(o[3],o[2]).astype(bf16),3)
    for t in tails: t.start(t.operand())
    one,*gots=lax.optimization_barrier((one,tail_a.got,tail_b.got))
    for t,got in zip(tails,gots): t.finish(got)
    hops=[partial(dp_flip,bit=bit) for bit in range(bits)]+[partial(flip,bits=1),partial(flip,bits=2)]
    while hops or tail_a.at<len(tail_a.stages):
        busy=[t for t in tails if t.at<len(t.stages)]
        for t in busy: t.start(t.operand())
        hop=hops.pop(0) if hops else None
        other=hop(one) if hop else one
        third=bool(busy) and busy[0].at==bits-1
        gots=[t.got for t in busy]
        if third:
            other,o_across,wsum,*gots=lax.optimization_barrier((other,o_across,wsum,*gots))
        else:
            other,*gots=lax.optimization_barrier((other,*gots))
        for t,got in zip(busy,gots): t.finish(got)
        one=one+other if hop else one
    tail_a,tail_b=tail_a.cur,tail_b.cur
    output=(resid_one+pair_sum(o[0],o[1])+o_across.astype(f32)+shifts[3]).astype(bf16)
    grad_w1,grad_w2=wsum[:d],wsum[d:]
    grad_wqkv=jnp.stack([tail_a[:d],tail_a[d:],tail_b[:d]]).astype(f32)
    grad_wproj=tail_b[d:2*d].reshape(cols,d).astype(f32)
    small=tail_b[2*d:].reshape(-1).astype(f32)
    grad_bqkv=small[:sizes[0]].reshape(3,cols)
    grad_b1=small[sizes[0]:sizes[0]+sizes[1]]
    grad_tokens=(grad_resid_one+grad_x_norm).astype(bf16)
    return (output,grad_tokens,grad_wqkv,grad_bqkv,grad_wproj,grad_w1.astype(f32),grad_b1,grad_w2.astype(f32),
            jnp.stack([one[0],one[2]]),jnp.stack([one[1],one[3],one[4],one[5]]))


def solution(mesh):
    rows=P(("dp","tensor"),None)
    return jax.shard_map(shards,mesh=mesh,
        in_specs=(rows,rows,P("dp",None),P(None,"dp"),P(None,None,"tensor"),P(None,"tensor"),P("tensor",None),
                  P(None,"tensor"),P("tensor"),P("tensor",None),P(),P()),
        out_specs=(rows,rows,P(None,None,"tensor"),P(None,"tensor"),P("tensor",None),P(None,"tensor"),P("tensor"),
                   P("tensor",None),P(),P()),
        check_vma=False)
```

```python
from functools import partial

import jax
import jax.numpy as jnp
from jax import lax
from jax.experimental import pallas as pl
from jax.experimental.pallas import tpu as pltpu
from jax.sharding import PartitionSpec as P

HDIM=64
LOG2E=1.4426950408889634
LN2=0.6931471805599453
f32=jnp.float32; bf16=jnp.bfloat16
BLK=256
VROWS=80
NT=(((1,),(1,)),((),()))

def work(flops):
    return pl.CostEstimate(flops=flops,bytes_accessed=0,transcendentals=0)

def lane_half(shape, which):
    lane=lax.broadcasted_iota(jnp.int32, shape, 1)
    return (lane//HDIM)%2==which

def attn_fwd_kernel(codes, q_ref, k_ref, v_ref, segq_ref, segk_ref, o_ref, lse_ref, vt, qm, m_sc, acc, s_sc):
    step=pl.program_id(0)
    nkb=k_ref.shape[0]//BLK
    heads=q_ref.shape[1]//HDIM
    @pl.when(step==0)
    def _():
        for blk in range(nkb):
            rows=pl.ds(blk*BLK,BLK)
            vT=v_ref[rows,:].T
            for h in range(heads):
                vt[h*VROWS:h*VROWS+HDIM, rows]=vT[h*HDIM:(h+1)*HDIM,:]
        for h in range(heads):
            vt[h*VROWS+HDIM:(h+1)*VROWS,:]=jnp.ones((VROWS-HDIM,vt.shape[1]),bf16)
    for p in range(heads//2):
        qp=q_ref[:,p*128:(p+1)*128]
        for w in range(2):
            qm[2*p+w]=jnp.where(lane_half(qp.shape,w),qp,jnp.zeros_like(qp))
    m_sc[...]=jnp.full(m_sc.shape,-1e30,f32)
    acc[...]=jnp.zeros(acc.shape,f32)
    scale=HDIM**-0.5*LOG2E

    def tile(kb,masked):
        rows=pl.ds(pl.multiple_of(kb*BLK,BLK),BLK)
        if masked:
            allowed=segk_ref[rows,:][:,0:1]==segq_ref[0:1,:]
        tops=[]
        for h in range(heads):
            p=h//2
            s=lax.dot_general(k_ref[rows,p*128:(p+1)*128],qm[h],NT,preferred_element_type=f32)*scale
            if masked: s=jnp.where(allowed,s,-1e30)
            s_sc[h]=s
            tops.append(jnp.max(s,axis=0,keepdims=True))
        m_prev=m_sc[0:heads,:]
        m_new=jnp.maximum(m_prev,jnp.concatenate(tops,axis=0))
        alpha=jnp.exp2(m_prev-m_new)
        m_sc[0:heads,:]=m_new
        for h in range(heads):
            prob=jnp.exp2(s_sc[h]-m_new[h:h+1,:]).astype(bf16)
            arows=slice(h*VROWS,(h+1)*VROWS)
            acc[arows,:]=acc[arows,:]*alpha[h:h+1,:]+jnp.dot(vt[arows,rows],prob,preferred_element_type=f32)

    def body(kb,carry):
        code=codes[step,kb]
        @pl.when(code==1)
        def _(): tile(kb,False)
        @pl.when(code==2)
        def _(): tile(kb,True)
        return carry
    lax.fori_loop(0,nkb,body,0)
    outs=[]
    for h in range(heads):
        total=acc[h*VROWS+HDIM:h*VROWS+HDIM+1,:]
        outs.append(acc[h*VROWS:h*VROWS+HDIM,:]/total)
        lse_ref[h:h+1,:]=m_sc[h:h+1,:]+jnp.log2(total)
    for h in range(heads,8):
        lse_ref[h:h+1,:]=jnp.zeros((1,BLK),f32)
    o_ref[...]=jnp.concatenate(outs,axis=0).T.astype(bf16)

def attn_fwd(codes,q,k,v,segq,segk,block0,nblocks):
    rows,cols=k.shape
    heads=cols//HDIM
    full=lambda i,c:(0,0)
    return pl.pallas_call(
        attn_fwd_kernel,
        out_shape=(jax.ShapeDtypeStruct((nblocks*BLK,cols),bf16),jax.ShapeDtypeStruct((8,nblocks*BLK),f32)),
        grid_spec=pltpu.PrefetchScalarGridSpec(num_scalar_prefetch=1,grid=(nblocks,),
            in_specs=[pl.BlockSpec((BLK,cols),lambda i,c:(i+block0,0)),
                      pl.BlockSpec((rows,cols),full),pl.BlockSpec((rows,cols),full),
                      pl.BlockSpec((1,BLK),lambda i,c:(0,i+block0)),
                      pl.BlockSpec((rows,1),full)],
            out_specs=[pl.BlockSpec((BLK,cols),lambda i,c:(i,0)),pl.BlockSpec((8,BLK),lambda i,c:(0,i))],
            scratch_shapes=[pltpu.VMEM((heads*VROWS,rows),bf16),pltpu.VMEM((heads,BLK,128),bf16),
                            pltpu.VMEM((8,BLK),f32),pltpu.VMEM((heads*VROWS,BLK),f32),pltpu.VMEM((heads,BLK,BLK),f32)]),
        compiler_params=pltpu.CompilerParams(dimension_semantics=("arbitrary",)),
        name="attn_fwd",
        cost_estimate=work((4 if block0 else 64)*nblocks*BLK*rows*cols),
    )(codes,q,k,v,segq,segk)

def swap_halves(x):
    n=x.shape[1]
    lane=lax.broadcasted_iota(jnp.int32,x.shape,1)
    up=pltpu.roll(x,n-HDIM//2,1)
    down=pltpu.roll(x,HDIM//2,1)
    return jnp.where(lane%HDIM<HDIM//2,up,down)

def attn_bwd_kernel(last, codes, q_ref,k_ref,v_ref,do_ref,o_ref,lse_ref,segq_ref,segk_ref,cos_ref,sin_ref,cosk_ref,sink_ref,*rest):
    if last:
        dk0_ref,dv0_ref,gq_ref,gk_ref,gv_ref,bsum_ref,kt,qm,dom,delta,dq,dk,dv,p_sc,low_sc,ds_sc=rest
    else:
        gq_ref,gk_ref,gv_ref,bsum_ref,kt,qm,dom,delta,dq,dk,dv,p_sc,low_sc,ds_sc=rest
    step=pl.program_id(0)
    nkb=pl.num_programs(0)
    nqb=q_ref.shape[0]//BLK
    heads=q_ref.shape[1]//HDIM
    scale=HDIM**-0.5
    def unrotate(x,cos,sin):
        out=[]
        for p in range(heads//2):
            xp=x[:,p*128:(p+1)*128]
            out.append(xp*cos-swap_halves(xp)*sin)
        return jnp.concatenate(out,axis=1)
    @pl.when(step==0)
    def _():
        def prep(blk,carry):
            rows=pl.ds(pl.multiple_of(blk*BLK,BLK),BLK)
            for p in range(heads//2):
                lanes=slice(p*128,(p+1)*128)
                qp=q_ref[rows,lanes]; dp=do_ref[rows,lanes]
                for w in range(2):
                    sel=lane_half(qp.shape,w)
                    qm[2*p+w,rows,:]=jnp.where(sel,qp,jnp.zeros_like(qp))
                    dom[2*p+w,rows,:]=jnp.where(sel,dp,jnp.zeros_like(dp))
            prod=(do_ref[rows,:].astype(f32)*o_ref[rows,:].astype(f32)).T
            for h in range(heads):
                delta[h:h+1,rows]=jnp.sum(prod[h*HDIM:(h+1)*HDIM,:],axis=0,keepdims=True)
            return carry
        lax.fori_loop(0,nqb,prep,0)
        dq[...]=jnp.zeros(dq.shape,f32)
        bsum_ref[...]=jnp.zeros(bsum_ref.shape,f32)
    kt[...]=k_ref[...].T
    if last:
        dk[...]=dk0_ref[...]
        dv[...]=dv0_ref[...]
    else:
        dk[...]=jnp.zeros(dk.shape,f32)
        dv[...]=jnp.zeros(dv.shape,f32)

    def tile(qb,masked):
        rows=pl.ds(pl.multiple_of(qb*BLK,BLK),BLK)
        if masked:
            allowed=segk_ref[:,0:1]==segq_ref[0:1,rows]
        for h in range(heads):
            lanes=slice(h//2*128,(h//2+1)*128)
            s=lax.dot_general(k_ref[:,lanes],qm[h,rows,:],NT,preferred_element_type=f32)*(scale*LOG2E)
            prob=jnp.exp2(s-lse_ref[h:h+1,rows])
            if masked: prob=jnp.where(allowed,prob,0.0)
            p_sc[h]=prob
        for h in range(heads):
            lanes=slice(h//2*128,(h//2+1)*128)
            side=slice(h%2*BLK,(h%2+1)*BLK)
            dp=lax.dot_general(v_ref[:,lanes],dom[h,rows,:],NT,preferred_element_type=f32)
            prob=p_sc[h]
            low_sc[h//2,:,side]=prob.astype(bf16)
            ds_sc[h//2,:,side]=(prob*(dp-delta[h:h+1,rows])).astype(bf16)
        for p in range(heads//2):
            lanes=slice(p*128,(p+1)*128)
            pair=slice(2*p,2*p+2)
            dv[:,lanes]+=jnp.dot(low_sc[p],dom[pair,rows,:].reshape(2*BLK,128),preferred_element_type=f32)
            dk[:,lanes]+=jnp.dot(ds_sc[p],qm[pair,rows,:].reshape(2*BLK,128),preferred_element_type=f32)
        for h in range(heads):
            hr=slice(h*HDIM,(h+1)*HDIM)
            side=slice(h%2*BLK,(h%2+1)*BLK)
            dq[hr,rows]+=jnp.dot(kt[hr,:],ds_sc[h//2,:,side],preferred_element_type=f32)

    def body(qb,carry):
        code=codes[qb,step]
        @pl.when(code==1)
        def _(): tile(qb,False)
        @pl.when(code==2)
        def _(): tile(qb,True)
        return carry
    lax.fori_loop(0,nqb,body,0)

    if last:
        gk=unrotate(dk[...]*scale,cosk_ref[...],sink_ref[...]).astype(bf16)
        gv=dv[...].astype(bf16)
        gk_ref[...]=gk
        gv_ref[...]=gv
        bsum_ref[1:2,:]+=jnp.sum(gk.astype(f32),axis=0,keepdims=True)
        bsum_ref[2:3,:]+=jnp.sum(gv.astype(f32),axis=0,keepdims=True)
    else:
        gk_ref[...]=dk[...]
        gv_ref[...]=dv[...]

    @pl.when(step==nkb-1)
    def _():
        def fin(blk,carry):
            rows=pl.ds(pl.multiple_of(blk*BLK,BLK),BLK)
            gq=unrotate(dq[:,rows].T*scale,cos_ref[rows,:],sin_ref[rows,:]).astype(bf16)
            gq_ref[rows,:]=gq
            bsum_ref[0:1,:]+=jnp.sum(gq.astype(f32),axis=0,keepdims=True)
            return carry
        lax.fori_loop(0,nqb,fin,0)

def attn_bwd(codes,q,k,v,do,o,lse,segq,segk,cos,sin,part,carried):
    rows,cols=k.shape
    half=do.shape[0]
    heads=cols//HDIM
    nb=rows//BLK
    last=carried is not None
    mine=lambda n: pl.BlockSpec((half,n),lambda i,c:(part,0))
    here=lambda n: pl.BlockSpec((half,n),lambda i,c:(0,0))
    blk=lambda n: pl.BlockSpec((BLK,n),lambda i,c:(i,0))
    kdtype=bf16 if last else f32
    return pl.pallas_call(
        partial(attn_bwd_kernel,last),
        out_shape=(jax.ShapeDtypeStruct((half,cols),bf16),jax.ShapeDtypeStruct((rows,cols),kdtype),
                   jax.ShapeDtypeStruct((rows,cols),kdtype),jax.ShapeDtypeStruct((8,cols),f32)),
        grid_spec=pltpu.PrefetchScalarGridSpec(num_scalar_prefetch=1,grid=(nb,),
            in_specs=[mine(cols),blk(cols),blk(cols),here(cols),here(cols),pl.BlockSpec((8,half),lambda i,c:(0,0)),
                      pl.BlockSpec((1,half),lambda i,c:(0,part)),blk(1),mine(128),mine(128),blk(128),blk(128)]
                     +([blk(cols),blk(cols)] if last else []),
            out_specs=[here(cols),blk(cols),blk(cols),pl.BlockSpec((8,cols),lambda i,c:(0,0))],
            scratch_shapes=[pltpu.VMEM((cols,BLK),bf16),pltpu.VMEM((heads,half,128),bf16),pltpu.VMEM((heads,half,128),bf16),
                            pltpu.VMEM((8,half),f32),pltpu.VMEM((cols,half),f32),pltpu.VMEM((BLK,cols),f32),pltpu.VMEM((BLK,cols),f32),
                            pltpu.VMEM((heads,BLK,BLK),f32),pltpu.VMEM((heads//2,BLK,2*BLK),bf16),pltpu.VMEM((heads//2,BLK,2*BLK),bf16)]),
        compiler_params=pltpu.CompilerParams(dimension_semantics=("arbitrary",)),
        name="attn_bwd",
        cost_estimate=work(45*half*rows*cols),
    )(codes,q,k,v,do,o,lse,segq,segk,cos,sin,cos,sin,*(carried or ()))

def block_codes(seg,pad_seg,skip_pad):
    sb=seg.reshape(-1,BLK)
    lo=jnp.min(sb,axis=1); hi=jnp.max(sb,axis=1)
    meet=(lo[:,None]<=hi[None,:])&(lo[None,:]<=hi[:,None])
    whole=(lo==hi)
    same=whole[:,None]&whole[None,:]&(lo[:,None]==lo[None,:])
    code=jnp.where(meet,jnp.where(same,1,2),0).astype(jnp.int32)
    if skip_pad:
        alive=lo<pad_seg
        code=jnp.where(alive[:,None]&alive[None,:],code,0)
    return code


def pick(i,n,a_ref,b_ref):
    return jnp.where(i<n,a_ref[...],b_ref[...])


def qkv_kernel(n, xa_ref, xb_ref, w_ref, b_ref, cos_ref, sin_ref, *rest):
    x=pick(pl.program_id(0),n,xa_ref,xb_ref)
    cos=cos_ref[...]; sin=sin_ref[...]
    for c,o_ref in enumerate(rest[-3:]):
        y=jnp.dot(x,w_ref[c],preferred_element_type=f32)+b_ref[c:c+1,:]
        if c<2:
            parts=[]
            for p in range(y.shape[1]//128):
                yp=y[:,p*128:(p+1)*128]
                parts.append(yp*cos+swap_halves(yp)*sin)
            y=jnp.concatenate(parts,axis=1)
        o_ref[...]=y.astype(bf16)


def two(tile,n,width):
    return [pl.BlockSpec((tile,width),lambda i:(jnp.minimum(i,n-1),0)),
            pl.BlockSpec((tile,width),lambda i:(jnp.maximum(i-n,0),0))]


def qkv_rows(xa,xb,w,b,cos,sin,part,full):
    rows,d=xa.shape
    cols=w.shape[2]
    tile=min(512,rows)
    n=rows//tile
    off=part*2*n
    row=lambda m: pl.BlockSpec((tile,m),lambda i:(i+off,0))
    kept=[] if full is None else list(full)
    return pl.pallas_call(
        partial(qkv_kernel,n),
        grid=(2*n,),
        out_shape=[jax.ShapeDtypeStruct((cos.shape[0],cols),bf16)]*3,
        in_specs=two(tile,n,d)+[pl.BlockSpec(w.shape,lambda i:(0,0,0)),pl.BlockSpec(b.shape,lambda i:(0,0)),
                  row(128),row(128)]+[pl.BlockSpec(memory_space=pl.ANY)]*len(kept),
        out_specs=[row(cols)]*3,
        input_output_aliases={6+i:i for i in range(len(kept))},
        compiler_params=pltpu.CompilerParams(dimension_semantics=("arbitrary",)),
        name="qkv",
        cost_estimate=work(20*rows*d*cols*2),
    )(xa,xb,w,b,cos,sin,*kept)


def mlp_kernel(n,xa_ref,xb_ref,ga_ref,gb_ref,w1_ref,b1_ref,w2_ref,*rest):
    hid_ref,gp_ref,na_ref,nb_ref,db_ref=rest[-5:]
    i=pl.program_id(0)
    @pl.when(i==0)
    def _():
        db_ref[...]=jnp.zeros(db_ref.shape,f32)
    pre=jnp.dot(pick(i,n,xa_ref,xb_ref),w1_ref[...],preferred_element_type=f32)+b1_ref[...]
    phi=0.5+0.5*lax.erf(pre*0.7071067811865476)
    hid_ref[...]=(pre*phi).astype(bf16)
    slope=phi+pre*(0.3989422804014327*jnp.exp2(pre*pre*(-0.5*LOG2E)))
    gh=lax.dot_general(pick(i,n,ga_ref,gb_ref),w2_ref[...],NT,preferred_element_type=f32)
    gp=(gh*slope).astype(bf16)
    gp_ref[...]=gp
    db_ref[...]+=jnp.sum(gp.astype(f32),axis=0,keepdims=True)
    gn=lax.dot_general(gp,w1_ref[...],NT,preferred_element_type=f32).astype(bf16)
    @pl.when(i<n)
    def _(): na_ref[...]=gn
    @pl.when(i>=n)
    def _(): nb_ref[...]=gn


def mlp_rows(xs,gs,w1,b1,w2,part,full):
    rows,d=xs[0].shape
    units=w1.shape[1]
    tile=min(256,rows)
    n=rows//tile
    off=part*2*n
    row=lambda m: pl.BlockSpec((tile,m),lambda i:(i+off,0))
    whole=lambda a: pl.BlockSpec(a.shape,lambda i:(0,0))
    kept=[] if full is None else list(full)
    return pl.pallas_call(
        partial(mlp_kernel,n),
        grid=(2*n,),
        out_shape=[jax.ShapeDtypeStruct((rows*4,units),bf16)]*2+[jax.ShapeDtypeStruct((rows,d),bf16)]*2+
                  [jax.ShapeDtypeStruct((1,units),f32)],
        in_specs=two(tile,n,d)+two(tile,n,d)+[whole(w1),whole(b1),whole(w2)]+[pl.BlockSpec(memory_space=pl.ANY)]*len(kept),
        out_specs=[row(units),row(units)]+two(tile,n,d)+[pl.BlockSpec((1,units),lambda i:(0,0))],
        input_output_aliases={7+i:i for i in range(len(kept))},
        compiler_params=pltpu.CompilerParams(dimension_semantics=("arbitrary",)),
        name="mlp",
        cost_estimate=work(12*rows*d*units),
    )(*xs,*gs,w1,b1,w2,*kept)


def back_kernel(n,gq_ref,gk_ref,gv_ref,w_ref,oa_ref,ob_ref):
    i=pl.program_id(0)
    y=lax.dot_general(gq_ref[...],w_ref[0],NT,preferred_element_type=f32)
    y=y+lax.dot_general(gk_ref[...],w_ref[1],NT,preferred_element_type=f32)
    y=(y+lax.dot_general(gv_ref[...],w_ref[2],NT,preferred_element_type=f32)).astype(bf16)
    @pl.when(i<n)
    def _(): oa_ref[...]=y
    @pl.when(i>=n)
    def _(): ob_ref[...]=y


def back_rows(gq,gk,gv,w,part):
    half,cols=gq.shape
    rows=half//2
    d=w.shape[1]
    tile=min(512,rows)
    n=rows//tile
    off=part*2*n
    row=pl.BlockSpec((tile,cols),lambda i:(i+off,0))
    return pl.pallas_call(
        partial(back_kernel,n),
        grid=(2*n,),
        out_shape=[jax.ShapeDtypeStruct((rows,d),bf16)]*2,
        in_specs=[pl.BlockSpec((tile,cols),lambda i:(i,0)),row,row,pl.BlockSpec(w.shape,lambda i:(0,0,0))],
        out_specs=two(tile,n,d),
        compiler_params=pltpu.CompilerParams(dimension_semantics=("arbitrary",)),
        name="back",
        cost_estimate=work(1),
    )(gq,gk,gv,w)


def norm_rows(values_in, gain_row, shift_row):
    row_mean = jnp.mean(values_in, axis=-1, keepdims=True)
    centred = values_in - row_mean
    variance = jnp.mean(centred * centred, axis=-1, keepdims=True)
    return centred * lax.rsqrt(variance + 1e-06) * gain_row + shift_row


def flip(x,bits):
    n=lax.axis_size("tensor")
    return lax.ppermute(x,"tensor",[(i,i^bits) for i in range(n)])


def pair_sum(mine,other):
    return mine.astype(f32)+flip(other,1).astype(f32)


def dp_flip(x,bit):
    n=lax.axis_size("dp")
    return lax.ppermute(x,"dp",[(i,i^(1<<bit)) for i in range(n)])


class DpSum:
    def __init__(self,x,order):
        self.cur=x
        self.stages=[(bit,True) for bit in order]+[(bit,False) for bit in reversed(order)]
        self.at=0

    def operand(self):
        bit,halving=self.stages[self.at]
        if not halving: return self.cur
        up=(lax.axis_index("dp")>>bit)&1
        halves=self.cur.reshape(2,-1,self.cur.shape[1])
        self.kept=lax.dynamic_index_in_dim(halves,up,0,False)
        return lax.dynamic_index_in_dim(halves,1-up,0,False)

    def start(self,operand):
        self.sent=operand
        self.got=dp_flip(operand,self.stages[self.at][0])

    def finish(self,got):
        bit,halving=self.stages[self.at]
        self.at+=1
        if halving:
            self.cur=(self.kept.astype(f32)+got.astype(f32)).astype(bf16)
        else:
            up=((lax.axis_index("dp")>>bit)&1)==1
            self.cur=jnp.concatenate([jnp.where(up,got,self.sent),jnp.where(up,self.sent,got)],axis=0)

    def rest(self):
        while self.at<len(self.stages):
            self.start(self.operand())
            self.finish(self.got)
        return self.cur


def begin(sums,value):
    value,*sends=lax.optimization_barrier((value,*[s.operand() for s in sums]))
    for s,x in zip(sums,sends): s.start(x)
    return value


def settle(sums,value):
    value,*gots=lax.optimization_barrier((value,*[s.got for s in sums]))
    for s,x in zip(sums,gots): s.finish(x)
    return value


def all_sum(x):
    for bits in (1,2):
        x=x+flip(x,bits)
    for bit in range(lax.axis_size("dp").bit_length()-1):
        x=x+dp_flip(x,bit)
    return x


def after(x,*others):
    return lax.optimization_barrier((x,)+others)[0]


def shards(tokens,grad_out,lengths,coords,w_qkv,b_qkv,w_proj,w_fc1,b_fc1,w_fc2,norm_gains,shift_biases):
    tok=tokens.shape[0]
    ranks=lax.axis_size("tensor")
    bits=lax.axis_size("dp").bit_length()-1
    me=lax.axis_index("tensor")
    rows_all=tok*ranks
    half=rows_all//2
    cols=w_qkv.shape[2]
    ends=jnp.cumsum(lengths[0])
    slots=lengths.shape[1]
    rel=jnp.arange(rows_all,dtype=jnp.int32)
    place=((rel//tok)^me)*tok+rel%tok
    seg=jnp.sum((place[:,None]>=ends[None,:]).astype(jnp.int32),axis=1)
    live=(place[:tok]<ends[-1]).astype(f32)[:,None]
    cgrp=jnp.concatenate([lax.dynamic_slice_in_dim(coords,(me^j)*tok,tok,1) for j in range(ranks)],axis=1).astype(f32)
    lane=jnp.arange(128,dtype=jnp.int32)
    pair=lane%(HDIM//2)
    freq=100.0**(-(pair//3).astype(f32)/(HDIM//2//3+1))
    angle=jnp.zeros((rows_all,128),f32)
    for a in range(3):
        angle=angle+cgrp[a][:,None]*jnp.where(pair%3==a,freq,0.0)[None,:]
    cos=jnp.cos(angle)
    sin=jnp.sin(angle)*jnp.where(lane%HDIM<HDIM//2,-1.0,1.0)[None,:]
    gains=norm_gains.astype(f32)
    shifts=shift_biases.astype(f32)
    x_rows=tokens.astype(f32)

    normed_one,norm_one_back=jax.vjp(norm_rows,x_rows,gains[0],shifts[0])
    low_one=normed_one.astype(bf16)
    far=flip(low_one,2)
    near=flip(low_one,1)
    grad_y=grad_out.astype(f32)*live
    grad_mlp=grad_y.astype(bf16)

    bq=b_qkv.astype(f32)
    qkv=qkv_rows(low_one,near,w_qkv,bq,cos,sin,0,None)
    far,*qkv=lax.optimization_barrier((far,*qkv))
    far_pair=flip(far,1)
    q,k,v=qkv_rows(far,far_pair,w_qkv,bq,cos,sin,1,qkv)
    n1=[low_one,near,far,far_pair]
    late=after(grad_mlp,far)
    gm=[late,flip(late,1),flip(late,2)]
    segq=seg[None,:]; segk=seg[:,None]
    hb=half//BLK
    codes=block_codes(seg,slots,False)
    att_far,lse_far=attn_fwd(codes[hb:],q,k,v,segq,segk,hb,hb)
    att_far,g2=lax.optimization_barrier((att_far,gm[2]))
    proj=lambda a: jnp.dot(a,w_proj,preferred_element_type=f32).astype(bf16)
    across=pair_sum(proj(att_far[tok:]),proj(att_far[:tok])).astype(bf16)
    q_late,across=lax.optimization_barrier((q,across))
    gm=[gm[0],gm[1],g2,flip(g2,1)]
    across=flip(across,3)
    att_near,lse_near=attn_fwd(codes[:hb],q_late,k,v,segq,segk,0,hb)
    across,att_near=lax.optimization_barrier((across,att_near))
    mine=pair_sum(proj(att_near[:tok]),proj(att_near[tok:]))
    resid_one=x_rows+mine+across.astype(f32)+shifts[2]
    normed_two,norm_two_back=jax.vjp(norm_rows,resid_one,gains[1],shifts[1])
    low_two=normed_two.astype(bf16)
    far=flip(low_two,2)
    near=flip(low_two,1)
    b1=b_fc1.astype(f32)[None,:]
    hid,gp,gn0,gn1,db0=mlp_rows((low_two,near),(gm[0],gm[1]),w_fc1,b1,w_fc2,0,None)
    far,hid,gp,allg=lax.optimization_barrier((far,hid,gp,jnp.concatenate(gm,axis=0)))
    far_pair=flip(far,1)
    hid,gp,gn2,gn3,db1=mlp_rows((far,far_pair),(gm[2],gm[3]),w_fc1,b1,w_fc2,1,(hid,gp))
    db=db0+db1
    across=pair_sum(gn3,gn2).astype(bf16)
    hid,gp,across=lax.optimization_barrier((hid,gp,across))
    across=flip(across,3)
    mine=pair_sum(gn0,gn1)
    tn=lambda a,b: lax.dot_general(a,b,(((0,),(0,)),((),())),preferred_element_type=f32)
    grad_w1=tn(jnp.concatenate([low_two,near,far,far_pair],axis=0),gp).astype(bf16)
    grad_w2=tn(hid,allg).astype(bf16)
    both=jnp.concatenate([grad_w1,grad_w2],axis=0)
    across=after(across,both)
    wsum=lax.psum_scatter(both,"dp",scatter_dimension=0,tiled=True)
    grad_resid_two,grad_gain_two,grad_shift_two=norm_two_back(mine+across.astype(f32))

    grad_resid_one=grad_y+grad_resid_two
    grad_attn=grad_resid_one.astype(bf16)
    far=flip(grad_attn,2)
    near=flip(grad_attn,1)
    ghead=lambda a: lax.dot_general(a,w_proj,NT,preferred_element_type=f32).astype(bf16)
    bcodes=block_codes(seg,slots,True)
    do_near=jnp.concatenate([ghead(grad_attn),ghead(near)],axis=0)
    gq_near,dk,dv,bs0=attn_bwd(bcodes[:hb],q,k,v,do_near,att_near,lse_near,segq,segk,cos,sin,0,None)
    early=jnp.stack([grad_gain_two,grad_shift_two,jnp.sum(grad_attn,axis=0,dtype=f32),jnp.sum(grad_mlp,axis=0,dtype=f32)])
    far,dk,dv,early=lax.optimization_barrier((far,dk,dv,early))
    far_pair=flip(far,1)
    do_far=jnp.concatenate([ghead(far),ghead(far_pair)],axis=0)
    alla=jnp.concatenate([grad_attn,near,far,far_pair],axis=0)
    grad_proj=tn(jnp.concatenate([att_near,att_far],axis=0),alla).astype(bf16)
    do_far,grad_proj=lax.optimization_barrier((do_far,grad_proj))
    gq_far,gk,gv,bs1=attn_bwd(bcodes[hb:],q,k,v,do_far,att_far,lse_far,segq,segk,cos,sin,1,(dk,dv))
    gk,wsum=lax.optimization_barrier((gk,wsum))
    wsum=lax.all_gather(wsum,"dp",axis=0,tiled=True)
    r2,r3=back_rows(gq_far,gk,gv,w_qkv,1)
    across=pair_sum(r3,r2).astype(bf16)
    gq_near,gk,gv,across=lax.optimization_barrier((gq_near,gk,gv,across))
    across=flip(across,3)
    g_all=jnp.concatenate([jnp.concatenate([gq_near,gq_far],axis=0),gk,gv],axis=1)
    grad_wqkv=tn(jnp.concatenate(n1,axis=0),g_all).astype(bf16)
    grad_wqkv,hid,gq_near=lax.optimization_barrier((grad_wqkv,hid,gq_near))
    d=tokens.shape[1]
    sizes=(3*cols,db.shape[1])
    pad=(-sum(sizes))%(8*cols<<bits)
    small=jnp.concatenate([(bs0+bs1)[:3].reshape(-1),db[0],jnp.zeros((pad,),f32)]).astype(bf16).reshape(-1,cols)
    tail_a=DpSum(jnp.concatenate([grad_wqkv[:,:cols],grad_wqkv[:,cols:2*cols]],axis=0),tuple(range(bits)))
    tail_b=DpSum(jnp.concatenate([grad_wqkv[:,2*cols:],grad_proj.reshape(-1,cols),small],axis=0),(1,0)+tuple(range(2,bits)))
    tails=(tail_a,tail_b)
    for t in tails: t.start(t.operand())
    *gots,across=lax.optimization_barrier((tail_a.got,tail_b.got,across))
    for t,got in zip(tails,gots): t.finish(got)
    r0,r1=back_rows(gq_near,gk,gv,w_qkv,0)
    mine=pair_sum(r0,r1)
    grad_x_norm,grad_gain_one,grad_shift_one=norm_one_back(mine+across.astype(f32))
    one=jnp.concatenate([jnp.stack([grad_gain_one,grad_shift_one]),early],axis=0)
    o=[jnp.dot(hid[j*tok:(j+1)*tok],w_fc2,preferred_element_type=f32).astype(bf16) for j in range(ranks)]
    o_across=flip(pair_sum(o[3],o[2]).astype(bf16),3)
    for t in tails: t.start(t.operand())
    hops=[partial(dp_flip,bit=bit) for bit in range(bits)]+[partial(flip,bits=1),partial(flip,bits=2)]
    other=hops.pop(0)(one)
    other,*gots=lax.optimization_barrier((other,tail_a.got,tail_b.got))
    for t,got in zip(tails,gots): t.finish(got)
    one=one+other
    while hops or tail_a.at<len(tail_a.stages):
        busy=[t for t in tails if t.at<len(t.stages)]
        for t in busy: t.start(t.operand())
        hop=hops.pop(0) if hops else None
        other=hop(one) if hop else one
        third=bool(busy) and busy[0].at==bits-1
        gots=[t.got for t in busy]
        if third:
            other,o_across,wsum,*gots=lax.optimization_barrier((other,o_across,wsum,*gots))
        else:
            other,*gots=lax.optimization_barrier((other,*gots))
        for t,got in zip(busy,gots): t.finish(got)
        one=one+other if hop else one
    tail_a,tail_b=tail_a.cur,tail_b.cur
    output=(resid_one+pair_sum(o[0],o[1])+o_across.astype(f32)+shifts[3]).astype(bf16)
    grad_w1,grad_w2=wsum[:d],wsum[d:]
    grad_wqkv=jnp.stack([tail_a[:d],tail_a[d:],tail_b[:d]]).astype(f32)
    grad_wproj=tail_b[d:2*d].reshape(cols,d).astype(f32)
    small=tail_b[2*d:].reshape(-1).astype(f32)
    grad_bqkv=small[:sizes[0]].reshape(3,cols)
    grad_b1=small[sizes[0]:sizes[0]+sizes[1]]
    grad_tokens=(grad_resid_one+grad_x_norm).astype(bf16)
    return (output,grad_tokens,grad_wqkv,grad_bqkv,grad_wproj,grad_w1.astype(f32),grad_b1,grad_w2.astype(f32),
            jnp.stack([one[0],one[2]]),jnp.stack([one[1],one[3],one[4],one[5]]))


def solution(mesh):
    rows=P(("dp","tensor"),None)
    return jax.shard_map(shards,mesh=mesh,
        in_specs=(rows,rows,P("dp",None),P(None,"dp"),P(None,None,"tensor"),P(None,"tensor"),P("tensor",None),
                  P(None,"tensor"),P("tensor"),P("tensor",None),P(),P()),
        out_specs=(rows,rows,P(None,None,"tensor"),P(None,"tensor"),P("tensor",None),P(None,"tensor"),P("tensor"),
                   P("tensor",None),P(),P()),
        check_vma=False)
```

```python
from functools import partial

import jax
import jax.numpy as jnp
from jax import lax
from jax.experimental import pallas as pl
from jax.experimental.pallas import tpu as pltpu
from jax.sharding import PartitionSpec as P

HDIM=64
LOG2E=1.4426950408889634
LN2=0.6931471805599453
f32=jnp.float32; bf16=jnp.bfloat16
BLK=256
VROWS=80
NT=(((1,),(1,)),((),()))

def work(flops):
    return pl.CostEstimate(flops=flops,bytes_accessed=0,transcendentals=0)

def lane_half(shape, which):
    lane=lax.broadcasted_iota(jnp.int32, shape, 1)
    return (lane//HDIM)%2==which

def attn_fwd_kernel(codes, q_ref, k_ref, v_ref, segq_ref, segk_ref, o_ref, lse_ref, vt, qm, m_sc, acc, s_sc):
    step=pl.program_id(0)
    nkb=k_ref.shape[0]//BLK
    heads=q_ref.shape[1]//HDIM
    @pl.when(step==0)
    def _():
        for blk in range(nkb):
            rows=pl.ds(blk*BLK,BLK)
            vT=v_ref[rows,:].T
            for h in range(heads):
                vt[h*VROWS:h*VROWS+HDIM, rows]=vT[h*HDIM:(h+1)*HDIM,:]
        for h in range(heads):
            vt[h*VROWS+HDIM:(h+1)*VROWS,:]=jnp.ones((VROWS-HDIM,vt.shape[1]),bf16)
    for p in range(heads//2):
        qp=q_ref[:,p*128:(p+1)*128]
        for w in range(2):
            qm[2*p+w]=jnp.where(lane_half(qp.shape,w),qp,jnp.zeros_like(qp))
    m_sc[...]=jnp.full(m_sc.shape,-1e30,f32)
    acc[...]=jnp.zeros(acc.shape,f32)
    scale=HDIM**-0.5*LOG2E

    def tile(kb,masked):
        rows=pl.ds(pl.multiple_of(kb*BLK,BLK),BLK)
        if masked:
            allowed=segk_ref[rows,:][:,0:1]==segq_ref[0:1,:]
        tops=[]
        for h in range(heads):
            p=h//2
            s=lax.dot_general(k_ref[rows,p*128:(p+1)*128],qm[h],NT,preferred_element_type=f32)*scale
            if masked: s=jnp.where(allowed,s,-1e30)
            s_sc[h]=s
            tops.append(jnp.max(s,axis=0,keepdims=True))
        m_prev=m_sc[0:heads,:]
        m_new=jnp.maximum(m_prev,jnp.concatenate(tops,axis=0))
        alpha=jnp.exp2(m_prev-m_new)
        m_sc[0:heads,:]=m_new
        for h in range(heads):
            prob=jnp.exp2(s_sc[h]-m_new[h:h+1,:]).astype(bf16)
            arows=slice(h*VROWS,(h+1)*VROWS)
            acc[arows,:]=acc[arows,:]*alpha[h:h+1,:]+jnp.dot(vt[arows,rows],prob,preferred_element_type=f32)

    def body(kb,carry):
        code=codes[step,kb]
        @pl.when(code==1)
        def _(): tile(kb,False)
        @pl.when(code==2)
        def _(): tile(kb,True)
        return carry
    lax.fori_loop(0,nkb,body,0)
    outs=[]
    for h in range(heads):
        total=acc[h*VROWS+HDIM:h*VROWS+HDIM+1,:]
        outs.append(acc[h*VROWS:h*VROWS+HDIM,:]/total)
        lse_ref[h:h+1,:]=m_sc[h:h+1,:]+jnp.log2(total)
    for h in range(heads,8):
        lse_ref[h:h+1,:]=jnp.zeros((1,BLK),f32)
    o_ref[...]=jnp.concatenate(outs,axis=0).T.astype(bf16)

def attn_fwd(codes,q,k,v,segq,segk,block0,nblocks):
    rows,cols=k.shape
    heads=cols//HDIM
    full=lambda i,c:(0,0)
    return pl.pallas_call(
        attn_fwd_kernel,
        out_shape=(jax.ShapeDtypeStruct((nblocks*BLK,cols),bf16),jax.ShapeDtypeStruct((8,nblocks*BLK),f32)),
        grid_spec=pltpu.PrefetchScalarGridSpec(num_scalar_prefetch=1,grid=(nblocks,),
            in_specs=[pl.BlockSpec((BLK,cols),lambda i,c:(i+block0,0)),
                      pl.BlockSpec((rows,cols),full),pl.BlockSpec((rows,cols),full),
                      pl.BlockSpec((1,BLK),lambda i,c:(0,i+block0)),
                      pl.BlockSpec((rows,1),full)],
            out_specs=[pl.BlockSpec((BLK,cols),lambda i,c:(i,0)),pl.BlockSpec((8,BLK),lambda i,c:(0,i))],
            scratch_shapes=[pltpu.VMEM((heads*VROWS,rows),bf16),pltpu.VMEM((heads,BLK,128),bf16),
                            pltpu.VMEM((8,BLK),f32),pltpu.VMEM((heads*VROWS,BLK),f32),pltpu.VMEM((heads,BLK,BLK),f32)]),
        compiler_params=pltpu.CompilerParams(dimension_semantics=("arbitrary",)),
        name="attn_fwd",
        cost_estimate=work((4 if block0 else 64)*nblocks*BLK*rows*cols),
    )(codes,q,k,v,segq,segk)

def swap_halves(x):
    n=x.shape[1]
    lane=lax.broadcasted_iota(jnp.int32,x.shape,1)
    up=pltpu.roll(x,n-HDIM//2,1)
    down=pltpu.roll(x,HDIM//2,1)
    return jnp.where(lane%HDIM<HDIM//2,up,down)

def attn_bwd_kernel(last, codes, q_ref,k_ref,v_ref,do_ref,o_ref,lse_ref,segq_ref,segk_ref,cos_ref,sin_ref,cosk_ref,sink_ref,*rest):
    if last:
        dk0_ref,dv0_ref,gq_ref,gk_ref,gv_ref,bsum_ref,kt,qm,dom,delta,dq,dk,dv,p_sc,low_sc,ds_sc=rest
    else:
        gq_ref,gk_ref,gv_ref,bsum_ref,kt,qm,dom,delta,dq,dk,dv,p_sc,low_sc,ds_sc=rest
    step=pl.program_id(0)
    nkb=pl.num_programs(0)
    nqb=q_ref.shape[0]//BLK
    heads=q_ref.shape[1]//HDIM
    scale=HDIM**-0.5
    def unrotate(x,cos,sin):
        out=[]
        for p in range(heads//2):
            xp=x[:,p*128:(p+1)*128]
            out.append(xp*cos-swap_halves(xp)*sin)
        return jnp.concatenate(out,axis=1)
    @pl.when(step==0)
    def _():
        def prep(blk,carry):
            rows=pl.ds(pl.multiple_of(blk*BLK,BLK),BLK)
            for p in range(heads//2):
                lanes=slice(p*128,(p+1)*128)
                qp=q_ref[rows,lanes]; dp=do_ref[rows,lanes]
                for w in range(2):
                    sel=lane_half(qp.shape,w)
                    qm[2*p+w,rows,:]=jnp.where(sel,qp,jnp.zeros_like(qp))
                    dom[2*p+w,rows,:]=jnp.where(sel,dp,jnp.zeros_like(dp))
            prod=(do_ref[rows,:].astype(f32)*o_ref[rows,:].astype(f32)).T
            for h in range(heads):
                delta[h:h+1,rows]=jnp.sum(prod[h*HDIM:(h+1)*HDIM,:],axis=0,keepdims=True)
            return carry
        lax.fori_loop(0,nqb,prep,0)
        dq[...]=jnp.zeros(dq.shape,f32)
        bsum_ref[...]=jnp.zeros(bsum_ref.shape,f32)
    kt[...]=k_ref[...].T
    if last:
        dk[...]=dk0_ref[...]
        dv[...]=dv0_ref[...]
    else:
        dk[...]=jnp.zeros(dk.shape,f32)
        dv[...]=jnp.zeros(dv.shape,f32)

    def tile(qb,masked):
        rows=pl.ds(pl.multiple_of(qb*BLK,BLK),BLK)
        if masked:
            allowed=segk_ref[:,0:1]==segq_ref[0:1,rows]
        for h in range(heads):
            lanes=slice(h//2*128,(h//2+1)*128)
            s=lax.dot_general(k_ref[:,lanes],qm[h,rows,:],NT,preferred_element_type=f32)*(scale*LOG2E)
            prob=jnp.exp2(s-lse_ref[h:h+1,rows])
            if masked: prob=jnp.where(allowed,prob,0.0)
            p_sc[h]=prob
        for h in range(heads):
            lanes=slice(h//2*128,(h//2+1)*128)
            side=slice(h%2*BLK,(h%2+1)*BLK)
            dp=lax.dot_general(v_ref[:,lanes],dom[h,rows,:],NT,preferred_element_type=f32)
            prob=p_sc[h]
            low_sc[h//2,:,side]=prob.astype(bf16)
            ds_sc[h//2,:,side]=(prob*(dp-delta[h:h+1,rows])).astype(bf16)
        for p in range(heads//2):
            lanes=slice(p*128,(p+1)*128)
            pair=slice(2*p,2*p+2)
            dv[:,lanes]+=jnp.dot(low_sc[p],dom[pair,rows,:].reshape(2*BLK,128),preferred_element_type=f32)
            dk[:,lanes]+=jnp.dot(ds_sc[p],qm[pair,rows,:].reshape(2*BLK,128),preferred_element_type=f32)
        for h in range(heads):
            hr=slice(h*HDIM,(h+1)*HDIM)
            side=slice(h%2*BLK,(h%2+1)*BLK)
            dq[hr,rows]+=jnp.dot(kt[hr,:],ds_sc[h//2,:,side],preferred_element_type=f32)

    def body(qb,carry):
        code=codes[qb,step]
        @pl.when(code==1)
        def _(): tile(qb,False)
        @pl.when(code==2)
        def _(): tile(qb,True)
        return carry
    lax.fori_loop(0,nqb,body,0)

    if last:
        gk=unrotate(dk[...]*scale,cosk_ref[...],sink_ref[...]).astype(bf16)
        gv=dv[...].astype(bf16)
        gk_ref[...]=gk
        gv_ref[...]=gv
        bsum_ref[1:2,:]+=jnp.sum(gk.astype(f32),axis=0,keepdims=True)
        bsum_ref[2:3,:]+=jnp.sum(gv.astype(f32),axis=0,keepdims=True)
    else:
        gk_ref[...]=dk[...]
        gv_ref[...]=dv[...]

    @pl.when(step==nkb-1)
    def _():
        def fin(blk,carry):
            rows=pl.ds(pl.multiple_of(blk*BLK,BLK),BLK)
            gq=unrotate(dq[:,rows].T*scale,cos_ref[rows,:],sin_ref[rows,:]).astype(bf16)
            gq_ref[rows,:]=gq
            bsum_ref[0:1,:]+=jnp.sum(gq.astype(f32),axis=0,keepdims=True)
            return carry
        lax.fori_loop(0,nqb,fin,0)

def attn_bwd(codes,q,k,v,do,o,lse,segq,segk,cos,sin,part,carried):
    rows,cols=k.shape
    half=do.shape[0]
    heads=cols//HDIM
    nb=rows//BLK
    last=carried is not None
    mine=lambda n: pl.BlockSpec((half,n),lambda i,c:(part,0))
    here=lambda n: pl.BlockSpec((half,n),lambda i,c:(0,0))
    blk=lambda n: pl.BlockSpec((BLK,n),lambda i,c:(i,0))
    kdtype=bf16 if last else f32
    return pl.pallas_call(
        partial(attn_bwd_kernel,last),
        out_shape=(jax.ShapeDtypeStruct((half,cols),bf16),jax.ShapeDtypeStruct((rows,cols),kdtype),
                   jax.ShapeDtypeStruct((rows,cols),kdtype),jax.ShapeDtypeStruct((8,cols),f32)),
        grid_spec=pltpu.PrefetchScalarGridSpec(num_scalar_prefetch=1,grid=(nb,),
            in_specs=[mine(cols),blk(cols),blk(cols),here(cols),here(cols),pl.BlockSpec((8,half),lambda i,c:(0,0)),
                      pl.BlockSpec((1,half),lambda i,c:(0,part)),blk(1),mine(128),mine(128),blk(128),blk(128)]
                     +([blk(cols),blk(cols)] if last else []),
            out_specs=[here(cols),blk(cols),blk(cols),pl.BlockSpec((8,cols),lambda i,c:(0,0))],
            scratch_shapes=[pltpu.VMEM((cols,BLK),bf16),pltpu.VMEM((heads,half,128),bf16),pltpu.VMEM((heads,half,128),bf16),
                            pltpu.VMEM((8,half),f32),pltpu.VMEM((cols,half),f32),pltpu.VMEM((BLK,cols),f32),pltpu.VMEM((BLK,cols),f32),
                            pltpu.VMEM((heads,BLK,BLK),f32),pltpu.VMEM((heads//2,BLK,2*BLK),bf16),pltpu.VMEM((heads//2,BLK,2*BLK),bf16)]),
        compiler_params=pltpu.CompilerParams(dimension_semantics=("arbitrary",)),
        name="attn_bwd",
        cost_estimate=work(45*half*rows*cols),
    )(codes,q,k,v,do,o,lse,segq,segk,cos,sin,cos,sin,*(carried or ()))

def block_codes(seg,pad_seg,skip_pad):
    sb=seg.reshape(-1,BLK)
    lo=jnp.min(sb,axis=1); hi=jnp.max(sb,axis=1)
    meet=(lo[:,None]<=hi[None,:])&(lo[None,:]<=hi[:,None])
    whole=(lo==hi)
    same=whole[:,None]&whole[None,:]&(lo[:,None]==lo[None,:])
    code=jnp.where(meet,jnp.where(same,1,2),0).astype(jnp.int32)
    if skip_pad:
        alive=lo<pad_seg
        code=jnp.where(alive[:,None]&alive[None,:],code,0)
    return code


def pick(i,n,a_ref,b_ref):
    return jnp.where(i<n,a_ref[...],b_ref[...])


def qkv_kernel(n, xa_ref, xb_ref, w_ref, b_ref, cos_ref, sin_ref, *rest):
    x=pick(pl.program_id(0),n,xa_ref,xb_ref)
    cos=cos_ref[...]; sin=sin_ref[...]
    for c,o_ref in enumerate(rest[-3:]):
        y=jnp.dot(x,w_ref[c],preferred_element_type=f32)+b_ref[c:c+1,:]
        if c<2:
            parts=[]
            for p in range(y.shape[1]//128):
                yp=y[:,p*128:(p+1)*128]
                parts.append(yp*cos+swap_halves(yp)*sin)
            y=jnp.concatenate(parts,axis=1)
        o_ref[...]=y.astype(bf16)


def two(tile,n,width):
    return [pl.BlockSpec((tile,width),lambda i:(jnp.minimum(i,n-1),0)),
            pl.BlockSpec((tile,width),lambda i:(jnp.maximum(i-n,0),0))]


def qkv_rows(xa,xb,w,b,cos,sin,part,full):
    rows,d=xa.shape
    cols=w.shape[2]
    tile=min(512,rows)
    n=rows//tile
    off=part*2*n
    row=lambda m: pl.BlockSpec((tile,m),lambda i:(i+off,0))
    kept=[] if full is None else list(full)
    return pl.pallas_call(
        partial(qkv_kernel,n),
        grid=(2*n,),
        out_shape=[jax.ShapeDtypeStruct((cos.shape[0],cols),bf16)]*3,
        in_specs=two(tile,n,d)+[pl.BlockSpec(w.shape,lambda i:(0,0,0)),pl.BlockSpec(b.shape,lambda i:(0,0)),
                  row(128),row(128)]+[pl.BlockSpec(memory_space=pl.ANY)]*len(kept),
        out_specs=[row(cols)]*3,
        input_output_aliases={6+i:i for i in range(len(kept))},
        compiler_params=pltpu.CompilerParams(dimension_semantics=("arbitrary",)),
        name="qkv",
        cost_estimate=work(20*rows*d*cols*2),
    )(xa,xb,w,b,cos,sin,*kept)


def mlp_kernel(n,xa_ref,xb_ref,ga_ref,gb_ref,w1_ref,b1_ref,w2_ref,*rest):
    hid_ref,gp_ref,na_ref,nb_ref,db_ref=rest[-5:]
    i=pl.program_id(0)
    @pl.when(i==0)
    def _():
        db_ref[...]=jnp.zeros(db_ref.shape,f32)
    pre=jnp.dot(pick(i,n,xa_ref,xb_ref),w1_ref[...],preferred_element_type=f32)+b1_ref[...]
    phi=0.5+0.5*lax.erf(pre*0.7071067811865476)
    hid_ref[...]=(pre*phi).astype(bf16)
    slope=phi+pre*(0.3989422804014327*jnp.exp2(pre*pre*(-0.5*LOG2E)))
    gh=lax.dot_general(pick(i,n,ga_ref,gb_ref),w2_ref[...],NT,preferred_element_type=f32)
    gp=(gh*slope).astype(bf16)
    gp_ref[...]=gp
    db_ref[...]+=jnp.sum(gp.astype(f32),axis=0,keepdims=True)
    gn=lax.dot_general(gp,w1_ref[...],NT,preferred_element_type=f32).astype(bf16)
    @pl.when(i<n)
    def _(): na_ref[...]=gn
    @pl.when(i>=n)
    def _(): nb_ref[...]=gn


def mlp_rows(xs,gs,w1,b1,w2,part,full):
    rows,d=xs[0].shape
    units=w1.shape[1]
    tile=min(256,rows)
    n=rows//tile
    off=part*2*n
    row=lambda m: pl.BlockSpec((tile,m),lambda i:(i+off,0))
    whole=lambda a: pl.BlockSpec(a.shape,lambda i:(0,0))
    kept=[] if full is None else list(full)
    return pl.pallas_call(
        partial(mlp_kernel,n),
        grid=(2*n,),
        out_shape=[jax.ShapeDtypeStruct((rows*4,units),bf16)]*2+[jax.ShapeDtypeStruct((rows,d),bf16)]*2+
                  [jax.ShapeDtypeStruct((1,units),f32)],
        in_specs=two(tile,n,d)+two(tile,n,d)+[whole(w1),whole(b1),whole(w2)]+[pl.BlockSpec(memory_space=pl.ANY)]*len(kept),
        out_specs=[row(units),row(units)]+two(tile,n,d)+[pl.BlockSpec((1,units),lambda i:(0,0))],
        input_output_aliases={7+i:i for i in range(len(kept))},
        compiler_params=pltpu.CompilerParams(dimension_semantics=("arbitrary",)),
        name="mlp",
        cost_estimate=work(12*rows*d*units),
    )(*xs,*gs,w1,b1,w2,*kept)


def back_kernel(n,gq_ref,gk_ref,gv_ref,w_ref,oa_ref,ob_ref):
    i=pl.program_id(0)
    y=lax.dot_general(gq_ref[...],w_ref[0],NT,preferred_element_type=f32)
    y=y+lax.dot_general(gk_ref[...],w_ref[1],NT,preferred_element_type=f32)
    y=(y+lax.dot_general(gv_ref[...],w_ref[2],NT,preferred_element_type=f32)).astype(bf16)
    @pl.when(i<n)
    def _(): oa_ref[...]=y
    @pl.when(i>=n)
    def _(): ob_ref[...]=y


def back_rows(gq,gk,gv,w,part):
    half,cols=gq.shape
    rows=half//2
    d=w.shape[1]
    tile=min(512,rows)
    n=rows//tile
    off=part*2*n
    row=pl.BlockSpec((tile,cols),lambda i:(i+off,0))
    return pl.pallas_call(
        partial(back_kernel,n),
        grid=(2*n,),
        out_shape=[jax.ShapeDtypeStruct((rows,d),bf16)]*2,
        in_specs=[pl.BlockSpec((tile,cols),lambda i:(i,0)),row,row,pl.BlockSpec(w.shape,lambda i:(0,0,0))],
        out_specs=two(tile,n,d),
        compiler_params=pltpu.CompilerParams(dimension_semantics=("arbitrary",)),
        name="back",
        cost_estimate=work(1),
    )(gq,gk,gv,w)


def norm_rows(values_in, gain_row, shift_row):
    row_mean = jnp.mean(values_in, axis=-1, keepdims=True)
    centred = values_in - row_mean
    variance = jnp.mean(centred * centred, axis=-1, keepdims=True)
    return centred * lax.rsqrt(variance + 1e-06) * gain_row + shift_row


def flip(x,bits):
    n=lax.axis_size("tensor")
    return lax.ppermute(x,"tensor",[(i,i^bits) for i in range(n)])


def pair_sum(mine,other):
    return mine.astype(f32)+flip(other,1).astype(f32)


def dp_flip(x,bit):
    n=lax.axis_size("dp")
    return lax.ppermute(x,"dp",[(i,i^(1<<bit)) for i in range(n)])


class DpSum:
    def __init__(self,x,order):
        self.cur=x
        self.stages=[(bit,True) for bit in order]+[(bit,False) for bit in reversed(order)]
        self.at=0

    def operand(self):
        bit,halving=self.stages[self.at]
        if not halving: return self.cur
        up=(lax.axis_index("dp")>>bit)&1
        halves=self.cur.reshape(2,-1,self.cur.shape[1])
        self.kept=lax.dynamic_index_in_dim(halves,up,0,False)
        return lax.dynamic_index_in_dim(halves,1-up,0,False)

    def start(self,operand):
        self.sent=operand
        self.got=dp_flip(operand,self.stages[self.at][0])

    def finish(self,got):
        bit,halving=self.stages[self.at]
        self.at+=1
        if halving:
            self.cur=(self.kept.astype(f32)+got.astype(f32)).astype(bf16)
        else:
            up=((lax.axis_index("dp")>>bit)&1)==1
            self.cur=jnp.concatenate([jnp.where(up,got,self.sent),jnp.where(up,self.sent,got)],axis=0)

    def rest(self):
        while self.at<len(self.stages):
            self.start(self.operand())
            self.finish(self.got)
        return self.cur


def begin(sums,value):
    value,*sends=lax.optimization_barrier((value,*[s.operand() for s in sums]))
    for s,x in zip(sums,sends): s.start(x)
    return value


def settle(sums,value):
    value,*gots=lax.optimization_barrier((value,*[s.got for s in sums]))
    for s,x in zip(sums,gots): s.finish(x)
    return value


def all_sum(x):
    for bits in (1,2):
        x=x+flip(x,bits)
    for bit in range(lax.axis_size("dp").bit_length()-1):
        x=x+dp_flip(x,bit)
    return x


def after(x,*others):
    return lax.optimization_barrier((x,)+others)[0]


def shards(tokens,grad_out,lengths,coords,w_qkv,b_qkv,w_proj,w_fc1,b_fc1,w_fc2,norm_gains,shift_biases):
    tok=tokens.shape[0]
    ranks=lax.axis_size("tensor")
    bits=lax.axis_size("dp").bit_length()-1
    me=lax.axis_index("tensor")
    rows_all=tok*ranks
    half=rows_all//2
    cols=w_qkv.shape[2]
    ends=jnp.cumsum(lengths[0])
    slots=lengths.shape[1]
    rel=jnp.arange(rows_all,dtype=jnp.int32)
    place=((rel//tok)^me)*tok+rel%tok
    seg=jnp.sum((place[:,None]>=ends[None,:]).astype(jnp.int32),axis=1)
    live=(place[:tok]<ends[-1]).astype(f32)[:,None]
    cgrp=jnp.concatenate([lax.dynamic_slice_in_dim(coords,(me^j)*tok,tok,1) for j in range(ranks)],axis=1).astype(f32)
    lane=jnp.arange(128,dtype=jnp.int32)
    pair=lane%(HDIM//2)
    freq=100.0**(-(pair//3).astype(f32)/(HDIM//2//3+1))
    angle=jnp.zeros((rows_all,128),f32)
    for a in range(3):
        angle=angle+cgrp[a][:,None]*jnp.where(pair%3==a,freq,0.0)[None,:]
    cos=jnp.cos(angle)
    sin=jnp.sin(angle)*jnp.where(lane%HDIM<HDIM//2,-1.0,1.0)[None,:]
    gains=norm_gains.astype(f32)
    shifts=shift_biases.astype(f32)
    x_rows=tokens.astype(f32)

    normed_one,norm_one_back=jax.vjp(norm_rows,x_rows,gains[0],shifts[0])
    low_one=normed_one.astype(bf16)
    far=flip(low_one,2)
    near=flip(low_one,1)
    grad_y=grad_out.astype(f32)*live
    grad_mlp=grad_y.astype(bf16)

    bq=b_qkv.astype(f32)
    qkv=qkv_rows(low_one,near,w_qkv,bq,cos,sin,0,None)
    far,*qkv=lax.optimization_barrier((far,*qkv))
    far_pair=flip(far,1)
    q,k,v=qkv_rows(far,far_pair,w_qkv,bq,cos,sin,1,qkv)
    n1=[low_one,near,far,far_pair]
    late=after(grad_mlp,far)
    gm=[late,flip(late,1),flip(late,2)]
    segq=seg[None,:]; segk=seg[:,None]
    hb=half//BLK
    codes=block_codes(seg,slots,False)
    att_far,lse_far=attn_fwd(codes[hb:],q,k,v,segq,segk,hb,hb)
    att_far,g2=lax.optimization_barrier((att_far,gm[2]))
    proj=lambda a: jnp.dot(a,w_proj,preferred_element_type=f32).astype(bf16)
    across=pair_sum(proj(att_far[tok:]),proj(att_far[:tok])).astype(bf16)
    q_late,across=lax.optimization_barrier((q,across))
    gm=[gm[0],gm[1],g2,flip(g2,1)]
    across=flip(across,3)
    att_near,lse_near=attn_fwd(codes[:hb],q_late,k,v,segq,segk,0,hb)
    across,att_near=lax.optimization_barrier((across,att_near))
    mine=pair_sum(proj(att_near[:tok]),proj(att_near[tok:]))
    resid_one=x_rows+mine+across.astype(f32)+shifts[2]
    normed_two,norm_two_back=jax.vjp(norm_rows,resid_one,gains[1],shifts[1])
    low_two=normed_two.astype(bf16)
    far=flip(low_two,2)
    near=flip(low_two,1)
    b1=b_fc1.astype(f32)[None,:]
    hid,gp,gn0,gn1,db0=mlp_rows((low_two,near),(gm[0],gm[1]),w_fc1,b1,w_fc2,0,None)
    far,hid,gp=lax.optimization_barrier((far,hid,gp))
    far_pair=flip(far,1)
    hid,gp,gn2,gn3,db1=mlp_rows((far,far_pair),(gm[2],gm[3]),w_fc1,b1,w_fc2,1,(hid,gp))
    db=db0+db1
    across=pair_sum(gn3,gn2).astype(bf16)
    hid,gp,across=lax.optimization_barrier((hid,gp,across))
    across=flip(across,3)
    mine=pair_sum(gn0,gn1)
    tn=lambda a,b: lax.dot_general(a,b,(((0,),(0,)),((),())),preferred_element_type=f32)
    grad_w1=tn(jnp.concatenate([low_two,near,far,far_pair],axis=0),gp).astype(bf16)
    grad_w2=tn(hid,jnp.concatenate(gm,axis=0)).astype(bf16)
    both=jnp.concatenate([grad_w1,grad_w2],axis=0)
    across=after(across,both)
    wsum=lax.psum_scatter(both,"dp",scatter_dimension=0,tiled=True)
    grad_resid_two,grad_gain_two,grad_shift_two=norm_two_back(mine+across.astype(f32))

    grad_resid_one=grad_y+grad_resid_two
    grad_attn=grad_resid_one.astype(bf16)
    far=flip(grad_attn,2)
    near=flip(grad_attn,1)
    ghead=lambda a: lax.dot_general(a,w_proj,NT,preferred_element_type=f32).astype(bf16)
    bcodes=block_codes(seg,slots,True)
    do_near=jnp.concatenate([ghead(grad_attn),ghead(near)],axis=0)
    gq_near,dk,dv,bs0=attn_bwd(bcodes[:hb],q,k,v,do_near,att_near,lse_near,segq,segk,cos,sin,0,None)
    early=jnp.stack([grad_gain_two,grad_shift_two,jnp.sum(grad_attn,axis=0,dtype=f32),jnp.sum(grad_mlp,axis=0,dtype=f32)])
    far,dk,dv,early=lax.optimization_barrier((far,dk,dv,early))
    far_pair=flip(far,1)
    do_far=jnp.concatenate([ghead(far),ghead(far_pair)],axis=0)
    alla=jnp.concatenate([grad_attn,near,far,far_pair],axis=0)
    grad_proj=tn(jnp.concatenate([att_near,att_far],axis=0),alla).astype(bf16)
    do_far,grad_proj=lax.optimization_barrier((do_far,grad_proj))
    gq_far,gk,gv,bs1=attn_bwd(bcodes[hb:],q,k,v,do_far,att_far,lse_far,segq,segk,cos,sin,1,(dk,dv))
    gk,wsum=lax.optimization_barrier((gk,wsum))
    wsum=lax.all_gather(wsum,"dp",axis=0,tiled=True)
    r2,r3=back_rows(gq_far,gk,gv,w_qkv,1)
    across=pair_sum(r3,r2).astype(bf16)
    gq_near,gk,gv,across=lax.optimization_barrier((gq_near,gk,gv,across))
    across=flip(across,3)
    g_all=jnp.concatenate([jnp.concatenate([gq_near,gq_far],axis=0),gk,gv],axis=1)
    grad_wqkv=tn(jnp.concatenate(n1,axis=0),g_all).astype(bf16)
    grad_wqkv,hid,gq_near=lax.optimization_barrier((grad_wqkv,hid,gq_near))
    d=tokens.shape[1]
    sizes=(3*cols,db.shape[1])
    pad=(-sum(sizes))%(8*cols<<bits)
    small=jnp.concatenate([(bs0+bs1)[:3].reshape(-1),db[0],jnp.zeros((pad,),f32)]).astype(bf16).reshape(-1,cols)
    tail_a=DpSum(jnp.concatenate([grad_wqkv[:,:cols],grad_wqkv[:,cols:2*cols]],axis=0),tuple(range(bits)))
    tail_b=DpSum(jnp.concatenate([grad_wqkv[:,2*cols:],grad_proj.reshape(-1,cols),small],axis=0),(1,0)+tuple(range(2,bits)))
    tails=(tail_a,tail_b)
    for t in tails: t.start(t.operand())
    *gots,across=lax.optimization_barrier((tail_a.got,tail_b.got,across))
    for t,got in zip(tails,gots): t.finish(got)
    r0,r1=back_rows(gq_near,gk,gv,w_qkv,0)
    mine=pair_sum(r0,r1)
    grad_x_norm,grad_gain_one,grad_shift_one=norm_one_back(mine+across.astype(f32))
    one=jnp.concatenate([jnp.stack([grad_gain_one,grad_shift_one]),early],axis=0)
    o=[jnp.dot(hid[j*tok:(j+1)*tok],w_fc2,preferred_element_type=f32).astype(bf16) for j in range(ranks)]
    o_across=flip(pair_sum(o[3],o[2]).astype(bf16),3)
    for t in tails: t.start(t.operand())
    hops=[partial(dp_flip,bit=bit) for bit in range(bits)]+[partial(flip,bits=1),partial(flip,bits=2)]
    other=hops.pop(0)(one)
    other,*gots=lax.optimization_barrier((other,tail_a.got,tail_b.got))
    for t,got in zip(tails,gots): t.finish(got)
    one=one+other
    while hops or tail_a.at<len(tail_a.stages):
        busy=[t for t in tails if t.at<len(t.stages)]
        for t in busy: t.start(t.operand())
        hop=hops.pop(0) if hops else None
        other=hop(one) if hop else one
        third=bool(busy) and busy[0].at==bits-1
        gots=[t.got for t in busy]
        if third:
            other,o_across,wsum,*gots=lax.optimization_barrier((other,o_across,wsum,*gots))
        else:
            other,*gots=lax.optimization_barrier((other,*gots))
        for t,got in zip(busy,gots): t.finish(got)
        one=one+other if hop else one
    tail_a,tail_b=tail_a.cur,tail_b.cur
    output=(resid_one+pair_sum(o[0],o[1])+o_across.astype(f32)+shifts[3]).astype(bf16)
    grad_w1,grad_w2=wsum[:d],wsum[d:]
    grad_wqkv=jnp.stack([tail_a[:d],tail_a[d:],tail_b[:d]]).astype(f32)
    grad_wproj=tail_b[d:2*d].reshape(cols,d).astype(f32)
    small=tail_b[2*d:].reshape(-1).astype(f32)
    grad_bqkv=small[:sizes[0]].reshape(3,cols)
    grad_b1=small[sizes[0]:sizes[0]+sizes[1]]
    grad_tokens=(grad_resid_one+grad_x_norm).astype(bf16)
    return (output,grad_tokens,grad_wqkv,grad_bqkv,grad_wproj,grad_w1.astype(f32),grad_b1,grad_w2.astype(f32),
            jnp.stack([one[0],one[2]]),jnp.stack([one[1],one[3],one[4],one[5]]))


def solution(mesh):
    rows=P(("dp","tensor"),None)
    return jax.shard_map(shards,mesh=mesh,
        in_specs=(rows,rows,P("dp",None),P(None,"dp"),P(None,None,"tensor"),P(None,"tensor"),P("tensor",None),
                  P(None,"tensor"),P("tensor"),P("tensor",None),P(),P()),
        out_specs=(rows,rows,P(None,None,"tensor"),P(None,"tensor"),P("tensor",None),P(None,"tensor"),P("tensor"),
                   P("tensor",None),P(),P()),
        check_vma=False)
```
